128 devices in a mesh: section: 4 (over x_hi, core), gx: 8 (over y, x_lo), gy: 4 (over z).
Axes of the slice: x: 4 (x_hi: 2, x_lo: 2; x = x_hi * 2 + x_lo), y: 4, z: 4, core: 2. Of those that a mesh axis runs over, the one named last changes fastest.
Arguments:
- voltage: float32 [8, 256, 1024], P(None, ('section', 'gx'), 'gy'), may hold values from -1.8 to 1.8
- capacity: float32 [8, 256, 1024], P(None, ('section', 'gx'), 'gy'), may hold values from 0.05 to 0.5
- node_class: int32 [8, 256, 1024], P(None, ('section', 'gx'), 'gy'), may hold values from 0 to 7
- via_sites: int32 [7, 256, 1024], P(None, ('section', 'gx'), 'gy'), may hold values 0 or 1
- ball_sites: int32 [256, 1024], P(('section', 'gx'), 'gy'), may hold values 0 or 1
- load_type: int32 [256, 1024], P(('section', 'gx'), 'gy'), may hold values from 0 to 15
- load_table: float32 [16, 5], replicated, may hold values from -4 to 4
Outputs:
- sections: float32 [5, 8, 256, 1024], P(None, None, ('section', 'gx'), 'gy')
- next_voltage: float32 [8, 256, 1024], P(None, ('section', 'gx'), 'gy')
The draws below stay inside these ranges and needn't reach their ends.
Inputs may be any that keep to these rules, and one draw needn't show every extreme that they name: `node_class`: index into the table of 8 conductances. `load_type`: row of load_table.
All inputs are finite; a program needn't handle non-finite values. No bound on the sum of `via_sites` or of `ball_sites` on one device may be relied on, other than what follows from the above.
Results may differ from the reference program's by a relative error of at most 0.0003.
Values sent between devices are 32-bit elements; how exact they have to be, the bound alone decides.
No kernel may reach another device: no remote copies, remote signals or barrier semaphores. Data moves between devices by JAX's collectives and lax.ppermute only.
A program may use at most 128 MiB of HBM per device.

```python
import math
import jax
import jax.numpy as jnp
import numpy as np
from jax import lax

LAYERS = 8
SECTIONS = 5
LEVELS = 3
SWEEPS = 2
COARSE_SWEEPS = 4
CYCLES = 2
CLASSES = 8
LOADS = 16
NX = 256
NY = 1024


def place_ends(drawn, key, low, high):
    longest = drawn.shape.index(max(drawn.shape))
    spots = []
    for shift in (0, 1):
        where = [jax.random.randint(jax.random.fold_in(key, axis), (), 0, length) for axis, length in enumerate(drawn.shape)]
        where[longest] = (where[longest] + shift) % drawn.shape[longest]
        spots.append(tuple(where))
    return drawn.at[spots[0]].set(low).at[spots[1]].set(high)


def block_scale(own_key, dims, cuts, low, top_value):
    def one(position, parts):
        heights = jax.random.uniform(jax.random.fold_in(jax.random.fold_in(own_key, 6), position), (parts,), jnp.float32, low / len(cuts), top_value / len(cuts))
        return jnp.repeat(jnp.exp(heights), dims[position] // parts).reshape((-1,) + (1,) * (len(dims) - position - 1))

    gain = one(*cuts[0])
    for cut in cuts[1:]:
        gain = gain * one(*cut)
    return gain


def cumulative_ranks(count, slope):
    weights = [(1 << 20) // math.isqrt(grade ** slope) + 1 for grade in range(1, count + 1)]
    deviation = 1 + sum(weights) // (1 << 30)
    return np.cumsum(np.array([max(1, weight // deviation) for weight in weights]))


def ranked(stream_key, shape, amount, skew):
    grid = cumulative_ranks(amount, skew)
    ticket = jax.random.randint(jax.random.fold_in(stream_key, 1), shape, 0, int(grid[amount - 1]))
    grade = jnp.searchsorted(jnp.asarray(grid, jnp.int32), ticket, side="right")
    return jax.random.permutation(jax.random.fold_in(stream_key, 2), amount)[grade].astype(jnp.int32)


def normal_values(stream_key, shape, width, limit, split=(), dtype=jnp.bfloat16):
    values = jax.random.normal(stream_key, shape, jnp.float32) * width
    if len(split) > 0:
        values = block_scale(stream_key, shape, split, -0.22, 0.18) * values
    return jnp.clip(values, min=-limit, max=limit).astype(dtype)


def setup_inputs(seed: int = 0) -> dict:
    key_of = jax.random.split(jax.random.key(seed), 8)
    return {
        "voltage": normal_values(key_of[0], (LAYERS, NX, NY), 0.3, 1.8, ((1, 32), (2, 4)), jnp.float32),
        "capacity": jnp.clip(jnp.exp(math.log(0.5) - 2.3025851 * jax.random.uniform(key_of[1], (LAYERS, NX, NY), jnp.float32) ** block_scale(key_of[1], (LAYERS, NX, NY), ((1, 32), (2, 4)), -0.2, 0.2)), 0.05, 0.5),
        "node_class": place_ends(jax.random.randint(key_of[2], (LAYERS, NX, NY), 0, CLASSES), jax.random.fold_in(key_of[2], 1), 0, CLASSES - 1).astype(jnp.int32),
        "via_sites": place_ends((jax.random.randint(key_of[3], (LAYERS - 1, NX, NY), 0, 3) < 1).astype(jnp.int32), jax.random.fold_in(key_of[3], 1), 0, 1),
        "ball_sites": place_ends((jax.random.randint(key_of[4], (NX, NY), 0, 16) < 1).astype(jnp.int32), jax.random.fold_in(key_of[4], 1), 0, 1),
        "load_type": place_ends(ranked(key_of[5], (NX, NY), LOADS, 2), jax.random.fold_in(key_of[5], 3), 0, LOADS - 1).astype(jnp.int32),
        "load_table": normal_values(key_of[6], (LOADS, SECTIONS), 1.0, 4.0, (), jnp.float32),
    }


node_table = (0.35, 0.55, 0.8, 1.1, 1.5, 2.0, 2.7, 3.6)
via_conductance = 2.5
ball_conductance = 4.0
damping = 0.8
slab_partner = (0, 2, 1, 4, 3)


def pair_times(first, second):
    return (first[0] * second[0] - first[1] * second[1], first[0] * second[1] + first[1] * second[0])


def pair_over(first, second):
    divisor = second[0] * second[0] + second[1] * second[1]
    return ((first[0] * second[0] + first[1] * second[1]) / divisor,
            (first[1] * second[0] - first[0] * second[1]) / divisor)


def pair_minus(first, second):
    return (first[0] - second[0], first[1] - second[1])


def poly_value(coeffs, point):
    total = (0.0, 0.0)
    for c in reversed(coeffs):
        total = pair_times(total, point)
        total = (total[0] + c, total[1])
    return total


def poly_product(first, second):
    result = [0.0] * (len(first) + len(second) - 1)
    for i in range(len(first)):
        for j in range(len(second)):
            result[i + j] = result[i + j] + first[i] * second[j]
    return result


def poly_roots(coeffs):
    leading = coeffs[-1]
    scaled = [c / leading for c in coeffs]
    degree = len(coeffs) - 1
    guesses = []
    current = (1.0, 0.0)
    for k in range(degree):
        guesses.append(current)
        current = pair_times(current, (0.4, 0.9))
    for repeat_index in range(800):
        for k in range(degree):
            divisor = (1.0, 0.0)
            for j in range(degree):
                if j != k:
                    divisor = pair_times(divisor, pair_minus(guesses[k], guesses[j]))
            guesses[k] = pair_minus(guesses[k], pair_over(poly_value(scaled, guesses[k]), divisor))
    return guesses


def matrix_product(first, second):
    return [[sum(first[i][k] * second[k][j] for k in range(len(second))) for j in range(len(second[0]))]
            for i in range(len(first))]


def matrix_inverse(matrix):
    order = len(matrix)
    work = [list(matrix[i]) + [1.0 if i == j else 0.0 for j in range(order)] for i in range(order)]
    for column in range(order):
        pivot = column
        for i in range(column + 1, order):
            if abs(work[i][column]) > abs(work[pivot][column]):
                pivot = i
        work[column], work[pivot] = work[pivot], work[column]
        factor = work[column][column]
        work[column] = [entry / factor for entry in work[column]]
        for i in range(order):
            if i != column:
                scale_row = work[i][column]
                work[i] = [work[i][j] - scale_row * work[column][j] for j in range(2 * order)]
    return [row[order:] for row in work]


def eigen_vector(matrix, value):
    order = len(matrix)
    size_inner = order - 1
    system = []
    for i in range(size_inner):
        row = []
        for j in range(order):
            entry = (matrix[i][j], 0.0)
            if i == j:
                entry = pair_minus(entry, value)
            row.append(entry)
        row[order - 1] = (-row[order - 1][0], -row[order - 1][1])
        system.append(row)
    for column in range(size_inner):
        pivot = column
        for i in range(column + 1, size_inner):
            left_size = system[i][column][0] ** 2 + system[i][column][1] ** 2
            right_size = system[pivot][column][0] ** 2 + system[pivot][column][1] ** 2
            if left_size > right_size:
                pivot = i
        system[column], system[pivot] = system[pivot], system[column]
        for i in range(size_inner):
            if i != column:
                factor = pair_over(system[i][column], system[column][column])
                system[i] = [pair_minus(system[i][j], pair_times(factor, system[column][j])) for j in range(order)]
    vector = [pair_over(system[i][order - 1], system[i][i]) for i in range(size_inner)]
    vector.append((1.0, 0.0))
    return vector


def radau_tables():
    section_count = 5
    generator = [1.0]
    for k in range(section_count - 1):
        generator = poly_product(generator, [0.0, 1.0])
    for k in range(section_count):
        generator = poly_product(generator, [-1.0, 1.0])
    for k in range(section_count - 1):
        generator = [j * generator[j] for j in range(1, len(generator))]
    abscissae = sorted(root[0] for root in poly_roots(generator))
    vander = [[abscissae[i] ** j for j in range(section_count)] for i in range(section_count)]
    integrals = [[abscissae[i] ** (j + 1) / (j + 1) for j in range(section_count)] for i in range(section_count)]
    butcher = matrix_product(integrals, matrix_inverse(vander))
    inverse = matrix_inverse(butcher)
    coeffs = [0.0] * (section_count + 1)
    coeffs[section_count] = 1.0
    current = [[0.0] * section_count for _ in range(section_count)]
    for k in range(1, section_count + 1):
        current = matrix_product(inverse, current)
        for i in range(section_count):
            current[i][i] = current[i][i] + coeffs[section_count - k + 1]
        applied = matrix_product(inverse, current)
        coeffs[section_count - k] = -sum(applied[i][i] for i in range(section_count)) / k
    eigen_values = poly_roots(coeffs)
    real_pick = 0
    for k in range(section_count):
        if abs(eigen_values[k][1]) < abs(eigen_values[real_pick][1]):
            real_pick = k
    upper_half = [k for k in range(section_count) if eigen_values[k][1] > 1e-9]
    upper_half = sorted(upper_half, key=lambda k: -eigen_values[k][0])
    columns = [[entry[0] for entry in eigen_vector(inverse, (eigen_values[real_pick][0], 0.0))]]
    for k in upper_half:
        vector = eigen_vector(inverse, eigen_values[k])
        columns.append([entry[0] for entry in vector])
        columns.append([entry[1] for entry in vector])
    transform = [[columns[j][i] for j in range(section_count)] for i in range(section_count)]
    inverse_transform = matrix_inverse(transform)
    blocks = matrix_product(matrix_product(inverse_transform, inverse), transform)
    diagonal = [blocks[k][k] for k in range(section_count)]
    coupling = [blocks[k][slab_partner[k]] if slab_partner[k] != k else 0.0 for k in range(section_count)]
    return transform, inverse_transform, diagonal, coupling


def lookup(classes, values_table):
    result = jnp.zeros(classes.shape, jnp.float32)
    for k in range(len(values_table)):
        result = result + jnp.where(classes == k, jnp.float32(values_table[k]), jnp.float32(0.0))
    return result


def series(near_side, far_side):
    return 2.0 * near_side * far_side / (near_side + far_side)


def branch_set(conduct, padded, via_sites, ball_sites, capacity):
    lower_x = series(padded[:, :-2, 1:-1], conduct)
    upper_x = series(conduct, padded[:, 2:, 1:-1])
    lower_y = series(padded[:, 1:-1, :-2], conduct)
    upper_y = series(conduct, padded[:, 1:-1, 2:])
    vertical = jnp.where(via_sites == 1, jnp.float32(via_conductance), jnp.float32(0.0))
    ground = jnp.where(ball_sites == 1, jnp.float32(ball_conductance), jnp.float32(0.0))
    return (capacity, lower_x, upper_x, lower_y, upper_y, vertical, ground)


def layer_terms(vertical, ground, layers):
    zero_plane = jnp.zeros((1,) + vertical.shape[1:], jnp.float32)
    via_above = jnp.concatenate([vertical, zero_plane], axis=0)
    via_below = jnp.concatenate([zero_plane, vertical], axis=0)
    grounded = jnp.concatenate([ground[None], jnp.zeros((layers - 1,) + ground.shape, jnp.float32)], axis=0)
    return via_above, via_below, grounded


def network(voltage, padded_voltage, branches):
    capacity, lower_x, upper_x, lower_y, upper_y, vertical, ground = branches
    via_above, via_below, grounded = layer_terms(vertical, ground, voltage.shape[0])
    branch_total = lower_x + upper_x + lower_y + upper_y + via_above + via_below + grounded
    zero_plane = jnp.zeros((1,) + voltage.shape[1:], jnp.float32)
    volt_above = jnp.concatenate([voltage[1:], zero_plane], axis=0)
    volt_below = jnp.concatenate([zero_plane, voltage[:-1]], axis=0)
    inflow = (upper_x * padded_voltage[:, 2:, 1:-1] + lower_x * padded_voltage[:, :-2, 1:-1]
              + upper_y * padded_voltage[:, 1:-1, 2:] + lower_y * padded_voltage[:, 1:-1, :-2]
              + via_above * volt_above + via_below * volt_below)
    return branch_total * voltage - inflow


def section_sources(load_type, load_table):
    surface = jnp.zeros((SECTIONS,) + load_type.shape, jnp.float32)
    for t in range(LOADS):
        surface = surface + jnp.where((load_type == t)[None], load_table[t][:, None, None], jnp.float32(0.0))
    return surface


def pair_rows(array):
    extent = array.shape
    return array.reshape(extent[:-2] + (extent[-2] // 2, 2, extent[-1])).sum(axis=-2)


def pair_cols(array):
    extent = array.shape
    return array.reshape(extent[:-1] + (extent[-1] // 2, 2)).sum(axis=-1)


def take_rows(array, offset):
    extent = array.shape
    return array.reshape(extent[:-2] + (extent[-2] // 2, 2, extent[-1]))[..., offset, :]


def take_cols(array, offset):
    extent = array.shape
    return array.reshape(extent[:-1] + (extent[-1] // 2, 2))[..., offset]


def block_sum(array):
    return pair_cols(pair_rows(array))


def coarsen(branches):
    capacity, lower_x, upper_x, lower_y, upper_y, vertical, ground = branches
    return (block_sum(capacity), pair_cols(take_rows(lower_x, 0)), pair_cols(take_rows(upper_x, 1)),
            pair_rows(take_cols(lower_y, 0)), pair_rows(take_cols(upper_y, 1)),
            block_sum(vertical), block_sum(ground))


def level_operator(branches, shifts, couple, partner):
    capacity, lower_x, upper_x, lower_y, upper_y, vertical, ground = branches
    via_above, via_below, grounded = layer_terms(vertical, ground, capacity.shape[0])
    branch_total = lower_x + upper_x + lower_y + upper_y + via_above + via_below + grounded
    diagonal = shifts[:, None, None, None] * capacity + branch_total
    coupled = couple[:, None, None, None] * capacity
    diagonal_mate = jnp.stack([diagonal[p] for p in partner])
    coupled_mate = jnp.stack([coupled[p] for p in partner])
    determinant = diagonal * diagonal_mate - coupled * coupled_mate
    self_weight = diagonal_mate / determinant
    mate_weight = -coupled / determinant
    return (lower_x, upper_x, lower_y, upper_y, via_above, via_below, diagonal, coupled, self_weight, mate_weight, partner)


def operate(iterate, operator, neighbours):
    lower_x, upper_x, lower_y, upper_y, via_above, via_below, diagonal, coupled, self_weight, mate_weight, partner = operator
    upper_rows, lower_rows, right_cols, left_cols = neighbours
    zero_plane = jnp.zeros_like(iterate[:, :1])
    from_above = jnp.concatenate([iterate[:, 1:], zero_plane], axis=1)
    from_below = jnp.concatenate([zero_plane, iterate[:, :-1]], axis=1)
    inflow = (upper_x * upper_rows + lower_x * lower_rows + upper_y * right_cols + lower_y * left_cols
              + via_above * from_above + via_below * from_below)
    partner_field = jnp.stack([iterate[p] for p in partner])
    return diagonal * iterate - inflow + coupled * partner_field


def relax(iterate, source, operator, neighbour_fn):
    partner = operator[-1]
    if iterate is None:
        residual = source
    else:
        residual = source - operate(iterate, operator, neighbour_fn(iterate))
    mate_values = jnp.stack([residual[p] for p in partner])
    update = operator[8] * residual + operator[9] * mate_values
    if iterate is None:
        return damping * update
    return iterate + damping * update


def vcycle(operators, level_index, iterate, source, neighbour_fn):
    operator = operators[level_index]
    if level_index == len(operators) - 1:
        for _ in range(COARSE_SWEEPS):
            iterate = relax(iterate, source, operator, neighbour_fn)
        return iterate
    for _ in range(SWEEPS):
        iterate = relax(iterate, source, operator, neighbour_fn)
    residual = source - operate(iterate, operator, neighbour_fn(iterate))
    coarse = vcycle(operators, level_index + 1, None, block_sum(residual), neighbour_fn)
    iterate = iterate + jnp.repeat(jnp.repeat(coarse, 2, axis=2), 2, axis=3)
    for _ in range(SWEEPS):
        iterate = relax(iterate, source, operator, neighbour_fn)
    return iterate


def solve(source, branches, shifts, couple, partner, neighbour_fn):
    operators = []
    for level_index in range(LEVELS):
        if level_index > 0:
            branches = coarsen(branches)
        operators.append(level_operator(branches, shifts, couple, partner))
    iterate = vcycle(operators, 0, None, source, neighbour_fn)
    for _ in range(CYCLES - 1):
        iterate = vcycle(operators, 0, iterate, source, neighbour_fn)
    return iterate


def padded_faces(iterate):
    padded = jnp.pad(iterate, ((0, 0), (0, 0), (1, 1), (1, 1)))
    return padded[:, :, 2:, 1:-1], padded[:, :, :-2, 1:-1], padded[:, :, 1:-1, 2:], padded[:, :, 1:-1, :-2]


def reference(voltage, capacity, node_class, via_sites, ball_sites, load_type, load_table):
    transform, inverse_transform, diagonal_np, coupling_np = radau_tables()
    conduct = lookup(node_class, node_table)
    padded = jnp.pad(conduct, ((0, 0), (1, 1), (1, 1)))
    padded_voltage = jnp.pad(voltage, ((0, 0), (1, 1), (1, 1)))
    branches = branch_set(conduct, padded, via_sites, ball_sites, capacity)
    leakage = network(voltage, padded_voltage, branches)
    surface = section_sources(load_type, load_table)
    forcing = jnp.concatenate([jnp.broadcast_to(-leakage[:-1], (SECTIONS,) + leakage[:-1].shape),
                               (surface - leakage[-1])[:, None]], axis=1)
    transformed = jnp.einsum("jk,klrc->jlrc", jnp.asarray(inverse_transform, jnp.float32), forcing,
                             precision=lax.Precision.HIGHEST)
    shifts = jnp.asarray(diagonal_np, jnp.float32)
    couple = jnp.asarray(coupling_np, jnp.float32)
    solution = solve(transformed, branches, shifts, couple, slab_partner, padded_faces)
    sections = jnp.einsum("jk,klrc->jlrc", jnp.asarray(transform, jnp.float32), solution,
                        precision=lax.Precision.HIGHEST)
    return sections, voltage + sections[SECTIONS - 1]
```

```python
import jax
import jax.numpy as jnp
from jax import lax
from jax.experimental import pallas as pl
from jax.experimental.pallas import tpu as pltpu
from jax.sharding import PartitionSpec as P

SECTIONS = 5
LOADS = 16
LAYERS = 8
LANES = 128
EXT0 = 40
EXT1 = 20
EXT2 = 10
WIDE2 = 14

node_table = (0.35, 0.55, 0.8, 1.1, 1.5, 2.0, 2.7, 3.6)
via_conductance = 2.5
ball_conductance = 4.0
damping = 0.8
slab_partner = (0, 2, 1, 4, 3)


def pair_times(first, second):
    return (
        first[0] * second[0] - first[1] * second[1],
        first[0] * second[1] + first[1] * second[0],
    )


def pair_over(first, second):
    divisor = second[0] * second[0] + second[1] * second[1]
    return (
        (first[0] * second[0] + first[1] * second[1]) / divisor,
        (first[1] * second[0] - first[0] * second[1]) / divisor,
    )


def pair_minus(first, second):
    return (first[0] - second[0], first[1] - second[1])


def poly_value(coeffs, point):
    total = (0.0, 0.0)
    for c in reversed(coeffs):
        total = pair_times(total, point)
        total = (total[0] + c, total[1])
    return total


def poly_product(first, second):
    result = [0.0] * (len(first) + len(second) - 1)
    for i in range(len(first)):
        for j in range(len(second)):
            result[i + j] = result[i + j] + first[i] * second[j]
    return result


def poly_roots(coeffs):
    leading = coeffs[-1]
    scaled = [c / leading for c in coeffs]
    degree = len(coeffs) - 1
    guesses = []
    current = (1.0, 0.0)
    for k in range(degree):
        guesses.append(current)
        current = pair_times(current, (0.4, 0.9))
    for repeat_index in range(800):
        for k in range(degree):
            divisor = (1.0, 0.0)
            for j in range(degree):
                if j != k:
                    divisor = pair_times(divisor, pair_minus(guesses[k], guesses[j]))
            guesses[k] = pair_minus(guesses[k], pair_over(poly_value(scaled, guesses[k]), divisor))
    return guesses


def matrix_product(first, second):
    return [
        [
            sum((first[i][k] * second[k][j] for k in range(len(second))))
            for j in range(len(second[0]))
        ]
        for i in range(len(first))
    ]


def matrix_inverse(matrix):
    order = len(matrix)
    work = [list(matrix[i]) + [1.0 if i == j else 0.0 for j in range(order)] for i in range(order)]
    for column in range(order):
        pivot = column
        for i in range(column + 1, order):
            if abs(work[i][column]) > abs(work[pivot][column]):
                pivot = i
        work[column], work[pivot] = (work[pivot], work[column])
        factor = work[column][column]
        work[column] = [entry / factor for entry in work[column]]
        for i in range(order):
            if i != column:
                scale_row = work[i][column]
                work[i] = [work[i][j] - scale_row * work[column][j] for j in range(2 * order)]
    return [row[order:] for row in work]


def eigen_vector(matrix, value):
    order = len(matrix)
    size_inner = order - 1
    system = []
    for i in range(size_inner):
        row = []
        for j in range(order):
            entry = (matrix[i][j], 0.0)
            if i == j:
                entry = pair_minus(entry, value)
            row.append(entry)
        row[order - 1] = (-row[order - 1][0], -row[order - 1][1])
        system.append(row)
    for column in range(size_inner):
        pivot = column
        for i in range(column + 1, size_inner):
            left_size = system[i][column][0] ** 2 + system[i][column][1] ** 2
            right_size = system[pivot][column][0] ** 2 + system[pivot][column][1] ** 2
            if left_size > right_size:
                pivot = i
        system[column], system[pivot] = (system[pivot], system[column])
        for i in range(size_inner):
            if i != column:
                factor = pair_over(system[i][column], system[column][column])
                system[i] = [
                    pair_minus(system[i][j], pair_times(factor, system[column][j]))
                    for j in range(order)
                ]
    vector = [pair_over(system[i][order - 1], system[i][i]) for i in range(size_inner)]
    vector.append((1.0, 0.0))
    return vector


def radau_tables():
    section_count = 5
    generator = [1.0]
    for k in range(section_count - 1):
        generator = poly_product(generator, [0.0, 1.0])
    for k in range(section_count):
        generator = poly_product(generator, [-1.0, 1.0])
    for k in range(section_count - 1):
        generator = [j * generator[j] for j in range(1, len(generator))]
    abscissae = sorted((root[0] for root in poly_roots(generator)))
    vander = [[abscissae[i] ** j for j in range(section_count)] for i in range(section_count)]
    integrals = [
        [abscissae[i] ** (j + 1) / (j + 1) for j in range(section_count)]
        for i in range(section_count)
    ]
    butcher = matrix_product(integrals, matrix_inverse(vander))
    inverse = matrix_inverse(butcher)
    coeffs = [0.0] * (section_count + 1)
    coeffs[section_count] = 1.0
    current = [[0.0] * section_count for _ in range(section_count)]
    for k in range(1, section_count + 1):
        current = matrix_product(inverse, current)
        for i in range(section_count):
            current[i][i] = current[i][i] + coeffs[section_count - k + 1]
        applied = matrix_product(inverse, current)
        coeffs[section_count - k] = -sum((applied[i][i] for i in range(section_count))) / k
    eigen_values = poly_roots(coeffs)
    real_pick = 0
    for k in range(section_count):
        if abs(eigen_values[k][1]) < abs(eigen_values[real_pick][1]):
            real_pick = k
    upper_half = [k for k in range(section_count) if eigen_values[k][1] > 1e-09]
    upper_half = sorted(upper_half, key=lambda k: -eigen_values[k][0])
    columns = [[entry[0] for entry in eigen_vector(inverse, (eigen_values[real_pick][0], 0.0))]]
    for k in upper_half:
        vector = eigen_vector(inverse, eigen_values[k])
        columns.append([entry[0] for entry in vector])
        columns.append([entry[1] for entry in vector])
    transform = [[columns[j][i] for j in range(section_count)] for i in range(section_count)]
    inverse_transform = matrix_inverse(transform)
    blocks = matrix_product(matrix_product(inverse_transform, inverse), transform)
    diagonal = [blocks[k][k] for k in range(section_count)]
    coupling = [
        blocks[k][slab_partner[k]] if slab_partner[k] != k else 0.0 for k in range(section_count)
    ]
    return (transform, inverse_transform, diagonal, coupling)


TRANSFORM, INVERSE, DIAGONAL, COUPLING = radau_tables()
SHIFTS = (
    DIAGONAL[0],
    0.5 * (DIAGONAL[1] + DIAGONAL[2]),
    0.5 * (DIAGONAL[3] + DIAGONAL[4]),
)
COUPLES = (0.5 * (COUPLING[1] - COUPLING[2]), 0.5 * (COUPLING[3] - COUPLING[4]))
ROW_SUMS = tuple(sum(row) for row in INVERSE)


def from_right(value):
    return pltpu.roll(value, LANES - 1, 1)


def from_left(value):
    return pltpu.roll(value, 1, 1)


def from_above(value):
    return pltpu.roll(value, LAYERS - 1, 0)


def from_below(value):
    return pltpu.roll(value, 1, 0)


def lane_index():
    return lax.broadcasted_iota(jnp.int32, (LAYERS, LANES), 1)


def layer_index():
    return lax.broadcasted_iota(jnp.int32, (LAYERS, LANES), 0)


def unpacked(packs):
    lane = lane_index()
    last = jnp.where(
        lane < 32,
        pltpu.roll(packs[0], 32, 1),
        jnp.where(lane < 64, pltpu.roll(packs[1], 64, 1), pltpu.roll(packs[2], 96, 1)),
    )
    return [packs[0], packs[1], packs[2], last]


def packed(phases):
    lane = lane_index()
    return [
        jnp.where(lane < 96, phases[s], pltpu.roll(phases[3], 96 - 32 * s, 1)) for s in range(3)
    ]


def rows_loop(low, high, body):
    def step(i, carry):
        body(i)
        return carry

    lax.fori_loop(low, high, step, 0)


class Level:
    def __init__(self, phases, gx, gy, via, below, cap, total, weights):
        self.phases = phases
        self.gx, self.gy = gx, gy
        self.via, self.below = via, below
        self.cap, self.total, self.weights = cap, total, weights

    def sides(self, centre, p):
        right = centre[p + 1] if p < self.phases - 1 else from_right(centre[0])
        left = centre[p - 1] if p > 0 else from_left(centre[self.phases - 1])
        return right, left

    def inflow(self, coeffs, centre, p, upper, lower):
        gx_lower, gx_upper, gy_left, gy_right, via, below = coeffs
        right, left = self.sides(centre, p)
        here = centre[p]
        return (
            (gx_upper * upper + gx_lower * lower)
            + (gy_right * right + gy_left * left)
            + (via * from_above(here) + below * from_below(here))
        )

    def coeffs(self, i, p):
        return (
            self.gx[i, p],
            self.gx[i + 1, p],
            self.gy[i, p],
            self.gy[i, p + 1],
            self.via[i, p],
            self.below[i, p],
        )

    def set_total(self, i):
        bottom = layer_index() == 0
        for p in range(self.phases):
            grounded = self.below[i, p]
            below = jnp.where(bottom, 0.0, grounded)
            via = from_above(below)
            total = (
                (self.gx[i, p] + self.gx[i + 1, p])
                + (self.gy[i, p] + self.gy[i, p + 1])
                + (via + grounded)
            )
            self.below[i, p] = below
            self.via[i, p] = via
            self.total[i, p] = total
            cap = self.cap[i, p]
            self.weights[i, p * 5] = damping / (SHIFTS[0] * cap + total)
            for s in range(2):
                direct = SHIFTS[s + 1] * cap + total
                cross = COUPLES[s] * cap
                scale = damping / (direct * direct + cross * cross)
                self.weights[i, p * 5 + 1 + 2 * s] = direct * scale
                self.weights[i, p * 5 + 2 + 2 * s] = -(cross * scale)

    def weighted(self, i, p, values):
        w = [self.weights[i, p * 5 + m] for m in range(5)]
        out = [w[0] * values[0]]
        for s in range(2):
            first, second = values[1 + 2 * s], values[2 + 2 * s]
            out.append(w[1 + 2 * s] * first + w[2 + 2 * s] * second)
            out.append(w[1 + 2 * s] * second - w[2 + 2 * s] * first)
        return out

    def first_relax(self, target, source, low, high):
        def body(i):
            for p in range(self.phases):
                values = [source[i, k * self.phases + p] for k in range(SECTIONS)]
                for k, value in enumerate(self.weighted(i, p, values)):
                    target[i, k * self.phases + p] = value

        rows_loop(low, high, body)

    def gathered(self, iterate, source, i):
        count = self.phases
        centres = [[iterate[i, k * count + p] for p in range(count)] for k in range(SECTIONS)]
        sums = []
        for p in range(count):
            coeffs = self.coeffs(i, p)
            sums.append(
                [
                    source[i, k * count + p]
                    + self.inflow(
                        coeffs,
                        centres[k],
                        p,
                        iterate[i + 1, k * count + p],
                        iterate[i - 1, k * count + p],
                    )
                    for k in range(SECTIONS)
                ]
            )
        return centres, sums

    def relax(self, target, iterate, source, low, high):
        count = self.phases

        def body(i):
            centres, sums = self.gathered(iterate, source, i)
            for p in range(count):
                for k, value in enumerate(self.weighted(i, p, sums[p])):
                    target[i, k * count + p] = (1.0 - damping) * centres[k][p] + value

        rows_loop(low, high, body)

    def residual(self, iterate, source, i):
        centres, sums = self.gathered(iterate, source, i)
        result = []
        for p in range(self.phases):
            cap, total = self.cap[i, p], self.total[i, p]
            x = [centres[k][p] for k in range(SECTIONS)]
            out = [sums[p][0] - (SHIFTS[0] * cap + total) * x[0]]
            for s in range(2):
                direct = SHIFTS[s + 1] * cap + total
                cross = COUPLES[s] * cap
                a, b = 1 + 2 * s, 2 + 2 * s
                out.append(sums[p][a] - (direct * x[a] + cross * x[b]))
                out.append(sums[p][b] - (direct * x[b] - cross * x[a]))
            result.append(out)
        return result

    def restrict(self, target, iterate, source, low, high, shift=0):
        half = self.phases // 2

        def body(row):
            one = self.residual(iterate, source, 2 * row)
            two = self.residual(iterate, source, 2 * row + 1)
            for k in range(SECTIONS):
                for q in range(half):
                    target[row + shift, k * half + q] = (one[2 * q][k] + one[2 * q + 1][k]) + (
                        two[2 * q][k] + two[2 * q + 1][k]
                    )

        rows_loop(low, high, body)

    def correct(self, target, iterate, coarse, low, high, shift=0):
        count, half = self.phases, self.phases // 2

        def body(i):
            row = lax.shift_right_logical(i, 1) + shift
            for k in range(SECTIONS):
                for q in range(half):
                    value = coarse[row, k * half + q]
                    for p in (2 * q, 2 * q + 1):
                        target[i, k * count + p] = iterate[i, k * count + p] + value

        rows_loop(low, high, body)


def coarsen(fine, coarse, rows):
    half = coarse.phases

    def body(row):
        for q in range(half):
            for ref_out, ref_in in ((coarse.cap, fine.cap),):
                ref_out[row, q] = (ref_in[2 * row, 2 * q] + ref_in[2 * row, 2 * q + 1]) + (
                    ref_in[2 * row + 1, 2 * q] + ref_in[2 * row + 1, 2 * q + 1]
                )
        for q in range(half + 1):
            coarse.gy[row, q] = fine.gy[2 * row, 2 * q] + fine.gy[2 * row + 1, 2 * q]

    rows_loop(0, rows, body)

    def body_gx(row):
        for q in range(half):
            coarse.gx[row, q] = fine.gx[2 * row, 2 * q] + fine.gx[2 * row, 2 * q + 1]

    rows_loop(1, rows, body_gx)


def sum_below(fine_below, coarse_below, phases, rows):
    def body(row):
        for q in range(phases):
            coarse_below[row, q] = (
                fine_below[2 * row, 2 * q] + fine_below[2 * row, 2 * q + 1]
            ) + (fine_below[2 * row + 1, 2 * q] + fine_below[2 * row + 1, 2 * q + 1])

    rows_loop(0, rows, body)


def gather_kernel(voltage, capacity, node_class, via, ball, load, whole, left, right, work):
    classes = node_class[...]
    conduct = jnp.full(classes.shape, node_table[0], jnp.float32)
    for c in range(1, len(node_table)):
        conduct = jnp.where(classes == c, node_table[c], conduct)
    grounded = jnp.where(ball[...] == 1, ball_conductance, 0.0)
    upright = jnp.where(via[...] == 1, via_conductance, 0.0)
    for h in range(2):
        half = slice(h * 128, h * 128 + 128)
        work[0, h] = voltage[:, half]
        work[1, h] = capacity[:, half]
        work[2, h] = conduct[:, half]
        work[3, h, 0:8] = grounded[:, half]
        work[3, h, 8:64] = upright[:, half]
    for row in range(8):
        for a in range(4):
            at = (row * 4 + a) * 8
            for h in range(2):
                whole[at : at + 8, h * 128 : h * 128 + 128] = work[
                    a, h, pl.ds(row, 8, stride=8), :
                ]
    whole[256:264] = load[...].astype(jnp.float32)
    left[...] = whole[:, :64]
    right[...] = whole[:, 192:]


def three_parts(value):
    high = value.astype(jnp.bfloat16)
    rest = value - high.astype(jnp.float32)
    middle = rest.astype(jnp.bfloat16)
    low = (rest - middle.astype(jnp.float32)).astype(jnp.bfloat16)
    return high, middle, low


def selected(value, chooser):
    high, middle, low = (
        jnp.dot(part, chooser, preferred_element_type=jnp.float32) for part in three_parts(value)
    )
    return high + (middle + low)


def phase_kernel(whole, from_lower, from_upper, out):
    def chooser(first, count):
        shape = (count, 384)
        column = first + lax.broadcasted_iota(jnp.int32, shape, 0)
        slot = lax.broadcasted_iota(jnp.int32, shape, 1)
        s, lane = slot // 128, slot % 128
        wanted = jnp.where(lane < 96, 4 * lane + s, 4 * (32 * s + lane - 96) + 3)
        return jnp.where(column == wanted, 1.0, 0.0).astype(jnp.bfloat16)

    result = selected(whole[...], chooser(64, 256))
    result = result + selected(from_lower[...], chooser(0, 64))
    result = result + selected(from_upper[...], chooser(320, 64))
    for n in range(33):
        for s in range(3):
            out[n, s] = result[8 * n : 8 * n + 8, 128 * s : 128 * s + 128]


def setup_kernel(
    place, mixed_table, *refs
):
    blocks = refs[:5]
    (gx0, gy0, via0, below0, cap0, total0, weights0, f0, x0) = refs[5:14]
    (gx1, gy1, via1, below1, cap1, total1, weights1, f1, x1) = refs[14:23]
    (gx2, gy2, below2, cap2, f2, go_up, go_down) = refs[23:30]
    volt, conduct, surface, spare0, spare1 = refs[30:35]
    fine = Level(4, gx0, gy0, via0, below0, cap0, total0, weights0)
    middle = Level(2, gx1, gy1, via1, below1, cap1, total1, weights1)
    coarse = Level(1, gx2, gy2, None, below2, cap2, None, None)
    row_block, column_block = place[0], place[1]
    lane = lane_index()

    for b, block in enumerate(blocks):

        def spread(s, block=block, b=b):
            for a, ref in enumerate((volt, cap0, conduct, below0)):
                phases = unpacked([block[4 * s + a, t] for t in range(3)])
                for p in range(4):
                    ref[8 * b + s, p] = phases[p]

        rows_loop(0, 8, spread)
        loads = unpacked([block[32, t] for t in range(3)])
        for p in range(4):
            values = [jnp.zeros((8, LANES), jnp.float32) for _ in range(SECTIONS)]
            for t in range(LOADS):
                chosen = loads[p] == float(t)
                values = [
                    jnp.where(chosen, mixed_table[t, k], values[k]) for k in range(SECTIONS)
                ]
            for k in range(SECTIONS):
                surface[4 * k + p, 8 * b : 8 * b + 8] = values[k]

    def series(near, far):
        return 2.0 * near * far / (near + far)

    def set_gx(i):
        row = 8 * row_block - 16 + i
        inside = jnp.where((row == 0) | (row == 256), 0.0, 1.0).astype(jnp.float32)
        for p in range(4):
            gx0[i, p] = inside * series(conduct[i - 1, p], conduct[i, p])

    rows_loop(1, EXT0, set_gx)
    edge = ((lane == 16) & (column_block == 0)) | ((lane == 80) & (column_block == 3))

    def set_gy(i):
        here = [conduct[i, p] for p in range(4)]
        first = jnp.where(edge, 0.0, series(from_left(here[3]), here[0]))
        gy0[i, 0] = first
        for p in range(1, 4):
            gy0[i, p] = series(here[p - 1], here[p])
        gy0[i, 4] = from_right(first)

    rows_loop(0, EXT0, set_gy)
    coarsen(fine, middle, EXT1)
    sum_below(below0, below1, 2, EXT1)
    coarsen(middle, coarse, EXT2)
    sum_below(below1, below2, 1, EXT2)
    rows_loop(1, EXT0 - 1, fine.set_total)
    rows_loop(1, EXT1 - 1, middle.set_total)

    top = layer_index() == LAYERS - 1

    def set_source(i):
        centre = [volt[i, p] for p in range(4)]
        for p in range(4):
            leak = total0[i, p] * centre[p] - fine.inflow(
                fine.coeffs(i, p), centre, p, volt[i + 1, p], volt[i - 1, p]
            )
            values = []
            for k in range(SECTIONS):
                drawn = jnp.broadcast_to(surface[4 * k + p, pl.ds(i, 1), :], (LAYERS, LANES))
                values.append(jnp.where(top, drawn, 0.0) - ROW_SUMS[k] * leak)
                f0[i, 4 * k + p] = values[k]
            for k, value in enumerate(fine.weighted(i, p, values)):
                spare0[i, 4 * k + p] = value

    rows_loop(1, EXT0 - 1, set_source)
    fine.relax(x0, spare0, f0, 2, 38)
    fine.restrict(f1, x0, f0, 2, 18)
    middle.first_relax(spare1, f1, 2, 18)
    middle.relax(x1, spare1, f1, 3, 17)
    middle.restrict(f2, x1, f1, 2, 8)
    for target, first, outer in ((go_up, 2, 2), (go_down, 4, 6)):
        for j in range(4):
            for k in range(SECTIONS):
                target[5 * j + k] = f2[first + j, k]
        for j in range(2):
            target[20 + 3 * j] = gy2[outer + j, 0]
            target[21 + 3 * j] = below2[outer + j, 0]
            target[22 + 3 * j] = cap2[outer + j, 0]
        for j in range(3):
            target[26 + j] = gx2[outer + j, 0]


def middle_kernel(*refs):
    (gx0, gy0, via0, below0, cap0, total0, weights0, f0, x0) = refs[0:9]
    (gx1, gy1, via1, below1, cap1, total1, weights1, f1, x1) = refs[9:18]
    (gx2, gy2, below2, cap2, f2, from_lower, from_upper) = refs[18:25]
    (x0_out, f1_out, gxw, gyw, viaw, beloww, weightsw) = refs[25:32]
    (capw, totalw, fw, xa, xb, ya, yb, za) = refs[32:40]
    fine = Level(4, gx0, gy0, via0, below0, cap0, total0, weights0)
    middle = Level(2, gx1, gy1, via1, below1, cap1, total1, weights1)
    coarse = Level(1, gxw, gyw, viaw, beloww, capw, totalw, weightsw)
    for j in range(4):
        for k in range(SECTIONS):
            fw[j, k] = from_lower[5 * j + k]
            fw[10 + j, k] = from_upper[5 * j + k]
    for j in range(2):
        for near, source in ((j, from_lower), (12 + j, from_upper)):
            gyw[near, 0] = source[20 + 3 * j]
            gyw[near, 1] = from_right(source[20 + 3 * j])
            beloww[near, 0] = source[21 + 3 * j]
            capw[near, 0] = source[22 + 3 * j]
    for j in range(3):
        gxw[j, 0] = from_lower[26 + j]
        gxw[12 + j, 0] = from_upper[26 + j]
    for j in range(6):
        for k in range(SECTIONS):
            fw[4 + j, k] = f2[2 + j, k]
    for j in range(10):
        gyw[2 + j, 0] = gy2[j, 0]
        gyw[2 + j, 1] = gy2[j, 1]
        beloww[2 + j, 0] = below2[j, 0]
        capw[2 + j, 0] = cap2[j, 0]
    for j in range(1, 10):
        gxw[2 + j, 0] = gx2[j, 0]
    rows_loop(0, WIDE2, coarse.set_total)
    coarse.first_relax(xa, fw, 0, 14)
    coarse.relax(xb, xa, fw, 1, 13)
    coarse.relax(xa, xb, fw, 2, 12)
    coarse.relax(xb, xa, fw, 3, 11)
    middle.correct(ya, x1, xb, 3, 17, 2)
    middle.relax(yb, ya, f1, 4, 16)
    middle.relax(ya, yb, f1, 5, 15)
    fine.correct(za, x0, ya, 10, 30)
    fine.relax(x0_out, za, f0, 11, 29)
    fine.relax(za, x0_out, f0, 12, 28)
    fine.relax(x0_out, za, f0, 13, 27)
    fine.relax(za, x0_out, f0, 14, 26)
    fine.restrict(f1_out, za, f0, 8, 12, -8)

    def keep(i):
        for n in range(20):
            x0_out[i, n] = za[i, n]

    rows_loop(14, 26, keep)


def lower_kernel(*refs):
    (gx1, gy1, via1, below1, cap1, total1, weights1) = refs[0:7]
    own, from_lower, from_upper = refs[7:10]
    f1, x1, f2_out = refs[10:13]
    (xa,) = refs[13:14]
    middle = Level(2, gx1, gy1, via1, below1, cap1, total1, weights1)
    for j in range(4):
        for n in range(10):
            f1[4 + j, n] = from_lower[j, n]
            f1[8 + j, n] = own[j, n]
            f1[12 + j, n] = from_upper[j, n]
    middle.first_relax(xa, f1, 4, 16)
    middle.relax(x1, xa, f1, 5, 15)
    middle.restrict(f2_out, x1, f1, 3, 7, -3)


def finish_kernel(*refs):
    (gx0, gy0, via0, below0, weights0, f0, x0) = refs[0:7]
    (gx1, gy1, via1, below1, weights1, f1, x1) = refs[7:14]
    (gxw, gyw, viaw, beloww, weightsw, own, from_lower, from_upper, voltage) = refs[14:23]
    sections, next_voltage = refs[23:25]
    fw, xa, xb, ya, yb, za, zb, mixed, turn = refs[25:34]
    fine = Level(4, gx0, gy0, via0, below0, None, None, weights0)
    middle = Level(2, gx1, gy1, via1, below1, None, None, weights1)
    coarse = Level(1, gxw, gyw, viaw, beloww, None, None, weightsw)
    for j in range(4):
        for k in range(SECTIONS):
            fw[1 + j, k] = from_lower[j, k]
            fw[5 + j, k] = own[j, k]
            fw[9 + j, k] = from_upper[j, k]
    coarse.first_relax(xa, fw, 1, 13)
    coarse.relax(xb, xa, fw, 2, 12)
    coarse.relax(xa, xb, fw, 3, 11)
    coarse.relax(xb, xa, fw, 4, 10)
    middle.correct(ya, x1, xb, 5, 15, 2)
    middle.relax(yb, ya, f1, 6, 14)
    middle.relax(ya, yb, f1, 7, 13)
    fine.correct(za, x0, ya, 14, 26)
    fine.relax(zb, za, f0, 15, 25)
    fine.relax(za, zb, f0, 16, 24)

    def mix(row):
        for p in range(4):
            values = [za[16 + row, 4 * k + p] for k in range(SECTIONS)]
            for j in range(SECTIONS):
                total = TRANSFORM[j][0] * values[0]
                for k in range(1, SECTIONS):
                    total = total + TRANSFORM[j][k] * values[k]
                mixed[p, 8 * j + row] = total

    rows_loop(0, 8, mix)
    result = None
    for p in range(4):
        lane = lax.broadcasted_iota(jnp.int32, (LANES, 256), 0)
        column = lax.broadcasted_iota(jnp.int32, (LANES, 256), 1)
        chooser = jnp.where(column == 4 * (lane - 16) + p, 1.0, 0.0).astype(jnp.bfloat16)
        part = selected(mixed[p].reshape(320, LANES), chooser)
        result = part if result is None else result + part
    for j in range(SECTIONS):
        for row in range(8):
            at = (8 * j + row) * 8
            for h in range(2):
                turn[j, h, pl.ds(row, 8, stride=8), :] = result[
                    at : at + 8, h * 128 : h * 128 + 128
                ]
        for h in range(2):
            sections[j, :, h * 128 : h * 128 + 128] = turn[j, h]
    next_voltage[...] = voltage[...] + sections[SECTIONS - 1]


VMEM = pltpu.MemorySpace.VMEM
SMEM = pltpu.MemorySpace.SMEM


def vregs(*shape):
    return jax.ShapeDtypeStruct(shape + (LAYERS, LANES), jnp.float32)


def scratch(*shape):
    return pltpu.VMEM(shape + (LAYERS, LANES), jnp.float32)


def call(kernel, inputs, outs, scratches=(), scalars=0):
    return pl.pallas_call(
        kernel,
        out_shape=outs,
        in_specs=[pl.BlockSpec(memory_space=SMEM)] * scalars
        + [pl.BlockSpec(memory_space=VMEM)] * (len(inputs) - scalars),
        out_specs=[pl.BlockSpec(memory_space=VMEM)] * len(outs),
        scratch_shapes=list(scratches),
        compiler_params=pltpu.CompilerParams(vmem_limit_bytes=60 * 2**20),
    )(*inputs)


def turned(value, axis, count, shift):
    return lax.ppermute(value, axis, [(i, (i + shift) % count) for i in range(count)])


ROWS = ("section", "gx")


def local(voltage, capacity, node_class, via_sites, ball_sites, load_type, load_table):
    rows = lax.axis_size("section") * lax.axis_size("gx")
    columns = lax.axis_size("gy")
    volts = voltage.reshape(64, 256)
    whole, left, right = call(
        gather_kernel,
        (
            volts,
            capacity.reshape(64, 256),
            node_class.reshape(64, 256),
            via_sites.reshape(56, 256),
            ball_sites,
            load_type,
        ),
        [
            jax.ShapeDtypeStruct((264, 256), jnp.float32),
            jax.ShapeDtypeStruct((264, 64), jnp.float32),
            jax.ShapeDtypeStruct((264, 64), jnp.float32),
        ],
        [pltpu.VMEM((4, 2, 64, LANES), jnp.float32)],
    )
    from_lower = turned(right, "gy", columns, 1)
    from_upper = turned(left, "gy", columns, -1)
    mixed_table = jnp.einsum(
        "tk,jk->tj", load_table, jnp.asarray(INVERSE, jnp.float32), precision=lax.Precision.HIGHEST
    )
    place = jnp.stack(
        [
            lax.axis_index("section") * lax.axis_size("gx") + lax.axis_index("gx"),
            lax.axis_index("gy"),
        ]
    ).astype(jnp.int32)
    (block,) = call(phase_kernel, (whole, from_lower, from_upper), [vregs(33, 3)])
    blocks = [turned(block, ROWS, rows, s) if s else block for s in (2, 1, 0, -1, -2)]
    level0 = [
        vregs(EXT0, 4),
        vregs(EXT0, 5),
        vregs(EXT0, 4),
        vregs(EXT0, 4),
        vregs(EXT0, 4),
        vregs(EXT0, 4),
        vregs(EXT0, 20),
        vregs(EXT0, 20),
        vregs(EXT0, 20),
    ]
    level1 = [
        vregs(EXT1, 2),
        vregs(EXT1, 3),
        vregs(EXT1, 2),
        vregs(EXT1, 2),
        vregs(EXT1, 2),
        vregs(EXT1, 2),
        vregs(EXT1, 10),
        vregs(EXT1, 10),
        vregs(EXT1, 10),
    ]
    level2 = [vregs(EXT2, 1), vregs(EXT2, 2), vregs(EXT2, 1), vregs(EXT2, 1), vregs(EXT2, 5)]
    state = call(
        setup_kernel,
        (place, mixed_table, *blocks),
        level0 + level1 + level2 + [vregs(29), vregs(29)],
        [
            scratch(EXT0, 4),
            scratch(EXT0, 4),
            pltpu.VMEM((20, EXT0, LANES), jnp.float32),
            scratch(EXT0, 20),
            scratch(EXT1, 10),
        ],
        2,
    )
    fine, middle, coarse = state[0:9], state[9:18], state[18:23]
    go_up, go_down = state[23:25]
    lower = turned(go_up, ROWS, rows, 2)
    upper = turned(go_down, ROWS, rows, -2)
    x0, f1_own, gxw, gyw, viaw, beloww, weightsw = call(
        middle_kernel,
        (*fine, *middle, *coarse, lower, upper),
        [
            vregs(EXT0, 20),
            vregs(4, 10),
            vregs(WIDE2 + 1, 1),
            vregs(WIDE2, 2),
            vregs(WIDE2, 1),
            vregs(WIDE2, 1),
            vregs(WIDE2, 5),
        ],
        [
            scratch(WIDE2, 1),
            scratch(WIDE2, 1),
            scratch(WIDE2, 5),
            scratch(WIDE2, 5),
            scratch(WIDE2, 5),
            scratch(EXT1, 10),
            scratch(EXT1, 10),
            scratch(EXT0, 20),
        ],
    )
    lower = turned(f1_own, ROWS, rows, 1)
    upper = turned(f1_own, ROWS, rows, -1)
    f1, x1, f2_own = call(
        lower_kernel,
        (*middle[:7], f1_own, lower, upper),
        [vregs(EXT1, 10), vregs(EXT1, 10), vregs(4, 5)],
        [scratch(EXT1, 10)],
    )
    lower = turned(f2_own, ROWS, rows, 2)
    upper = turned(f2_own, ROWS, rows, -2)
    sections, next_voltage = call(
        finish_kernel,
        (
            *fine[:4],
            *fine[6:8],
            x0,
            *middle[:4],
            middle[6],
            f1,
            x1,
            gxw,
            gyw,
            viaw,
            beloww,
            weightsw,
            f2_own,
            lower,
            upper,
            volts,
        ),
        [
            jax.ShapeDtypeStruct((SECTIONS, 64, 256), jnp.float32),
            jax.ShapeDtypeStruct((64, 256), jnp.float32),
        ],
        [
            scratch(WIDE2, 5),
            scratch(WIDE2, 5),
            scratch(WIDE2, 5),
            scratch(EXT1, 10),
            scratch(EXT1, 10),
            scratch(EXT0, 20),
            scratch(EXT0, 20),
            scratch(4, 40),
            pltpu.VMEM((SECTIONS, 2, 64, LANES), jnp.float32),
        ],
    )
    return sections.reshape((SECTIONS,) + voltage.shape), next_voltage.reshape(voltage.shape)


def solution(mesh):
    return jax.shard_map(
        local,
        mesh=mesh,
        in_specs=(
            P(None, ("section", "gx"), "gy"),
            P(None, ("section", "gx"), "gy"),
            P(None, ("section", "gx"), "gy"),
            P(None, ("section", "gx"), "gy"),
            P(("section", "gx"), "gy"),
            P(("section", "gx"), "gy"),
            P(),
        ),
        out_specs=(P(None, None, ("section", "gx"), "gy"), P(None, ("section", "gx"), "gy")),
        check_vma=False,
    )
```

```python
import jax
import jax.numpy as jnp
from jax import lax
from jax.experimental import pallas as pl
from jax.experimental.pallas import tpu as pltpu
from jax.sharding import PartitionSpec as P

SECTIONS = 5
LOADS = 16
LAYERS = 8
LANES = 128
EXT0 = 40
EXT1 = 20
EXT2 = 10
WIDE2 = 14

node_table = (0.35, 0.55, 0.8, 1.1, 1.5, 2.0, 2.7, 3.6)
via_conductance = 2.5
ball_conductance = 4.0
damping = 0.8
slab_partner = (0, 2, 1, 4, 3)


def pair_times(first, second):
    return (
        first[0] * second[0] - first[1] * second[1],
        first[0] * second[1] + first[1] * second[0],
    )


def pair_over(first, second):
    divisor = second[0] * second[0] + second[1] * second[1]
    return (
        (first[0] * second[0] + first[1] * second[1]) / divisor,
        (first[1] * second[0] - first[0] * second[1]) / divisor,
    )


def pair_minus(first, second):
    return (first[0] - second[0], first[1] - second[1])


def poly_value(coeffs, point):
    total = (0.0, 0.0)
    for c in reversed(coeffs):
        total = pair_times(total, point)
        total = (total[0] + c, total[1])
    return total


def poly_product(first, second):
    result = [0.0] * (len(first) + len(second) - 1)
    for i in range(len(first)):
        for j in range(len(second)):
            result[i + j] = result[i + j] + first[i] * second[j]
    return result


def poly_roots(coeffs):
    leading = coeffs[-1]
    scaled = [c / leading for c in coeffs]
    degree = len(coeffs) - 1
    guesses = []
    current = (1.0, 0.0)
    for k in range(degree):
        guesses.append(current)
        current = pair_times(current, (0.4, 0.9))
    for repeat_index in range(800):
        for k in range(degree):
            divisor = (1.0, 0.0)
            for j in range(degree):
                if j != k:
                    divisor = pair_times(divisor, pair_minus(guesses[k], guesses[j]))
            guesses[k] = pair_minus(guesses[k], pair_over(poly_value(scaled, guesses[k]), divisor))
    return guesses


def matrix_product(first, second):
    return [
        [
            sum((first[i][k] * second[k][j] for k in range(len(second))))
            for j in range(len(second[0]))
        ]
        for i in range(len(first))
    ]


def matrix_inverse(matrix):
    order = len(matrix)
    work = [list(matrix[i]) + [1.0 if i == j else 0.0 for j in range(order)] for i in range(order)]
    for column in range(order):
        pivot = column
        for i in range(column + 1, order):
            if abs(work[i][column]) > abs(work[pivot][column]):
                pivot = i
        work[column], work[pivot] = (work[pivot], work[column])
        factor = work[column][column]
        work[column] = [entry / factor for entry in work[column]]
        for i in range(order):
            if i != column:
                scale_row = work[i][column]
                work[i] = [work[i][j] - scale_row * work[column][j] for j in range(2 * order)]
    return [row[order:] for row in work]


def eigen_vector(matrix, value):
    order = len(matrix)
    size_inner = order - 1
    system = []
    for i in range(size_inner):
        row = []
        for j in range(order):
            entry = (matrix[i][j], 0.0)
            if i == j:
                entry = pair_minus(entry, value)
            row.append(entry)
        row[order - 1] = (-row[order - 1][0], -row[order - 1][1])
        system.append(row)
    for column in range(size_inner):
        pivot = column
        for i in range(column + 1, size_inner):
            left_size = system[i][column][0] ** 2 + system[i][column][1] ** 2
            right_size = system[pivot][column][0] ** 2 + system[pivot][column][1] ** 2
            if left_size > right_size:
                pivot = i
        system[column], system[pivot] = (system[pivot], system[column])
        for i in range(size_inner):
            if i != column:
                factor = pair_over(system[i][column], system[column][column])
                system[i] = [
                    pair_minus(system[i][j], pair_times(factor, system[column][j]))
                    for j in range(order)
                ]
    vector = [pair_over(system[i][order - 1], system[i][i]) for i in range(size_inner)]
    vector.append((1.0, 0.0))
    return vector


def radau_tables():
    section_count = 5
    generator = [1.0]
    for k in range(section_count - 1):
        generator = poly_product(generator, [0.0, 1.0])
    for k in range(section_count):
        generator = poly_product(generator, [-1.0, 1.0])
    for k in range(section_count - 1):
        generator = [j * generator[j] for j in range(1, len(generator))]
    abscissae = sorted((root[0] for root in poly_roots(generator)))
    vander = [[abscissae[i] ** j for j in range(section_count)] for i in range(section_count)]
    integrals = [
        [abscissae[i] ** (j + 1) / (j + 1) for j in range(section_count)]
        for i in range(section_count)
    ]
    butcher = matrix_product(integrals, matrix_inverse(vander))
    inverse = matrix_inverse(butcher)
    coeffs = [0.0] * (section_count + 1)
    coeffs[section_count] = 1.0
    current = [[0.0] * section_count for _ in range(section_count)]
    for k in range(1, section_count + 1):
        current = matrix_product(inverse, current)
        for i in range(section_count):
            current[i][i] = current[i][i] + coeffs[section_count - k + 1]
        applied = matrix_product(inverse, current)
        coeffs[section_count - k] = -sum((applied[i][i] for i in range(section_count))) / k
    eigen_values = poly_roots(coeffs)
    real_pick = 0
    for k in range(section_count):
        if abs(eigen_values[k][1]) < abs(eigen_values[real_pick][1]):
            real_pick = k
    upper_half = [k for k in range(section_count) if eigen_values[k][1] > 1e-09]
    upper_half = sorted(upper_half, key=lambda k: -eigen_values[k][0])
    columns = [[entry[0] for entry in eigen_vector(inverse, (eigen_values[real_pick][0], 0.0))]]
    for k in upper_half:
        vector = eigen_vector(inverse, eigen_values[k])
        columns.append([entry[0] for entry in vector])
        columns.append([entry[1] for entry in vector])
    transform = [[columns[j][i] for j in range(section_count)] for i in range(section_count)]
    inverse_transform = matrix_inverse(transform)
    blocks = matrix_product(matrix_product(inverse_transform, inverse), transform)
    diagonal = [blocks[k][k] for k in range(section_count)]
    coupling = [
        blocks[k][slab_partner[k]] if slab_partner[k] != k else 0.0 for k in range(section_count)
    ]
    return (transform, inverse_transform, diagonal, coupling)


TRANSFORM, INVERSE, DIAGONAL, COUPLING = radau_tables()
SHIFTS = (
    DIAGONAL[0],
    0.5 * (DIAGONAL[1] + DIAGONAL[2]),
    0.5 * (DIAGONAL[3] + DIAGONAL[4]),
)
COUPLES = (0.5 * (COUPLING[1] - COUPLING[2]), 0.5 * (COUPLING[3] - COUPLING[4]))
ROW_SUMS = tuple(sum(row) for row in INVERSE)


def from_right(value):
    return pltpu.roll(value, LANES - 1, 1)


def from_left(value):
    return pltpu.roll(value, 1, 1)


def from_above(value):
    return pltpu.roll(value, LAYERS - 1, 0)


def from_below(value):
    return pltpu.roll(value, 1, 0)


def lane_index():
    return lax.broadcasted_iota(jnp.int32, (LAYERS, LANES), 1)


def layer_index():
    return lax.broadcasted_iota(jnp.int32, (LAYERS, LANES), 0)


def unpacked(packs):
    lane = lane_index()
    last = jnp.where(
        lane < 32,
        pltpu.roll(packs[0], 32, 1),
        jnp.where(lane < 64, pltpu.roll(packs[1], 64, 1), pltpu.roll(packs[2], 96, 1)),
    )
    return [packs[0], packs[1], packs[2], last]


def packed(phases):
    lane = lane_index()
    return [
        jnp.where(lane < 96, phases[s], pltpu.roll(phases[3], 96 - 32 * s, 1)) for s in range(3)
    ]


def rows_loop(low, high, body, unroll=2):
    steps = (high - low) // unroll

    def step(n, carry):
        for j in range(unroll):
            body(low + n * unroll + j)
        return carry

    if steps > 1:
        lax.fori_loop(0, steps, step, 0)
    elif steps == 1:
        step(0, 0)
    for i in range(low + steps * unroll, high):
        body(i)


class Level:
    def __init__(self, phases, gx, gy, via, below, cap, total, weights):
        self.phases = phases
        self.unroll = 8 // phases
        self.gx, self.gy = gx, gy
        self.via, self.below = via, below
        self.cap, self.total, self.weights = cap, total, weights

    def sides(self, centre, p):
        right = centre[p + 1] if p < self.phases - 1 else from_right(centre[0])
        left = centre[p - 1] if p > 0 else from_left(centre[self.phases - 1])
        return right, left

    def inflow(self, coeffs, centre, p, upper, lower):
        gx_lower, gx_upper, gy_left, gy_right, via, below = coeffs
        right, left = self.sides(centre, p)
        here = centre[p]
        return (
            (gx_upper * upper + gx_lower * lower)
            + (gy_right * right + gy_left * left)
            + (via * from_above(here) + below * from_below(here))
        )

    def coeffs(self, i, p):
        return (
            self.gx[i, p],
            self.gx[i + 1, p],
            self.gy[i, p],
            self.gy[i, p + 1],
            self.via[i, p],
            self.below[i, p],
        )

    def set_total(self, i):
        bottom = layer_index() == 0
        for p in range(self.phases):
            grounded = self.below[i, p]
            below = jnp.where(bottom, 0.0, grounded)
            via = from_above(below)
            total = (
                (self.gx[i, p] + self.gx[i + 1, p])
                + (self.gy[i, p] + self.gy[i, p + 1])
                + (via + grounded)
            )
            self.below[i, p] = below
            self.via[i, p] = via
            self.total[i, p] = total
            cap = self.cap[i, p]
            self.weights[i, p * 5] = damping / (SHIFTS[0] * cap + total)
            for s in range(2):
                direct = SHIFTS[s + 1] * cap + total
                cross = COUPLES[s] * cap
                scale = damping / (direct * direct + cross * cross)
                self.weights[i, p * 5 + 1 + 2 * s] = direct * scale
                self.weights[i, p * 5 + 2 + 2 * s] = -(cross * scale)

    def weighted(self, i, p, values):
        w = [self.weights[i, p * 5 + m] for m in range(5)]
        out = [w[0] * values[0]]
        for s in range(2):
            first, second = values[1 + 2 * s], values[2 + 2 * s]
            out.append(w[1 + 2 * s] * first + w[2 + 2 * s] * second)
            out.append(w[1 + 2 * s] * second - w[2 + 2 * s] * first)
        return out

    def first_relax(self, target, source, low, high):
        def body(i):
            for p in range(self.phases):
                values = [source[i, k * self.phases + p] for k in range(SECTIONS)]
                for k, value in enumerate(self.weighted(i, p, values)):
                    target[i, k * self.phases + p] = value

        rows_loop(low, high, body, self.unroll)

    def gathered(self, iterate, source, i):
        count = self.phases
        centres = [[iterate[i, k * count + p] for p in range(count)] for k in range(SECTIONS)]
        sums = []
        for p in range(count):
            coeffs = self.coeffs(i, p)
            sums.append(
                [
                    source[i, k * count + p]
                    + self.inflow(
                        coeffs,
                        centres[k],
                        p,
                        iterate[i + 1, k * count + p],
                        iterate[i - 1, k * count + p],
                    )
                    for k in range(SECTIONS)
                ]
            )
        return centres, sums

    def relax(self, target, iterate, source, low, high):
        count = self.phases

        def body(i):
            centres, sums = self.gathered(iterate, source, i)
            for p in range(count):
                for k, value in enumerate(self.weighted(i, p, sums[p])):
                    target[i, k * count + p] = (1.0 - damping) * centres[k][p] + value

        rows_loop(low, high, body, self.unroll)

    def residual(self, iterate, source, i):
        centres, sums = self.gathered(iterate, source, i)
        result = []
        for p in range(self.phases):
            cap, total = self.cap[i, p], self.total[i, p]
            x = [centres[k][p] for k in range(SECTIONS)]
            out = [sums[p][0] - (SHIFTS[0] * cap + total) * x[0]]
            for s in range(2):
                direct = SHIFTS[s + 1] * cap + total
                cross = COUPLES[s] * cap
                a, b = 1 + 2 * s, 2 + 2 * s
                out.append(sums[p][a] - (direct * x[a] + cross * x[b]))
                out.append(sums[p][b] - (direct * x[b] - cross * x[a]))
            result.append(out)
        return result

    def restrict(self, target, iterate, source, low, high, shift=0):
        half = self.phases // 2

        def body(row):
            one = self.residual(iterate, source, 2 * row)
            two = self.residual(iterate, source, 2 * row + 1)
            for k in range(SECTIONS):
                for q in range(half):
                    target[row + shift, k * half + q] = (one[2 * q][k] + one[2 * q + 1][k]) + (
                        two[2 * q][k] + two[2 * q + 1][k]
                    )

        rows_loop(low, high, body, self.unroll // 2)

    def correct(self, target, iterate, coarse, low, high, shift=0):
        count, half = self.phases, self.phases // 2

        def body(i):
            row = lax.shift_right_logical(i, 1) + shift
            for k in range(SECTIONS):
                for q in range(half):
                    value = coarse[row, k * half + q]
                    for p in (2 * q, 2 * q + 1):
                        target[i, k * count + p] = iterate[i, k * count + p] + value

        rows_loop(low, high, body, self.unroll)


def coarsen(fine, coarse, rows):
    half = coarse.phases

    def body(row):
        for q in range(half):
            for ref_out, ref_in in ((coarse.cap, fine.cap),):
                ref_out[row, q] = (ref_in[2 * row, 2 * q] + ref_in[2 * row, 2 * q + 1]) + (
                    ref_in[2 * row + 1, 2 * q] + ref_in[2 * row + 1, 2 * q + 1]
                )
        for q in range(half + 1):
            coarse.gy[row, q] = fine.gy[2 * row, 2 * q] + fine.gy[2 * row + 1, 2 * q]

    rows_loop(0, rows, body)

    def body_gx(row):
        for q in range(half):
            coarse.gx[row, q] = fine.gx[2 * row, 2 * q] + fine.gx[2 * row, 2 * q + 1]

    rows_loop(1, rows, body_gx)


def sum_below(fine_below, coarse_below, phases, rows):
    def body(row):
        for q in range(phases):
            coarse_below[row, q] = (
                fine_below[2 * row, 2 * q] + fine_below[2 * row, 2 * q + 1]
            ) + (fine_below[2 * row + 1, 2 * q] + fine_below[2 * row + 1, 2 * q + 1])

    rows_loop(0, rows, body)


def gather_kernel(*refs):
    whole, left, right, work = refs[6:10]
    voltage, capacity, node_class, via, ball, load = refs[10:16]
    copies = [
        pltpu.make_async_copy(source, target, refs[16].at[n])
        for n, (source, target) in enumerate(zip(refs[:6], refs[10:16]))
    ]
    for copy in copies:
        copy.start()
    for copy in copies:
        copy.wait()
    classes = node_class[...]
    conduct = jnp.full(classes.shape, node_table[0], jnp.float32)
    for c in range(1, len(node_table)):
        conduct = jnp.where(classes == c, node_table[c], conduct)
    grounded = jnp.where(ball[...] == 1, ball_conductance, 0.0)
    upright = jnp.where(via[...] == 1, via_conductance, 0.0)
    for h in range(2):
        half = slice(h * 128, h * 128 + 128)
        work[0, h] = voltage[:, half]
        work[1, h] = capacity[:, half]
        work[2, h] = conduct[:, half]
        work[3, h, 0:8] = grounded[:, half]
        work[3, h, 8:64] = upright[:, half]
    for row in range(8):
        for a in range(4):
            at = (row * 4 + a) * 8
            for h in range(2):
                whole[at : at + 8, h * 128 : h * 128 + 128] = work[
                    a, h, pl.ds(row, 8, stride=8), :
                ]
    whole[256:264] = load[...].astype(jnp.float32)
    left[...] = whole[:, :64]
    right[...] = whole[:, 192:]


def three_parts(value):
    high = value.astype(jnp.bfloat16)
    rest = value - high.astype(jnp.float32)
    middle = rest.astype(jnp.bfloat16)
    low = (rest - middle.astype(jnp.float32)).astype(jnp.bfloat16)
    return high, middle, low


def selected(value, chooser):
    high, middle, low = (
        jnp.dot(part, chooser, preferred_element_type=jnp.float32) for part in three_parts(value)
    )
    return high + (middle + low)


def phase_kernel(whole, from_lower, from_upper, out):
    def chooser(first, count):
        shape = (count, 384)
        column = first + lax.broadcasted_iota(jnp.int32, shape, 0)
        slot = lax.broadcasted_iota(jnp.int32, shape, 1)
        s, lane = slot // 128, slot % 128
        wanted = jnp.where(lane < 96, 4 * lane + s, 4 * (32 * s + lane - 96) + 3)
        return jnp.where(column == wanted, 1.0, 0.0).astype(jnp.bfloat16)

    result = selected(whole[...], chooser(64, 256))
    result = result + selected(from_lower[...], chooser(0, 64))
    result = result + selected(from_upper[...], chooser(320, 64))
    for n in range(33):
        for s in range(3):
            out[n, s] = result[8 * n : 8 * n + 8, 128 * s : 128 * s + 128]


def setup_kernel(
    place, mixed_table, *refs
):
    blocks = refs[:5]
    (gx0, gy0, via0, below0, cap0, total0, weights0, f0, x0) = refs[5:14]
    (gx1, gy1, via1, below1, cap1, total1, weights1, f1, x1) = refs[14:23]
    (gx2, gy2, below2, cap2, f2, go_up, go_down) = refs[23:30]
    volt, conduct, surface, spare0, spare1 = refs[30:35]
    fine = Level(4, gx0, gy0, via0, below0, cap0, total0, weights0)
    middle = Level(2, gx1, gy1, via1, below1, cap1, total1, weights1)
    coarse = Level(1, gx2, gy2, None, below2, cap2, None, None)
    row_block, column_block = place[0], place[1]
    lane = lane_index()

    for b, block in enumerate(blocks):

        def spread(s, block=block, b=b):
            for a, ref in enumerate((volt, cap0, conduct, below0)):
                phases = unpacked([block[4 * s + a, t] for t in range(3)])
                for p in range(4):
                    ref[8 * b + s, p] = phases[p]

        rows_loop(0, 8, spread)
        loads = unpacked([block[32, t] for t in range(3)])
        for p in range(4):
            values = [jnp.zeros((8, LANES), jnp.float32) for _ in range(SECTIONS)]
            for t in range(LOADS):
                chosen = loads[p] == float(t)
                values = [
                    jnp.where(chosen, mixed_table[t, k], values[k]) for k in range(SECTIONS)
                ]
            for k in range(SECTIONS):
                surface[4 * k + p, 8 * b : 8 * b + 8] = values[k]

    def series(near, far):
        return 2.0 * near * far / (near + far)

    def set_gx(i):
        row = 8 * row_block - 16 + i
        inside = jnp.where((row == 0) | (row == 256), 0.0, 1.0).astype(jnp.float32)
        for p in range(4):
            gx0[i, p] = inside * series(conduct[i - 1, p], conduct[i, p])

    rows_loop(1, EXT0, set_gx)
    edge = ((lane == 16) & (column_block == 0)) | ((lane == 80) & (column_block == 3))

    def set_gy(i):
        here = [conduct[i, p] for p in range(4)]
        first = jnp.where(edge, 0.0, series(from_left(here[3]), here[0]))
        gy0[i, 0] = first
        for p in range(1, 4):
            gy0[i, p] = series(here[p - 1], here[p])
        gy0[i, 4] = from_right(first)

    rows_loop(0, EXT0, set_gy)
    coarsen(fine, middle, EXT1)
    sum_below(below0, below1, 2, EXT1)
    coarsen(middle, coarse, EXT2)
    sum_below(below1, below2, 1, EXT2)
    rows_loop(1, EXT0 - 1, fine.set_total)
    rows_loop(1, EXT1 - 1, middle.set_total)

    top = layer_index() == LAYERS - 1

    def set_source(i):
        centre = [volt[i, p] for p in range(4)]
        for p in range(4):
            leak = total0[i, p] * centre[p] - fine.inflow(
                fine.coeffs(i, p), centre, p, volt[i + 1, p], volt[i - 1, p]
            )
            values = []
            for k in range(SECTIONS):
                drawn = jnp.broadcast_to(surface[4 * k + p, pl.ds(i, 1), :], (LAYERS, LANES))
                values.append(jnp.where(top, drawn, 0.0) - ROW_SUMS[k] * leak)
                f0[i, 4 * k + p] = values[k]
            for k, value in enumerate(fine.weighted(i, p, values)):
                spare0[i, 4 * k + p] = value

    rows_loop(1, EXT0 - 1, set_source)
    fine.relax(x0, spare0, f0, 2, 38)
    fine.restrict(f1, x0, f0, 2, 18)
    middle.first_relax(spare1, f1, 2, 18)
    middle.relax(x1, spare1, f1, 3, 17)
    middle.restrict(f2, x1, f1, 2, 8)
    for target, first, outer in ((go_up, 2, 2), (go_down, 4, 6)):
        for j in range(4):
            for k in range(SECTIONS):
                target[5 * j + k] = f2[first + j, k]
        for j in range(2):
            target[20 + 3 * j] = gy2[outer + j, 0]
            target[21 + 3 * j] = below2[outer + j, 0]
            target[22 + 3 * j] = cap2[outer + j, 0]
        for j in range(3):
            target[26 + j] = gx2[outer + j, 0]


def middle_kernel(*refs):
    (gx0, gy0, via0, below0, cap0, total0, weights0, f0, x0) = refs[0:9]
    (gx1, gy1, via1, below1, cap1, total1, weights1, f1, x1) = refs[9:18]
    (gx2, gy2, below2, cap2, f2, from_lower, from_upper) = refs[18:25]
    (x0_out, f1_out, gxw, gyw, viaw, beloww, weightsw) = refs[25:32]
    (capw, totalw, fw, xa, xb, ya, yb, za) = refs[32:40]
    fine = Level(4, gx0, gy0, via0, below0, cap0, total0, weights0)
    middle = Level(2, gx1, gy1, via1, below1, cap1, total1, weights1)
    coarse = Level(1, gxw, gyw, viaw, beloww, capw, totalw, weightsw)
    for j in range(4):
        for k in range(SECTIONS):
            fw[j, k] = from_lower[5 * j + k]
            fw[10 + j, k] = from_upper[5 * j + k]
    for j in range(2):
        for near, source in ((j, from_lower), (12 + j, from_upper)):
            gyw[near, 0] = source[20 + 3 * j]
            gyw[near, 1] = from_right(source[20 + 3 * j])
            beloww[near, 0] = source[21 + 3 * j]
            capw[near, 0] = source[22 + 3 * j]
    for j in range(3):
        gxw[j, 0] = from_lower[26 + j]
        gxw[12 + j, 0] = from_upper[26 + j]
    for j in range(6):
        for k in range(SECTIONS):
            fw[4 + j, k] = f2[2 + j, k]
    for j in range(10):
        gyw[2 + j, 0] = gy2[j, 0]
        gyw[2 + j, 1] = gy2[j, 1]
        beloww[2 + j, 0] = below2[j, 0]
        capw[2 + j, 0] = cap2[j, 0]
    for j in range(1, 10):
        gxw[2 + j, 0] = gx2[j, 0]
    rows_loop(0, WIDE2, coarse.set_total)
    coarse.first_relax(xa, fw, 0, 14)
    coarse.relax(xb, xa, fw, 1, 13)
    coarse.relax(xa, xb, fw, 2, 12)
    coarse.relax(xb, xa, fw, 3, 11)
    middle.correct(ya, x1, xb, 3, 17, 2)
    middle.relax(yb, ya, f1, 4, 16)
    middle.relax(ya, yb, f1, 5, 15)
    fine.correct(za, x0, ya, 10, 30)
    fine.relax(x0_out, za, f0, 11, 29)
    fine.relax(za, x0_out, f0, 12, 28)
    fine.relax(x0_out, za, f0, 13, 27)
    fine.relax(za, x0_out, f0, 14, 26)
    fine.restrict(f1_out, za, f0, 8, 12, -8)

    def keep(i):
        for n in range(20):
            x0_out[i, n] = za[i, n]

    rows_loop(14, 26, keep)


def lower_kernel(*refs):
    (gx1, gy1, via1, below1, cap1, total1, weights1) = refs[0:7]
    own, from_lower, from_upper = refs[7:10]
    f1, x1, f2_out = refs[10:13]
    (xa,) = refs[13:14]
    middle = Level(2, gx1, gy1, via1, below1, cap1, total1, weights1)
    for j in range(4):
        for n in range(10):
            f1[4 + j, n] = from_lower[j, n]
            f1[8 + j, n] = own[j, n]
            f1[12 + j, n] = from_upper[j, n]
    middle.first_relax(xa, f1, 4, 16)
    middle.relax(x1, xa, f1, 5, 15)
    middle.restrict(f2_out, x1, f1, 3, 7, -3)


def finish_kernel(*refs):
    (gx0, gy0, via0, below0, weights0, f0, x0) = refs[0:7]
    (gx1, gy1, via1, below1, weights1, f1, x1) = refs[7:14]
    (gxw, gyw, viaw, beloww, weightsw, own, from_lower, from_upper, voltage) = refs[14:23]
    sections, next_voltage = refs[23:25]
    fw, xa, xb, ya, yb, za, zb, mixed, turn = refs[25:34]
    fine = Level(4, gx0, gy0, via0, below0, None, None, weights0)
    middle = Level(2, gx1, gy1, via1, below1, None, None, weights1)
    coarse = Level(1, gxw, gyw, viaw, beloww, None, None, weightsw)
    for j in range(4):
        for k in range(SECTIONS):
            fw[1 + j, k] = from_lower[j, k]
            fw[5 + j, k] = own[j, k]
            fw[9 + j, k] = from_upper[j, k]
    coarse.first_relax(xa, fw, 1, 13)
    coarse.relax(xb, xa, fw, 2, 12)
    coarse.relax(xa, xb, fw, 3, 11)
    coarse.relax(xb, xa, fw, 4, 10)
    middle.correct(ya, x1, xb, 5, 15, 2)
    middle.relax(yb, ya, f1, 6, 14)
    middle.relax(ya, yb, f1, 7, 13)
    fine.correct(za, x0, ya, 14, 26)
    fine.relax(zb, za, f0, 15, 25)
    fine.relax(za, zb, f0, 16, 24)

    def mix(row):
        for p in range(4):
            values = [za[16 + row, 4 * k + p] for k in range(SECTIONS)]
            for j in range(SECTIONS):
                total = TRANSFORM[j][0] * values[0]
                for k in range(1, SECTIONS):
                    total = total + TRANSFORM[j][k] * values[k]
                mixed[p, 8 * j + row] = total

    rows_loop(0, 8, mix)
    result = None
    for p in range(4):
        lane = lax.broadcasted_iota(jnp.int32, (LANES, 256), 0)
        column = lax.broadcasted_iota(jnp.int32, (LANES, 256), 1)
        chooser = jnp.where(column == 4 * (lane - 16) + p, 1.0, 0.0).astype(jnp.bfloat16)
        part = selected(mixed[p].reshape(320, LANES), chooser)
        result = part if result is None else result + part
    for j in range(SECTIONS):
        for row in range(8):
            at = (8 * j + row) * 8
            for h in range(2):
                turn[j, h, pl.ds(row, 8, stride=8), :] = result[
                    at : at + 8, h * 128 : h * 128 + 128
                ]
        for h in range(2):
            sections[j, :, h * 128 : h * 128 + 128] = turn[j, h]
    next_voltage[...] = voltage[...] + sections[SECTIONS - 1]


VMEM = pltpu.MemorySpace.VMEM
SMEM = pltpu.MemorySpace.SMEM


def vregs(*shape):
    return pltpu.VMEM(shape + (LAYERS, LANES), jnp.float32)


def scratch(*shape):
    return pltpu.VMEM(shape + (LAYERS, LANES), jnp.float32)


def call(kernel, inputs, outs, scratches=(), scalars=0, outside=False):
    space = pltpu.MemorySpace.HBM if outside else VMEM
    inputs = [
        value if n < scalars else pltpu.with_memory_space_constraint(value, space)
        for n, value in enumerate(inputs)
    ]
    return pl.pallas_call(
        kernel,
        out_shape=outs,
        in_specs=[pl.BlockSpec(memory_space=SMEM)] * scalars
        + [pl.BlockSpec(memory_space=space)] * (len(inputs) - scalars),
        out_specs=[pl.BlockSpec(memory_space=VMEM)] * len(outs),
        scratch_shapes=list(scratches),
        compiler_params=pltpu.CompilerParams(vmem_limit_bytes=12 * 2**20),
    )(*inputs)


def turned(value, axis, count, shift):
    return lax.ppermute(value, axis, [(i, (i + shift) % count) for i in range(count)])


ROWS = ("section", "gx")


def local(voltage, capacity, node_class, via_sites, ball_sites, load_type, load_table):
    rows = lax.axis_size("section") * lax.axis_size("gx")
    columns = lax.axis_size("gy")
    volts = voltage.reshape(64, 256)
    whole, left, right = call(
        gather_kernel,
        (
            volts,
            capacity.reshape(64, 256),
            node_class.reshape(64, 256),
            via_sites.reshape(56, 256),
            ball_sites,
            load_type,
        ),
        [
            pltpu.VMEM((264, 256), jnp.float32),
            pltpu.VMEM((264, 64), jnp.float32),
            pltpu.VMEM((264, 64), jnp.float32),
        ],
        [
            pltpu.VMEM((4, 2, 64, LANES), jnp.float32),
            pltpu.VMEM((64, 256), jnp.float32),
            pltpu.VMEM((64, 256), jnp.float32),
            pltpu.VMEM((64, 256), jnp.int32),
            pltpu.VMEM((56, 256), jnp.int32),
            pltpu.VMEM((8, 256), jnp.int32),
            pltpu.VMEM((8, 256), jnp.int32),
            pltpu.SemaphoreType.DMA((6,)),
        ],
        outside=True,
    )
    from_lower = turned(right, "gy", columns, 1)
    from_upper = turned(left, "gy", columns, -1)
    mixed_table = jnp.einsum(
        "tk,jk->tj", load_table, jnp.asarray(INVERSE, jnp.float32), precision=lax.Precision.HIGHEST
    )
    place = jnp.stack(
        [
            lax.axis_index("section") * lax.axis_size("gx") + lax.axis_index("gx"),
            lax.axis_index("gy"),
        ]
    ).astype(jnp.int32)
    (block,) = call(phase_kernel, (whole, from_lower, from_upper), [vregs(33, 3)])
    blocks = [turned(block, ROWS, rows, s) if s else block for s in (2, 1, 0, -1, -2)]
    level0 = [
        vregs(EXT0, 4),
        vregs(EXT0, 5),
        vregs(EXT0, 4),
        vregs(EXT0, 4),
        vregs(EXT0, 4),
        vregs(EXT0, 4),
        vregs(EXT0, 20),
        vregs(EXT0, 20),
        vregs(EXT0, 20),
    ]
    level1 = [
        vregs(EXT1, 2),
        vregs(EXT1, 3),
        vregs(EXT1, 2),
        vregs(EXT1, 2),
        vregs(EXT1, 2),
        vregs(EXT1, 2),
        vregs(EXT1, 10),
        vregs(EXT1, 10),
        vregs(EXT1, 10),
    ]
    level2 = [vregs(EXT2, 1), vregs(EXT2, 2), vregs(EXT2, 1), vregs(EXT2, 1), vregs(EXT2, 5)]
    state = call(
        setup_kernel,
        (place, mixed_table, *blocks),
        level0 + level1 + level2 + [vregs(29), vregs(29)],
        [
            scratch(EXT0, 4),
            scratch(EXT0, 4),
            pltpu.VMEM((20, EXT0, LANES), jnp.float32),
            scratch(EXT0, 20),
            scratch(EXT1, 10),
        ],
        2,
    )
    fine, middle, coarse = state[0:9], state[9:18], state[18:23]
    go_up, go_down = state[23:25]
    lower = turned(go_up, ROWS, rows, 2)
    upper = turned(go_down, ROWS, rows, -2)
    x0, f1_own, gxw, gyw, viaw, beloww, weightsw = call(
        middle_kernel,
        (*fine, *middle, *coarse, lower, upper),
        [
            vregs(EXT0, 20),
            vregs(4, 10),
            vregs(WIDE2 + 1, 1),
            vregs(WIDE2, 2),
            vregs(WIDE2, 1),
            vregs(WIDE2, 1),
            vregs(WIDE2, 5),
        ],
        [
            scratch(WIDE2, 1),
            scratch(WIDE2, 1),
            scratch(WIDE2, 5),
            scratch(WIDE2, 5),
            scratch(WIDE2, 5),
            scratch(EXT1, 10),
            scratch(EXT1, 10),
            scratch(EXT0, 20),
        ],
    )
    lower = turned(f1_own, ROWS, rows, 1)
    upper = turned(f1_own, ROWS, rows, -1)
    f1, x1, f2_own = call(
        lower_kernel,
        (*middle[:7], f1_own, lower, upper),
        [vregs(EXT1, 10), vregs(EXT1, 10), vregs(4, 5)],
        [scratch(EXT1, 10)],
    )
    lower = turned(f2_own, ROWS, rows, 2)
    upper = turned(f2_own, ROWS, rows, -2)
    sections, next_voltage = call(
        finish_kernel,
        (
            *fine[:4],
            *fine[6:8],
            x0,
            *middle[:4],
            middle[6],
            f1,
            x1,
            gxw,
            gyw,
            viaw,
            beloww,
            weightsw,
            f2_own,
            lower,
            upper,
            volts,
        ),
        [
            jax.ShapeDtypeStruct((SECTIONS, 64, 256), jnp.float32),
            jax.ShapeDtypeStruct((64, 256), jnp.float32),
        ],
        [
            scratch(WIDE2, 5),
            scratch(WIDE2, 5),
            scratch(WIDE2, 5),
            scratch(EXT1, 10),
            scratch(EXT1, 10),
            scratch(EXT0, 20),
            scratch(EXT0, 20),
            scratch(4, 40),
            pltpu.VMEM((SECTIONS, 2, 64, LANES), jnp.float32),
        ],
    )
    return sections.reshape((SECTIONS,) + voltage.shape), next_voltage.reshape(voltage.shape)


def solution(mesh):
    return jax.shard_map(
        local,
        mesh=mesh,
        in_specs=(
            P(None, ("section", "gx"), "gy"),
            P(None, ("section", "gx"), "gy"),
            P(None, ("section", "gx"), "gy"),
            P(None, ("section", "gx"), "gy"),
            P(("section", "gx"), "gy"),
            P(("section", "gx"), "gy"),
            P(),
        ),
        out_specs=(P(None, None, ("section", "gx"), "gy"), P(None, ("section", "gx"), "gy")),
        check_vma=False,
    )
```

```python
import jax
import jax.numpy as jnp
from jax import lax
from jax.experimental import pallas as pl
from jax.experimental.pallas import tpu as pltpu
from jax.sharding import PartitionSpec as P

SECTIONS = 5
LOADS = 16
LAYERS = 8
LANES = 128
EXT0 = 40
EXT1 = 20
EXT2 = 10
WIDE2 = 14

node_table = (0.35, 0.55, 0.8, 1.1, 1.5, 2.0, 2.7, 3.6)
via_conductance = 2.5
ball_conductance = 4.0
damping = 0.8
slab_partner = (0, 2, 1, 4, 3)


def pair_times(first, second):
    return (
        first[0] * second[0] - first[1] * second[1],
        first[0] * second[1] + first[1] * second[0],
    )


def pair_over(first, second):
    divisor = second[0] * second[0] + second[1] * second[1]
    return (
        (first[0] * second[0] + first[1] * second[1]) / divisor,
        (first[1] * second[0] - first[0] * second[1]) / divisor,
    )


def pair_minus(first, second):
    return (first[0] - second[0], first[1] - second[1])


def poly_value(coeffs, point):
    total = (0.0, 0.0)
    for c in reversed(coeffs):
        total = pair_times(total, point)
        total = (total[0] + c, total[1])
    return total


def poly_product(first, second):
    result = [0.0] * (len(first) + len(second) - 1)
    for i in range(len(first)):
        for j in range(len(second)):
            result[i + j] = result[i + j] + first[i] * second[j]
    return result


def poly_roots(coeffs):
    leading = coeffs[-1]
    scaled = [c / leading for c in coeffs]
    degree = len(coeffs) - 1
    guesses = []
    current = (1.0, 0.0)
    for k in range(degree):
        guesses.append(current)
        current = pair_times(current, (0.4, 0.9))
    for repeat_index in range(800):
        for k in range(degree):
            divisor = (1.0, 0.0)
            for j in range(degree):
                if j != k:
                    divisor = pair_times(divisor, pair_minus(guesses[k], guesses[j]))
            guesses[k] = pair_minus(guesses[k], pair_over(poly_value(scaled, guesses[k]), divisor))
    return guesses


def matrix_product(first, second):
    return [
        [
            sum((first[i][k] * second[k][j] for k in range(len(second))))
            for j in range(len(second[0]))
        ]
        for i in range(len(first))
    ]


def matrix_inverse(matrix):
    order = len(matrix)
    work = [list(matrix[i]) + [1.0 if i == j else 0.0 for j in range(order)] for i in range(order)]
    for column in range(order):
        pivot = column
        for i in range(column + 1, order):
            if abs(work[i][column]) > abs(work[pivot][column]):
                pivot = i
        work[column], work[pivot] = (work[pivot], work[column])
        factor = work[column][column]
        work[column] = [entry / factor for entry in work[column]]
        for i in range(order):
            if i != column:
                scale_row = work[i][column]
                work[i] = [work[i][j] - scale_row * work[column][j] for j in range(2 * order)]
    return [row[order:] for row in work]


def eigen_vector(matrix, value):
    order = len(matrix)
    size_inner = order - 1
    system = []
    for i in range(size_inner):
        row = []
        for j in range(order):
            entry = (matrix[i][j], 0.0)
            if i == j:
                entry = pair_minus(entry, value)
            row.append(entry)
        row[order - 1] = (-row[order - 1][0], -row[order - 1][1])
        system.append(row)
    for column in range(size_inner):
        pivot = column
        for i in range(column + 1, size_inner):
            left_size = system[i][column][0] ** 2 + system[i][column][1] ** 2
            right_size = system[pivot][column][0] ** 2 + system[pivot][column][1] ** 2
            if left_size > right_size:
                pivot = i
        system[column], system[pivot] = (system[pivot], system[column])
        for i in range(size_inner):
            if i != column:
                factor = pair_over(system[i][column], system[column][column])
                system[i] = [
                    pair_minus(system[i][j], pair_times(factor, system[column][j]))
                    for j in range(order)
                ]
    vector = [pair_over(system[i][order - 1], system[i][i]) for i in range(size_inner)]
    vector.append((1.0, 0.0))
    return vector


def radau_tables():
    section_count = 5
    generator = [1.0]
    for k in range(section_count - 1):
        generator = poly_product(generator, [0.0, 1.0])
    for k in range(section_count):
        generator = poly_product(generator, [-1.0, 1.0])
    for k in range(section_count - 1):
        generator = [j * generator[j] for j in range(1, len(generator))]
    abscissae = sorted((root[0] for root in poly_roots(generator)))
    vander = [[abscissae[i] ** j for j in range(section_count)] for i in range(section_count)]
    integrals = [
        [abscissae[i] ** (j + 1) / (j + 1) for j in range(section_count)]
        for i in range(section_count)
    ]
    butcher = matrix_product(integrals, matrix_inverse(vander))
    inverse = matrix_inverse(butcher)
    coeffs = [0.0] * (section_count + 1)
    coeffs[section_count] = 1.0
    current = [[0.0] * section_count for _ in range(section_count)]
    for k in range(1, section_count + 1):
        current = matrix_product(inverse, current)
        for i in range(section_count):
            current[i][i] = current[i][i] + coeffs[section_count - k + 1]
        applied = matrix_product(inverse, current)
        coeffs[section_count - k] = -sum((applied[i][i] for i in range(section_count))) / k
    eigen_values = poly_roots(coeffs)
    real_pick = 0
    for k in range(section_count):
        if abs(eigen_values[k][1]) < abs(eigen_values[real_pick][1]):
            real_pick = k
    upper_half = [k for k in range(section_count) if eigen_values[k][1] > 1e-09]
    upper_half = sorted(upper_half, key=lambda k: -eigen_values[k][0])
    columns = [[entry[0] for entry in eigen_vector(inverse, (eigen_values[real_pick][0], 0.0))]]
    for k in upper_half:
        vector = eigen_vector(inverse, eigen_values[k])
        columns.append([entry[0] for entry in vector])
        columns.append([entry[1] for entry in vector])
    transform = [[columns[j][i] for j in range(section_count)] for i in range(section_count)]
    inverse_transform = matrix_inverse(transform)
    blocks = matrix_product(matrix_product(inverse_transform, inverse), transform)
    diagonal = [blocks[k][k] for k in range(section_count)]
    coupling = [
        blocks[k][slab_partner[k]] if slab_partner[k] != k else 0.0 for k in range(section_count)
    ]
    return (transform, inverse_transform, diagonal, coupling)


TRANSFORM, INVERSE, DIAGONAL, COUPLING = radau_tables()
SHIFTS = (
    DIAGONAL[0],
    0.5 * (DIAGONAL[1] + DIAGONAL[2]),
    0.5 * (DIAGONAL[3] + DIAGONAL[4]),
)
COUPLES = (0.5 * (COUPLING[1] - COUPLING[2]), 0.5 * (COUPLING[3] - COUPLING[4]))
ROW_SUMS = tuple(sum(row) for row in INVERSE)


def from_right(value):
    return pltpu.roll(value, LANES - 1, 1)


def from_left(value):
    return pltpu.roll(value, 1, 1)


def from_above(value):
    return pltpu.roll(value, LAYERS - 1, 0)


def from_below(value):
    return pltpu.roll(value, 1, 0)


def lane_index():
    return lax.broadcasted_iota(jnp.int32, (LAYERS, LANES), 1)


def layer_index():
    return lax.broadcasted_iota(jnp.int32, (LAYERS, LANES), 0)


def spread(first, second, rim):
    own = lane_index() < 64
    inner = (first, pltpu.roll(first, 64, 1), second, pltpu.roll(second, 64, 1))
    outer = (rim, pltpu.roll(rim, 96, 1), pltpu.roll(rim, 64, 1), pltpu.roll(rim, 32, 1))
    return [jnp.where(own, near, far) for near, far in zip(inner, outer)]


def packed(values):
    lane = lane_index()
    dead = (lane >= 80) & (lane < 112)
    one, two, three, last = values
    tail = jnp.where(lane < 96, pltpu.roll(last, 96, 1), pltpu.roll(last, 32, 1))
    return [
        jnp.where(dead, pltpu.roll(last, 80, 1), one),
        jnp.where(dead, pltpu.roll(last, 48, 1), two),
        jnp.where(dead, tail, three),
    ]


def unpacked(packs):
    lane = lane_index()
    one, two, three = packs
    last = jnp.where(
        lane < 64,
        jnp.where(lane < 32, pltpu.roll(one, 48, 1), pltpu.roll(two, 80, 1)),
        jnp.where(lane < 96, pltpu.roll(three, 96, 1), pltpu.roll(three, 32, 1)),
    )
    return [one, two, three, last]


def rows_loop(low, high, body, unroll=2):
    steps = (high - low) // unroll

    def step(n, carry):
        for j in range(unroll):
            body(low + n * unroll + j)
        return carry

    if steps > 1:
        lax.fori_loop(0, steps, step, 0)
    elif steps == 1:
        step(0, 0)
    for i in range(low + steps * unroll, high):
        body(i)


class Level:
    def __init__(self, phases, gx, gy, via, below, cap, total, weights):
        self.phases = phases
        self.unroll = 8 // phases
        self.gx, self.gy = gx, gy
        self.via, self.below = via, below
        self.cap, self.total, self.weights = cap, total, weights

    def sides(self, centre, p):
        right = centre[p + 1] if p < self.phases - 1 else from_right(centre[0])
        left = centre[p - 1] if p > 0 else from_left(centre[self.phases - 1])
        return right, left

    def inflow(self, coeffs, centre, p, upper, lower):
        gx_lower, gx_upper, gy_left, gy_right, via, below = coeffs
        right, left = self.sides(centre, p)
        here = centre[p]
        return (
            (gx_upper * upper + gx_lower * lower)
            + (gy_right * right + gy_left * left)
            + (via * from_above(here) + below * from_below(here))
        )

    def coeffs(self, i, p):
        return (
            self.gx[i, p],
            self.gx[i + 1, p],
            self.gy[i, p],
            self.gy[i, p + 1],
            self.via[i, p],
            self.below[i, p],
        )

    def set_total(self, i):
        bottom = layer_index() == 0
        for p in range(self.phases):
            grounded = self.below[i, p]
            below = jnp.where(bottom, 0.0, grounded)
            via = from_above(below)
            total = (
                (self.gx[i, p] + self.gx[i + 1, p])
                + (self.gy[i, p] + self.gy[i, p + 1])
                + (via + grounded)
            )
            self.below[i, p] = below
            self.via[i, p] = via
            self.total[i, p] = total
            cap = self.cap[i, p]
            self.weights[i, p * 5] = damping / (SHIFTS[0] * cap + total)
            for s in range(2):
                direct = SHIFTS[s + 1] * cap + total
                cross = COUPLES[s] * cap
                scale = damping / (direct * direct + cross * cross)
                self.weights[i, p * 5 + 1 + 2 * s] = direct * scale
                self.weights[i, p * 5 + 2 + 2 * s] = -(cross * scale)

    def weighted(self, i, p, values):
        w = [self.weights[i, p * 5 + m] for m in range(5)]
        out = [w[0] * values[0]]
        for s in range(2):
            first, second = values[1 + 2 * s], values[2 + 2 * s]
            out.append(w[1 + 2 * s] * first + w[2 + 2 * s] * second)
            out.append(w[1 + 2 * s] * second - w[2 + 2 * s] * first)
        return out

    def first_relax(self, target, source, low, high):
        def body(i):
            for p in range(self.phases):
                values = [source[i, k * self.phases + p] for k in range(SECTIONS)]
                for k, value in enumerate(self.weighted(i, p, values)):
                    target[i, k * self.phases + p] = value

        rows_loop(low, high, body, self.unroll)

    def gathered(self, iterate, source, i):
        count = self.phases
        centres = [[iterate[i, k * count + p] for p in range(count)] for k in range(SECTIONS)]
        sums = []
        for p in range(count):
            coeffs = self.coeffs(i, p)
            sums.append(
                [
                    source[i, k * count + p]
                    + self.inflow(
                        coeffs,
                        centres[k],
                        p,
                        iterate[i + 1, k * count + p],
                        iterate[i - 1, k * count + p],
                    )
                    for k in range(SECTIONS)
                ]
            )
        return centres, sums

    def relax(self, target, iterate, source, low, high):
        count = self.phases

        def body(i):
            centres, sums = self.gathered(iterate, source, i)
            for p in range(count):
                for k, value in enumerate(self.weighted(i, p, sums[p])):
                    target[i, k * count + p] = (1.0 - damping) * centres[k][p] + value

        rows_loop(low, high, body, self.unroll)

    def residual(self, iterate, source, i):
        centres, sums = self.gathered(iterate, source, i)
        result = []
        for p in range(self.phases):
            cap, total = self.cap[i, p], self.total[i, p]
            x = [centres[k][p] for k in range(SECTIONS)]
            out = [sums[p][0] - (SHIFTS[0] * cap + total) * x[0]]
            for s in range(2):
                direct = SHIFTS[s + 1] * cap + total
                cross = COUPLES[s] * cap
                a, b = 1 + 2 * s, 2 + 2 * s
                out.append(sums[p][a] - (direct * x[a] + cross * x[b]))
                out.append(sums[p][b] - (direct * x[b] - cross * x[a]))
            result.append(out)
        return result

    def restrict(self, target, iterate, source, low, high, shift=0):
        half = self.phases // 2

        def body(row):
            one = self.residual(iterate, source, 2 * row)
            two = self.residual(iterate, source, 2 * row + 1)
            for k in range(SECTIONS):
                for q in range(half):
                    target[row + shift, k * half + q] = (one[2 * q][k] + one[2 * q + 1][k]) + (
                        two[2 * q][k] + two[2 * q + 1][k]
                    )

        rows_loop(low, high, body, self.unroll // 2)

    def correct(self, target, iterate, coarse, low, high, shift=0):
        count, half = self.phases, self.phases // 2

        def body(i):
            row = lax.shift_right_logical(i, 1) + shift
            for k in range(SECTIONS):
                for q in range(half):
                    value = coarse[row, k * half + q]
                    for p in (2 * q, 2 * q + 1):
                        target[i, k * count + p] = iterate[i, k * count + p] + value

        rows_loop(low, high, body, self.unroll)


def coarsen(fine, coarse, rows):
    half = coarse.phases

    def body(row):
        for q in range(half):
            for ref_out, ref_in in ((coarse.cap, fine.cap),):
                ref_out[row, q] = (ref_in[2 * row, 2 * q] + ref_in[2 * row, 2 * q + 1]) + (
                    ref_in[2 * row + 1, 2 * q] + ref_in[2 * row + 1, 2 * q + 1]
                )
        for q in range(half + 1):
            coarse.gy[row, q] = fine.gy[2 * row, 2 * q] + fine.gy[2 * row + 1, 2 * q]

    rows_loop(0, rows, body, 4)

    def body_gx(row):
        for q in range(half):
            coarse.gx[row, q] = fine.gx[2 * row, 2 * q] + fine.gx[2 * row, 2 * q + 1]

    rows_loop(1, rows, body_gx, 4)


def sum_below(fine_below, coarse_below, phases, low, high):
    def body(row):
        for q in range(phases):
            coarse_below[row, q] = (
                fine_below[2 * row, 2 * q] + fine_below[2 * row, 2 * q + 1]
            ) + (fine_below[2 * row + 1, 2 * q] + fine_below[2 * row + 1, 2 * q + 1])

    rows_loop(low, high, body, 4)


def gather_kernel(*refs):
    own, left, right, work = refs[6:10]
    whole = refs[17]
    voltage, capacity, node_class, via, ball, load = refs[10:16]
    copies = [
        pltpu.make_async_copy(source, target, refs[16].at[n])
        for n, (source, target) in enumerate(zip(refs[:6], refs[10:16]))
    ]
    for copy in copies:
        copy.start()
    for copy in copies:
        copy.wait()
    classes = node_class[...]
    conduct = jnp.full(classes.shape, node_table[0], jnp.float32)
    for c in range(1, len(node_table)):
        conduct = jnp.where(classes == c, node_table[c], conduct)
    grounded = jnp.where(ball[...] == 1, ball_conductance, 0.0)
    upright = jnp.where(via[...] == 1, via_conductance, 0.0)
    for h in range(2):
        half = slice(h * 128, h * 128 + 128)
        work[0, h] = voltage[:, half]
        work[1, h] = capacity[:, half]
        work[2, h] = conduct[:, half]
        work[3, h, 0:8] = grounded[:, half]
        work[3, h, 8:64] = upright[:, half]
    for row in range(8):
        for a in range(4):
            at = (row * 4 + a) * 8
            for h in range(2):
                whole[at : at + 8, h * 128 : h * 128 + 128] = work[
                    a, h, pl.ds(row, 8, stride=8), :
                ]
    whole[256:264] = load[...].astype(jnp.float32)
    left[...] = whole[:, :64]
    right[...] = whole[:, 192:]
    column = lax.broadcasted_iota(jnp.int32, (256, 256), 0)
    slot = lax.broadcasted_iota(jnp.int32, (256, 256), 1)
    wanted = 4 * (slot % 64) + slot // 64
    result = selected(whole[...], jnp.where(column == wanted, 1.0, 0.0).astype(jnp.bfloat16))
    for n in range(33):
        for h in range(2):
            own[n, h] = result[8 * n : 8 * n + 8, 128 * h : 128 * h + 128]


def three_parts(value):
    high = value.astype(jnp.bfloat16)
    rest = value - high.astype(jnp.float32)
    middle = rest.astype(jnp.bfloat16)
    low = (rest - middle.astype(jnp.float32)).astype(jnp.bfloat16)
    return high, middle, low


def selected(value, chooser):
    high, middle, low = (
        jnp.dot(part, chooser, preferred_element_type=jnp.float32) for part in three_parts(value)
    )
    return high + (middle + low)


def rim_kernel(own, from_lower, from_upper, whole):
    column = lax.broadcasted_iota(jnp.int32, (64, LANES), 0)
    slot = lax.broadcasted_iota(jnp.int32, (64, LANES), 1)
    group, place = slot // 32, slot % 32
    below = (place >= 16) & (column == 4 * (place - 16) + (group + 1) % 4)
    above = (place < 16) & (column == 4 * place + (group + 2) % 4)
    result = selected(from_lower[...], jnp.where(below, 1.0, 0.0).astype(jnp.bfloat16))
    result = result + selected(
        from_upper[...], jnp.where(above, 1.0, 0.0).astype(jnp.bfloat16)
    )
    for n in range(33):
        whole[n, 2] = result[8 * n : 8 * n + 8]
        for h in range(2):
            whole[n, h] = own[n, h]


def edge_kernel(near_lower, near_upper, go_right, go_left):
    lane = lane_index()
    group = lane // 32
    late = lane % 32 >= 16

    def chosen(one, two, three, four):
        return jnp.where(
            group < 2, jnp.where(group == 0, one, two), jnp.where(group == 2, three, four)
        )

    def body(n):
        rights, lefts = [], []
        for block in (near_lower, near_upper):
            first, second = block[n, 0], block[n, 1]
            first_far, first_near = pltpu.roll(first, 64, 1), pltpu.roll(first, 32, 1)
            second_far = pltpu.roll(second, 96, 1)
            rights.append(chosen(first_near, second, second_far, first_far))
            lefts.append(chosen(second, second_far, first_far, first_near))
        go_right[n] = jnp.where(late, rights[0], pltpu.roll(rights[1], 112, 1))
        go_left[n] = jnp.where(late, pltpu.roll(lefts[1], 16, 1), lefts[0])

    rows_loop(0, 33, body, 11)


def prepare(place, mixed_table, state, f1, blocks, gx_rows, total_rows, relax_rows, sum_rows):
    (gx0, gy0, via0, below0, cap0, total0, weights0, f0, x0) = state[:9]
    below1, volt, conduct, surface, spare = state[9:14]
    fine = Level(4, gx0, gy0, via0, below0, cap0, total0, weights0)
    row_block, column_block = place[0], place[1]
    lane = lane_index()
    edge = ((lane == 0) & (column_block == 0)) | ((lane == 64) & (column_block == 3))
    joined = jnp.where(edge, 0.0, 2.0)
    top = layer_index() == LAYERS - 1

    def series(near, far):
        return 2.0 * near * far / (near + far)

    def set_gy(i):
        here = [conduct[i, p] for p in range(4)]
        before = from_left(here[3])
        first = joined * before * here[0] / (before + here[0])
        gy0[i, 0] = first
        for p in range(1, 4):
            gy0[i, p] = series(here[p - 1], here[p])

    def turn_gy(i):
        gy0[i, 4] = from_right(gy0[i, 0])

    for b, block, rim in blocks:

        def place_row(s, block=block, rim=rim, b=b):
            for a, ref in enumerate((volt, cap0, conduct, below0)):
                n = 4 * s + a
                phases = spread(block[n, 0], block[n, 1], rim(n))
                for p in range(4):
                    ref[8 * b + s, p] = phases[p]

        rows_loop(0, 8, place_row, 4)
        loads = spread(block[32, 0], block[32, 1], rim(32))
        for p in range(4):
            values = [jnp.zeros((8, LANES), jnp.float32) for _ in range(SECTIONS)]
            for t in range(LOADS):
                chosen = loads[p] == float(t)
                values = [
                    jnp.where(chosen, mixed_table[t, k], values[k]) for k in range(SECTIONS)
                ]
            for k in range(SECTIONS):
                surface[4 * k + p, 8 * b : 8 * b + 8] = values[k]
        rows_loop(8 * b, 8 * b + 8, set_gy, 8)
        rows_loop(8 * b, 8 * b + 8, turn_gy, 8)
        sum_below(below0, below1, 2, 4 * b, 4 * b + 4)

    def set_gx(i):
        row = 8 * row_block - 16 + i
        inside = jnp.where((row == 0) | (row == 256), 0.0, 1.0).astype(jnp.float32)
        for p in range(4):
            gx0[i, p] = inside * series(conduct[i - 1, p], conduct[i, p])

    def set_source(i):
        centre = [volt[i, p] for p in range(4)]
        for p in range(4):
            leak = total0[i, p] * centre[p] - fine.inflow(
                fine.coeffs(i, p), centre, p, volt[i + 1, p], volt[i - 1, p]
            )
            values = []
            for k in range(SECTIONS):
                drawn = jnp.broadcast_to(surface[4 * k + p, pl.ds(i, 1), :], (LAYERS, LANES))
                values.append(jnp.where(top, drawn, 0.0) - ROW_SUMS[k] * leak)
                f0[i, 4 * k + p] = values[k]
            for k, value in enumerate(fine.weighted(i, p, values)):
                spare[i, 4 * k + p] = value

    for low, high in gx_rows:
        rows_loop(low, high, set_gx, 4)
    for low, high in total_rows:
        rows_loop(low, high, fine.set_total)
        rows_loop(low, high, set_source)
    for low, high in relax_rows:
        fine.relax(x0, spare, f0, low, high)
    for low, high in sum_rows:
        fine.restrict(f1, x0, f0, low, high)


STATE = 14


def own_kernel(place, mixed_table, whole, *refs):
    prepare(
        place,
        mixed_table,
        refs,
        None,
        ((2, whole, lambda n: whole[n, 2]),),
        ((17, 24),),
        ((17, 23),),
        ((18, 22),),
        (),
    )


def near_kernel(place, mixed_table, near_lower, near_upper, edge_left, edge_right, *refs):
    refs = refs[STATE:]
    late = lane_index() % 32 >= 16

    def rim_lower(n):
        return jnp.where(late, edge_left[n], edge_right[n])

    def rim_upper(n):
        return jnp.where(
            late, pltpu.roll(edge_left[n], 16, 1), pltpu.roll(edge_right[n], 112, 1)
        )

    prepare(
        place,
        mixed_table,
        refs[:STATE],
        refs[STATE],
        ((1, near_lower, rim_lower), (3, near_upper, rim_upper)),
        ((9, 17), (24, 32)),
        ((9, 17), (23, 31)),
        ((10, 18), (22, 30)),
        ((6, 14),),
    )


def setup_kernel(place, mixed_table, far_lower, far_upper, *refs):
    refs = refs[STATE + 1 :]
    state, f1 = refs[:STATE], refs[STATE]
    gx1, gy1, via1, cap1, total1, weights1, x1 = refs[STATE + 1 : STATE + 8]
    gx2, gy2, below2, cap2, f2, go_up, go_down, spare1 = refs[STATE + 8 :]
    below1 = state[9]
    prepare(
        place,
        mixed_table,
        state,
        f1,
        ((0, far_lower, lambda n: far_lower[n, 2]), (4, far_upper, lambda n: far_upper[n, 2])),
        ((1, 9), (32, 40)),
        ((1, 9), (31, 39)),
        ((2, 10), (30, 38)),
        ((2, 6), (14, 18)),
    )
    fine = Level(4, *state[:7])
    middle = Level(2, gx1, gy1, via1, below1, cap1, total1, weights1)
    coarse = Level(1, gx2, gy2, None, below2, cap2, None, None)
    coarsen(fine, middle, EXT1)
    coarsen(middle, coarse, EXT2)
    sum_below(below1, below2, 1, 0, EXT2)
    rows_loop(1, EXT1 - 1, middle.set_total)
    middle.first_relax(spare1, f1, 2, 18)
    middle.relax(x1, spare1, f1, 3, 17)
    middle.restrict(f2, x1, f1, 2, 8)
    for target, first, outer in ((go_up, 2, 2), (go_down, 4, 6)):
        for j in range(4):
            for k in range(SECTIONS):
                target[5 * j + k] = f2[first + j, k]
        for j in range(2):
            target[20 + 3 * j] = gy2[outer + j, 0]
            target[21 + 3 * j] = below2[outer + j, 0]
            target[22 + 3 * j] = cap2[outer + j, 0]
        for j in range(3):
            target[26 + j] = gx2[outer + j, 0]


def middle_kernel(*refs):
    (gx0, gy0, via0, below0, cap0, total0, weights0, f0, x0) = refs[0:9]
    (gx1, gy1, via1, below1, cap1, total1, weights1, f1, x1) = refs[9:18]
    (gx2, gy2, below2, cap2, f2, from_lower, from_upper) = refs[18:25]
    (x0_out, f1_out, go_side, gxw, gyw, viaw, beloww, weightsw) = refs[25:33]
    (capw, totalw, fw, xa, xb, ya, yb, za, f1_own) = refs[33:42]
    fine = Level(4, gx0, gy0, via0, below0, cap0, total0, weights0)
    middle = Level(2, gx1, gy1, via1, below1, cap1, total1, weights1)
    coarse = Level(1, gxw, gyw, viaw, beloww, capw, totalw, weightsw)
    for j in range(4):
        for k in range(SECTIONS):
            fw[j, k] = from_lower[5 * j + k]
            fw[10 + j, k] = from_upper[5 * j + k]
    for j in range(2):
        for near, source in ((j, from_lower), (12 + j, from_upper)):
            gyw[near, 0] = source[20 + 3 * j]
            gyw[near, 1] = from_right(source[20 + 3 * j])
            beloww[near, 0] = source[21 + 3 * j]
            capw[near, 0] = source[22 + 3 * j]
    for j in range(3):
        gxw[j, 0] = from_lower[26 + j]
        gxw[12 + j, 0] = from_upper[26 + j]
    for j in range(6):
        for k in range(SECTIONS):
            fw[4 + j, k] = f2[2 + j, k]
    for j in range(10):
        gyw[2 + j, 0] = gy2[j, 0]
        gyw[2 + j, 1] = gy2[j, 1]
        beloww[2 + j, 0] = below2[j, 0]
        capw[2 + j, 0] = cap2[j, 0]
    for j in range(1, 10):
        gxw[2 + j, 0] = gx2[j, 0]
    rows_loop(0, WIDE2, coarse.set_total)
    coarse.first_relax(xa, fw, 0, 14)
    coarse.relax(xb, xa, fw, 1, 13)
    coarse.relax(xa, xb, fw, 2, 12)
    coarse.relax(xb, xa, fw, 3, 11)
    middle.correct(ya, x1, xb, 3, 17, 2)
    middle.relax(yb, ya, f1, 4, 16)
    middle.relax(ya, yb, f1, 5, 15)
    fine.correct(za, x0, ya, 10, 30)
    fine.relax(x0_out, za, f0, 11, 29)
    fine.relax(za, x0_out, f0, 12, 28)
    fine.relax(x0_out, za, f0, 13, 27)
    fine.relax(za, x0_out, f0, 14, 26)
    fine.restrict(f1_own, za, f0, 8, 12, -8)
    for j in range(4):
        for n in range(10):
            f1_out[10 * j + n] = f1_own[j, n]
    for j in range(10):
        packs = packed([f1_own[n // 10, n % 10] for n in range(4 * j, 4 * j + 4)])
        for t in range(3):
            go_side[3 * j + t] = packs[t]

    def keep(i):
        for n in range(20):
            x0_out[i, n] = za[i, n]

    rows_loop(14, 26, keep)


def lower_kernel(*refs):
    (gx1, gy1, via1, below1, cap1, total1, weights1) = refs[0:7]
    own, from_lower, from_upper = refs[7:10]
    f1, x1, f2_out = refs[10:13]
    (xa,) = refs[13:14]
    middle = Level(2, gx1, gy1, via1, below1, cap1, total1, weights1)
    for j in range(10):
        for first, source in ((4, from_lower), (12, from_upper)):
            values = unpacked([source[3 * j + t] for t in range(3)])
            for t in range(4):
                n = 4 * j + t
                f1[first + n // 10, n % 10] = values[t]
        for n in range(4 * j, 4 * j + 4):
            f1[8 + n // 10, n % 10] = own[n]
    middle.first_relax(xa, f1, 4, 16)
    middle.relax(x1, xa, f1, 5, 15)
    middle.restrict(f2_out, x1, f1, 3, 7, -3)


def finish_kernel(*refs):
    (gx0, gy0, via0, below0, weights0, f0, x0) = refs[0:7]
    (gx1, gy1, via1, below1, weights1, f1, x1) = refs[7:14]
    (gxw, gyw, viaw, beloww, weightsw, own, from_lower, from_upper, voltage) = refs[14:23]
    sections, next_voltage = refs[23:25]
    fw, xa, xb, ya, yb, za, zb, mixed, turn = refs[25:34]
    fine = Level(4, gx0, gy0, via0, below0, None, None, weights0)
    middle = Level(2, gx1, gy1, via1, below1, None, None, weights1)
    coarse = Level(1, gxw, gyw, viaw, beloww, None, None, weightsw)
    for j in range(4):
        for k in range(SECTIONS):
            fw[1 + j, k] = from_lower[j, k]
            fw[5 + j, k] = own[j, k]
            fw[9 + j, k] = from_upper[j, k]
    coarse.first_relax(xa, fw, 1, 13)
    coarse.relax(xb, xa, fw, 2, 12)
    coarse.relax(xa, xb, fw, 3, 11)
    coarse.relax(xb, xa, fw, 4, 10)
    middle.correct(ya, x1, xb, 5, 15, 2)
    middle.relax(yb, ya, f1, 6, 14)
    middle.relax(ya, yb, f1, 7, 13)
    fine.correct(za, x0, ya, 14, 26)
    fine.relax(zb, za, f0, 15, 25)
    fine.relax(za, zb, f0, 16, 24)

    def mix(row):
        for p in range(4):
            values = [za[16 + row, 4 * k + p] for k in range(SECTIONS)]
            for j in range(SECTIONS):
                total = TRANSFORM[j][0] * values[0]
                for k in range(1, SECTIONS):
                    total = total + TRANSFORM[j][k] * values[k]
                mixed[p, 8 * j + row] = total

    rows_loop(0, 8, mix)
    result = None
    for p in range(4):
        lane = lax.broadcasted_iota(jnp.int32, (LANES, 256), 0)
        column = lax.broadcasted_iota(jnp.int32, (LANES, 256), 1)
        chooser = jnp.where((lane < 64) & (column == 4 * lane + p), 1.0, 0.0).astype(jnp.bfloat16)
        part = selected(mixed[p].reshape(320, LANES), chooser)
        result = part if result is None else result + part
    for j in range(SECTIONS):
        for row in range(8):
            at = (8 * j + row) * 8
            for h in range(2):
                turn[j, h, pl.ds(row, 8, stride=8), :] = result[
                    at : at + 8, h * 128 : h * 128 + 128
                ]
        for h in range(2):
            sections[j, :, h * 128 : h * 128 + 128] = turn[j, h]
    next_voltage[...] = voltage[...] + sections[SECTIONS - 1]


VMEM = pltpu.MemorySpace.VMEM
SMEM = pltpu.MemorySpace.SMEM


def vregs(*shape):
    return pltpu.VMEM(shape + (LAYERS, LANES), jnp.float32)


def scratch(*shape):
    return pltpu.VMEM(shape + (LAYERS, LANES), jnp.float32)


def call(kernel, inputs, outs, scratches=(), scalars=0, outside=False, aliases=()):
    space = pltpu.MemorySpace.HBM if outside else VMEM
    inputs = [
        value if n < scalars else pltpu.with_memory_space_constraint(value, space)
        for n, value in enumerate(inputs)
    ]
    return pl.pallas_call(
        kernel,
        out_shape=outs,
        in_specs=[pl.BlockSpec(memory_space=SMEM)] * scalars
        + [pl.BlockSpec(memory_space=space)] * (len(inputs) - scalars),
        out_specs=[pl.BlockSpec(memory_space=VMEM)] * len(outs),
        scratch_shapes=list(scratches),
        input_output_aliases=dict(aliases),
        compiler_params=pltpu.CompilerParams(vmem_limit_bytes=12 * 2**20),
    )(*inputs)


def turned(value, axis, count, shift):
    return lax.ppermute(value, axis, [(i, (i + shift) % count) for i in range(count)])


ROWS = ("section", "gx")


def local(voltage, capacity, node_class, via_sites, ball_sites, load_type, load_table):
    rows = lax.axis_size("section") * lax.axis_size("gx")
    columns = lax.axis_size("gy")
    volts = voltage.reshape(64, 256)
    own, left, right = call(
        gather_kernel,
        (
            volts,
            capacity.reshape(64, 256),
            node_class.reshape(64, 256),
            via_sites.reshape(56, 256),
            ball_sites,
            load_type,
        ),
        [
            vregs(33, 2),
            pltpu.VMEM((264, 64), jnp.float32),
            pltpu.VMEM((264, 64), jnp.float32),
        ],
        [
            pltpu.VMEM((4, 2, 64, LANES), jnp.float32),
            pltpu.VMEM((64, 256), jnp.float32),
            pltpu.VMEM((64, 256), jnp.float32),
            pltpu.VMEM((64, 256), jnp.int32),
            pltpu.VMEM((56, 256), jnp.int32),
            pltpu.VMEM((8, 256), jnp.int32),
            pltpu.VMEM((8, 256), jnp.int32),
            pltpu.SemaphoreType.DMA((6,)),
            pltpu.VMEM((264, 256), jnp.float32),
        ],
        outside=True,
    )
    near_lower, near_upper = (turned(own, ROWS, rows, s) for s in (1, -1))
    from_lower = turned(right, "gy", columns, 1)
    from_upper = turned(left, "gy", columns, -1)
    mixed_table = jnp.einsum(
        "tk,jk->tj", load_table, jnp.asarray(INVERSE, jnp.float32), precision=lax.Precision.HIGHEST
    )
    place = jnp.stack(
        [
            lax.axis_index("section") * lax.axis_size("gx") + lax.axis_index("gx"),
            lax.axis_index("gy"),
        ]
    ).astype(jnp.int32)
    (whole,) = call(rim_kernel, (own, from_lower, from_upper), [vregs(33, 3)])
    far_lower, far_upper = (turned(whole, ROWS, rows, s) for s in (2, -2))
    go_right, go_left = call(edge_kernel, (near_lower, near_upper), [vregs(33), vregs(33)])
    edge_left = turned(go_right, "gy", columns, 1)
    edge_right = turned(go_left, "gy", columns, -1)
    state_shapes = [
        vregs(EXT0, 4),
        vregs(EXT0, 5),
        vregs(EXT0, 4),
        vregs(EXT0, 4),
        vregs(EXT0, 4),
        vregs(EXT0, 4),
        vregs(EXT0, 20),
        vregs(EXT0, 20),
        vregs(EXT0, 20),
        vregs(EXT1, 2),
        vregs(EXT0, 4),
        vregs(EXT0, 4),
        pltpu.VMEM((20, EXT0, LANES), jnp.float32),
        vregs(EXT0, 20),
    ]
    state = call(own_kernel, (place, mixed_table, whole), state_shapes, (), 2)
    state = call(
        near_kernel,
        (place, mixed_table, near_lower, near_upper, edge_left, edge_right, *state),
        [*state_shapes, vregs(EXT1, 10)],
        (),
        2,
        aliases=[(6 + n, n) for n in range(STATE)],
    )
    state = call(
        setup_kernel,
        (place, mixed_table, far_lower, far_upper, *state),
        [
            *state_shapes,
            vregs(EXT1, 10),
            vregs(EXT1, 2),
            vregs(EXT1, 3),
            vregs(EXT1, 2),
            vregs(EXT1, 2),
            vregs(EXT1, 2),
            vregs(EXT1, 10),
            vregs(EXT1, 10),
            vregs(EXT2, 1),
            vregs(EXT2, 2),
            vregs(EXT2, 1),
            vregs(EXT2, 1),
            vregs(EXT2, 5),
            vregs(29),
            vregs(29),
        ],
        [scratch(EXT1, 10)],
        2,
        aliases=[(4 + n, n) for n in range(STATE + 1)],
    )
    fine, below1, f1 = state[:9], state[9], state[STATE]
    gx1, gy1, via1, cap1, total1, weights1, x1 = state[STATE + 1 : STATE + 8]
    middle = (gx1, gy1, via1, below1, cap1, total1, weights1, f1, x1)
    coarse = state[STATE + 8 : STATE + 13]
    go_up, go_down = state[STATE + 13 :]
    lower = turned(go_up, ROWS, rows, 2)
    upper = turned(go_down, ROWS, rows, -2)
    x0, f1_own, go_side, gxw, gyw, viaw, beloww, weightsw = call(
        middle_kernel,
        (*fine, *middle, *coarse, lower, upper),
        [
            vregs(EXT0, 20),
            vregs(40),
            vregs(30),
            vregs(WIDE2 + 1, 1),
            vregs(WIDE2, 2),
            vregs(WIDE2, 1),
            vregs(WIDE2, 1),
            vregs(WIDE2, 5),
        ],
        [
            scratch(WIDE2, 1),
            scratch(WIDE2, 1),
            scratch(WIDE2, 5),
            scratch(WIDE2, 5),
            scratch(WIDE2, 5),
            scratch(EXT1, 10),
            scratch(EXT1, 10),
            scratch(EXT0, 20),
            scratch(4, 10),
        ],
    )
    lower = turned(go_side, ROWS, rows, 1)
    upper = turned(go_side, ROWS, rows, -1)
    f1, x1, f2_own = call(
        lower_kernel,
        (*middle[:7], f1_own, lower, upper),
        [vregs(EXT1, 10), vregs(EXT1, 10), vregs(4, 5)],
        [scratch(EXT1, 10)],
    )
    lower = turned(f2_own, ROWS, rows, 2)
    upper = turned(f2_own, ROWS, rows, -2)
    sections, next_voltage = call(
        finish_kernel,
        (
            *fine[:4],
            *fine[6:8],
            x0,
            *middle[:4],
            middle[6],
            f1,
            x1,
            gxw,
            gyw,
            viaw,
            beloww,
            weightsw,
            f2_own,
            lower,
            upper,
            volts,
        ),
        [
            jax.ShapeDtypeStruct((SECTIONS, 64, 256), jnp.float32),
            jax.ShapeDtypeStruct((64, 256), jnp.float32),
        ],
        [
            scratch(WIDE2, 5),
            scratch(WIDE2, 5),
            scratch(WIDE2, 5),
            scratch(EXT1, 10),
            scratch(EXT1, 10),
            scratch(EXT0, 20),
            scratch(EXT0, 20),
            scratch(4, 40),
            pltpu.VMEM((SECTIONS, 2, 64, LANES), jnp.float32),
        ],
    )
    return sections.reshape((SECTIONS,) + voltage.shape), next_voltage.reshape(voltage.shape)


def solution(mesh):
    return jax.shard_map(
        local,
        mesh=mesh,
        in_specs=(
            P(None, ("section", "gx"), "gy"),
            P(None, ("section", "gx"), "gy"),
            P(None, ("section", "gx"), "gy"),
            P(None, ("section", "gx"), "gy"),
            P(("section", "gx"), "gy"),
            P(("section", "gx"), "gy"),
            P(),
        ),
        out_specs=(P(None, None, ("section", "gx"), "gy"), P(None, ("section", "gx"), "gy")),
        check_vma=False,
    )
```

```python
import jax
import jax.numpy as jnp
from jax import lax
from jax.experimental import pallas as pl
from jax.experimental.pallas import tpu as pltpu
from jax.sharding import PartitionSpec as P

SECTIONS = 5
LOADS = 16
LAYERS = 8
LANES = 128
EXT0 = 40
EXT1 = 20
EXT2 = 10
WIDE2 = 14

node_table = (0.35, 0.55, 0.8, 1.1, 1.5, 2.0, 2.7, 3.6)
via_conductance = 2.5
ball_conductance = 4.0
damping = 0.8
slab_partner = (0, 2, 1, 4, 3)


def pair_times(first, second):
    return (
        first[0] * second[0] - first[1] * second[1],
        first[0] * second[1] + first[1] * second[0],
    )


def pair_over(first, second):
    divisor = second[0] * second[0] + second[1] * second[1]
    return (
        (first[0] * second[0] + first[1] * second[1]) / divisor,
        (first[1] * second[0] - first[0] * second[1]) / divisor,
    )


def pair_minus(first, second):
    return (first[0] - second[0], first[1] - second[1])


def poly_value(coeffs, point):
    total = (0.0, 0.0)
    for c in reversed(coeffs):
        total = pair_times(total, point)
        total = (total[0] + c, total[1])
    return total


def poly_product(first, second):
    result = [0.0] * (len(first) + len(second) - 1)
    for i in range(len(first)):
        for j in range(len(second)):
            result[i + j] = result[i + j] + first[i] * second[j]
    return result


def poly_roots(coeffs):
    leading = coeffs[-1]
    scaled = [c / leading for c in coeffs]
    degree = len(coeffs) - 1
    guesses = []
    current = (1.0, 0.0)
    for k in range(degree):
        guesses.append(current)
        current = pair_times(current, (0.4, 0.9))
    for repeat_index in range(800):
        for k in range(degree):
            divisor = (1.0, 0.0)
            for j in range(degree):
                if j != k:
                    divisor = pair_times(divisor, pair_minus(guesses[k], guesses[j]))
            guesses[k] = pair_minus(guesses[k], pair_over(poly_value(scaled, guesses[k]), divisor))
    return guesses


def matrix_product(first, second):
    return [
        [
            sum((first[i][k] * second[k][j] for k in range(len(second))))
            for j in range(len(second[0]))
        ]
        for i in range(len(first))
    ]


def matrix_inverse(matrix):
    order = len(matrix)
    work = [list(matrix[i]) + [1.0 if i == j else 0.0 for j in range(order)] for i in range(order)]
    for column in range(order):
        pivot = column
        for i in range(column + 1, order):
            if abs(work[i][column]) > abs(work[pivot][column]):
                pivot = i
        work[column], work[pivot] = (work[pivot], work[column])
        factor = work[column][column]
        work[column] = [entry / factor for entry in work[column]]
        for i in range(order):
            if i != column:
                scale_row = work[i][column]
                work[i] = [work[i][j] - scale_row * work[column][j] for j in range(2 * order)]
    return [row[order:] for row in work]


def eigen_vector(matrix, value):
    order = len(matrix)
    size_inner = order - 1
    system = []
    for i in range(size_inner):
        row = []
        for j in range(order):
            entry = (matrix[i][j], 0.0)
            if i == j:
                entry = pair_minus(entry, value)
            row.append(entry)
        row[order - 1] = (-row[order - 1][0], -row[order - 1][1])
        system.append(row)
    for column in range(size_inner):
        pivot = column
        for i in range(column + 1, size_inner):
            left_size = system[i][column][0] ** 2 + system[i][column][1] ** 2
            right_size = system[pivot][column][0] ** 2 + system[pivot][column][1] ** 2
            if left_size > right_size:
                pivot = i
        system[column], system[pivot] = (system[pivot], system[column])
        for i in range(size_inner):
            if i != column:
                factor = pair_over(system[i][column], system[column][column])
                system[i] = [
                    pair_minus(system[i][j], pair_times(factor, system[column][j]))
                    for j in range(order)
                ]
    vector = [pair_over(system[i][order - 1], system[i][i]) for i in range(size_inner)]
    vector.append((1.0, 0.0))
    return vector


def radau_tables():
    section_count = 5
    generator = [1.0]
    for k in range(section_count - 1):
        generator = poly_product(generator, [0.0, 1.0])
    for k in range(section_count):
        generator = poly_product(generator, [-1.0, 1.0])
    for k in range(section_count - 1):
        generator = [j * generator[j] for j in range(1, len(generator))]
    abscissae = sorted((root[0] for root in poly_roots(generator)))
    vander = [[abscissae[i] ** j for j in range(section_count)] for i in range(section_count)]
    integrals = [
        [abscissae[i] ** (j + 1) / (j + 1) for j in range(section_count)]
        for i in range(section_count)
    ]
    butcher = matrix_product(integrals, matrix_inverse(vander))
    inverse = matrix_inverse(butcher)
    coeffs = [0.0] * (section_count + 1)
    coeffs[section_count] = 1.0
    current = [[0.0] * section_count for _ in range(section_count)]
    for k in range(1, section_count + 1):
        current = matrix_product(inverse, current)
        for i in range(section_count):
            current[i][i] = current[i][i] + coeffs[section_count - k + 1]
        applied = matrix_product(inverse, current)
        coeffs[section_count - k] = -sum((applied[i][i] for i in range(section_count))) / k
    eigen_values = poly_roots(coeffs)
    real_pick = 0
    for k in range(section_count):
        if abs(eigen_values[k][1]) < abs(eigen_values[real_pick][1]):
            real_pick = k
    upper_half = [k for k in range(section_count) if eigen_values[k][1] > 1e-09]
    upper_half = sorted(upper_half, key=lambda k: -eigen_values[k][0])
    columns = [[entry[0] for entry in eigen_vector(inverse, (eigen_values[real_pick][0], 0.0))]]
    for k in upper_half:
        vector = eigen_vector(inverse, eigen_values[k])
        columns.append([entry[0] for entry in vector])
        columns.append([entry[1] for entry in vector])
    transform = [[columns[j][i] for j in range(section_count)] for i in range(section_count)]
    inverse_transform = matrix_inverse(transform)
    blocks = matrix_product(matrix_product(inverse_transform, inverse), transform)
    diagonal = [blocks[k][k] for k in range(section_count)]
    coupling = [
        blocks[k][slab_partner[k]] if slab_partner[k] != k else 0.0 for k in range(section_count)
    ]
    return (transform, inverse_transform, diagonal, coupling)


TRANSFORM, INVERSE, DIAGONAL, COUPLING = radau_tables()
SHIFTS = (
    DIAGONAL[0],
    0.5 * (DIAGONAL[1] + DIAGONAL[2]),
    0.5 * (DIAGONAL[3] + DIAGONAL[4]),
)
COUPLES = (0.5 * (COUPLING[1] - COUPLING[2]), 0.5 * (COUPLING[3] - COUPLING[4]))
ROW_SUMS = tuple(sum(row) for row in INVERSE)


def from_right(value):
    return pltpu.roll(value, LANES - 1, 1)


def from_left(value):
    return pltpu.roll(value, 1, 1)


def from_above(value):
    return pltpu.roll(value, LAYERS - 1, 0)


def from_below(value):
    return pltpu.roll(value, 1, 0)


def lane_index():
    return lax.broadcasted_iota(jnp.int32, (LAYERS, LANES), 1)


def layer_index():
    return lax.broadcasted_iota(jnp.int32, (LAYERS, LANES), 0)


def spread(first, second, rim):
    own = lane_index() < 64
    inner = (first, pltpu.roll(first, 64, 1), second, pltpu.roll(second, 64, 1))
    outer = (rim, pltpu.roll(rim, 96, 1), pltpu.roll(rim, 64, 1), pltpu.roll(rim, 32, 1))
    return [jnp.where(own, near, far) for near, far in zip(inner, outer)]


def packed(values):
    lane = lane_index()
    dead = (lane >= 80) & (lane < 112)
    one, two, three, last = values
    tail = jnp.where(lane < 96, pltpu.roll(last, 96, 1), pltpu.roll(last, 32, 1))
    return [
        jnp.where(dead, pltpu.roll(last, 80, 1), one),
        jnp.where(dead, pltpu.roll(last, 48, 1), two),
        jnp.where(dead, tail, three),
    ]


def unpacked(packs):
    lane = lane_index()
    one, two, three = packs
    last = jnp.where(
        lane < 64,
        jnp.where(lane < 32, pltpu.roll(one, 48, 1), pltpu.roll(two, 80, 1)),
        jnp.where(lane < 96, pltpu.roll(three, 96, 1), pltpu.roll(three, 32, 1)),
    )
    return [one, two, three, last]


def rows_loop(low, high, body, unroll=2):
    steps = (high - low) // unroll

    def step(n, carry):
        for j in range(unroll):
            body(low + n * unroll + j)
        return carry

    if steps > 1:
        lax.fori_loop(0, steps, step, 0)
    elif steps == 1:
        step(0, 0)
    for i in range(low + steps * unroll, high):
        body(i)


class Sides:
    def __init__(self, place, distance, first, second):
        block = jnp.full((LAYERS, LANES), place[0], jnp.int32)
        self.odd = (block & distance) != 0
        self.first, self.second = first, second

    def lower(self, *at):
        return jnp.where(self.odd, self.first[at], self.second[at])

    def upper(self, *at):
        return jnp.where(self.odd, self.second[at], self.first[at])


class Level:
    def __init__(self, phases, gx, gy, via, below, cap, total, weights):
        self.phases = phases
        self.unroll = 8 // phases
        self.gx, self.gy = gx, gy
        self.via, self.below = via, below
        self.cap, self.total, self.weights = cap, total, weights

    def sides(self, centre, p):
        right = centre[p + 1] if p < self.phases - 1 else from_right(centre[0])
        left = centre[p - 1] if p > 0 else from_left(centre[self.phases - 1])
        return right, left

    def inflow(self, coeffs, centre, p, upper, lower):
        gx_lower, gx_upper, gy_left, gy_right, via, below = coeffs
        right, left = self.sides(centre, p)
        here = centre[p]
        return (
            (gx_upper * upper + gx_lower * lower)
            + (gy_right * right + gy_left * left)
            + (via * from_above(here) + below * from_below(here))
        )

    def coeffs(self, i, p):
        return (
            self.gx[i, p],
            self.gx[i + 1, p],
            self.gy[i, p],
            self.gy[i, p + 1],
            self.via[i, p],
            self.below[i, p],
        )

    def set_total(self, i):
        bottom = layer_index() == 0
        for p in range(self.phases):
            grounded = self.below[i, p]
            below = jnp.where(bottom, 0.0, grounded)
            via = from_above(below)
            total = (
                (self.gx[i, p] + self.gx[i + 1, p])
                + (self.gy[i, p] + self.gy[i, p + 1])
                + (via + grounded)
            )
            self.below[i, p] = below
            self.via[i, p] = via
            self.total[i, p] = total
            cap = self.cap[i, p]
            self.weights[i, p * 5] = damping / (SHIFTS[0] * cap + total)
            for s in range(2):
                direct = SHIFTS[s + 1] * cap + total
                cross = COUPLES[s] * cap
                scale = damping / (direct * direct + cross * cross)
                self.weights[i, p * 5 + 1 + 2 * s] = direct * scale
                self.weights[i, p * 5 + 2 + 2 * s] = -(cross * scale)

    def weighted(self, i, p, values):
        w = [self.weights[i, p * 5 + m] for m in range(5)]
        out = [w[0] * values[0]]
        for s in range(2):
            first, second = values[1 + 2 * s], values[2 + 2 * s]
            out.append(w[1 + 2 * s] * first + w[2 + 2 * s] * second)
            out.append(w[1 + 2 * s] * second - w[2 + 2 * s] * first)
        return out

    def first_relax(self, target, source, low, high):
        def body(i):
            for p in range(self.phases):
                values = [source[i, k * self.phases + p] for k in range(SECTIONS)]
                for k, value in enumerate(self.weighted(i, p, values)):
                    target[i, k * self.phases + p] = value

        rows_loop(low, high, body, self.unroll)

    def gathered(self, iterate, source, i):
        count = self.phases
        centres = [[iterate[i, k * count + p] for p in range(count)] for k in range(SECTIONS)]
        sums = []
        for p in range(count):
            coeffs = self.coeffs(i, p)
            sums.append(
                [
                    source[i, k * count + p]
                    + self.inflow(
                        coeffs,
                        centres[k],
                        p,
                        iterate[i + 1, k * count + p],
                        iterate[i - 1, k * count + p],
                    )
                    for k in range(SECTIONS)
                ]
            )
        return centres, sums

    def relax(self, target, iterate, source, low, high):
        count = self.phases

        def body(i):
            centres, sums = self.gathered(iterate, source, i)
            for p in range(count):
                for k, value in enumerate(self.weighted(i, p, sums[p])):
                    target[i, k * count + p] = (1.0 - damping) * centres[k][p] + value

        rows_loop(low, high, body, self.unroll)

    def residual(self, iterate, source, i):
        centres, sums = self.gathered(iterate, source, i)
        result = []
        for p in range(self.phases):
            cap, total = self.cap[i, p], self.total[i, p]
            x = [centres[k][p] for k in range(SECTIONS)]
            out = [sums[p][0] - (SHIFTS[0] * cap + total) * x[0]]
            for s in range(2):
                direct = SHIFTS[s + 1] * cap + total
                cross = COUPLES[s] * cap
                a, b = 1 + 2 * s, 2 + 2 * s
                out.append(sums[p][a] - (direct * x[a] + cross * x[b]))
                out.append(sums[p][b] - (direct * x[b] - cross * x[a]))
            result.append(out)
        return result

    def restrict(self, target, iterate, source, low, high, shift=0):
        half = self.phases // 2

        def body(row):
            one = self.residual(iterate, source, 2 * row)
            two = self.residual(iterate, source, 2 * row + 1)
            for k in range(SECTIONS):
                for q in range(half):
                    target[row + shift, k * half + q] = (one[2 * q][k] + one[2 * q + 1][k]) + (
                        two[2 * q][k] + two[2 * q + 1][k]
                    )

        rows_loop(low, high, body, self.unroll // 2)

    def correct(self, target, iterate, coarse, low, high, shift=0):
        count, half = self.phases, self.phases // 2

        def body(i):
            row = lax.shift_right_logical(i, 1) + shift
            for k in range(SECTIONS):
                for q in range(half):
                    value = coarse[row, k * half + q]
                    for p in (2 * q, 2 * q + 1):
                        target[i, k * count + p] = iterate[i, k * count + p] + value

        rows_loop(low, high, body, self.unroll)


def coarsen(fine, coarse, rows):
    half = coarse.phases

    def body(row):
        for q in range(half):
            for ref_out, ref_in in ((coarse.cap, fine.cap),):
                ref_out[row, q] = (ref_in[2 * row, 2 * q] + ref_in[2 * row, 2 * q + 1]) + (
                    ref_in[2 * row + 1, 2 * q] + ref_in[2 * row + 1, 2 * q + 1]
                )
        for q in range(half + 1):
            coarse.gy[row, q] = fine.gy[2 * row, 2 * q] + fine.gy[2 * row + 1, 2 * q]

    rows_loop(0, rows, body, 4)

    def body_gx(row):
        for q in range(half):
            coarse.gx[row, q] = fine.gx[2 * row, 2 * q] + fine.gx[2 * row, 2 * q + 1]

    rows_loop(1, rows, body_gx, 4)


def sum_below(fine_below, coarse_below, phases, low, high):
    def body(row):
        for q in range(phases):
            coarse_below[row, q] = (
                fine_below[2 * row, 2 * q] + fine_below[2 * row, 2 * q + 1]
            ) + (fine_below[2 * row + 1, 2 * q] + fine_below[2 * row + 1, 2 * q + 1])

    rows_loop(low, high, body, 4)


def gather_kernel(*refs):
    own, left, right, work = refs[6:10]
    whole = refs[17]
    voltage, capacity, node_class, via, ball, load = refs[10:16]
    copies = [
        pltpu.make_async_copy(source, target, refs[16].at[n])
        for n, (source, target) in enumerate(zip(refs[:6], refs[10:16]))
    ]
    for copy in copies:
        copy.start()
    for copy in copies:
        copy.wait()
    classes = node_class[...]
    conduct = jnp.full(classes.shape, node_table[0], jnp.float32)
    for c in range(1, len(node_table)):
        conduct = jnp.where(classes == c, node_table[c], conduct)
    grounded = jnp.where(ball[...] == 1, ball_conductance, 0.0)
    upright = jnp.where(via[...] == 1, via_conductance, 0.0)
    for h in range(2):
        half = slice(h * 128, h * 128 + 128)
        work[0, h] = voltage[:, half]
        work[1, h] = capacity[:, half]
        work[2, h] = conduct[:, half]
        work[3, h, 0:8] = grounded[:, half]
        work[3, h, 8:64] = upright[:, half]
    for row in range(8):
        for a in range(4):
            at = (row * 4 + a) * 8
            for h in range(2):
                whole[at : at + 8, h * 128 : h * 128 + 128] = work[
                    a, h, pl.ds(row, 8, stride=8), :
                ]
    whole[256:264] = load[...].astype(jnp.float32)
    left[...] = whole[:, :64]
    right[...] = whole[:, 192:]
    column = lax.broadcasted_iota(jnp.int32, (256, 256), 0)
    slot = lax.broadcasted_iota(jnp.int32, (256, 256), 1)
    wanted = 4 * (slot % 64) + slot // 64
    result = selected(whole[...], jnp.where(column == wanted, 1.0, 0.0).astype(jnp.bfloat16))
    for n in range(33):
        for h in range(2):
            own[n, h] = result[8 * n : 8 * n + 8, 128 * h : 128 * h + 128]


def three_parts(value):
    high = value.astype(jnp.bfloat16)
    rest = value - high.astype(jnp.float32)
    middle = rest.astype(jnp.bfloat16)
    low = (rest - middle.astype(jnp.float32)).astype(jnp.bfloat16)
    return high, middle, low


def selected(value, chooser):
    high, middle, low = (
        jnp.dot(part, chooser, preferred_element_type=jnp.float32) for part in three_parts(value)
    )
    return high + (middle + low)


def rim_kernel(own, from_lower, from_upper, whole):
    column = lax.broadcasted_iota(jnp.int32, (64, LANES), 0)
    slot = lax.broadcasted_iota(jnp.int32, (64, LANES), 1)
    group, place = slot // 32, slot % 32
    below = (place >= 16) & (column == 4 * (place - 16) + (group + 1) % 4)
    above = (place < 16) & (column == 4 * place + (group + 2) % 4)
    result = selected(from_lower[...], jnp.where(below, 1.0, 0.0).astype(jnp.bfloat16))
    result = result + selected(
        from_upper[...], jnp.where(above, 1.0, 0.0).astype(jnp.bfloat16)
    )
    for n in range(33):
        whole[n, 2] = result[8 * n : 8 * n + 8]
        for h in range(2):
            whole[n, h] = own[n, h]


def edge_kernel(place, near0, near1, go_right, go_left):
    lane = lane_index()
    group = lane // 32
    late = lane % 32 >= 16
    near = Sides(place, 1, near0, near1)

    def chosen(one, two, three, four):
        return jnp.where(
            group < 2, jnp.where(group == 0, one, two), jnp.where(group == 2, three, four)
        )

    def body(n):
        rights, lefts = [], []
        for block in (near.lower, near.upper):
            first, second = block(n, 0), block(n, 1)
            first_far, first_near = pltpu.roll(first, 64, 1), pltpu.roll(first, 32, 1)
            second_far = pltpu.roll(second, 96, 1)
            rights.append(chosen(first_near, second, second_far, first_far))
            lefts.append(chosen(second, second_far, first_far, first_near))
        go_right[n] = jnp.where(late, rights[0], pltpu.roll(rights[1], 112, 1))
        go_left[n] = jnp.where(late, pltpu.roll(lefts[1], 16, 1), lefts[0])

    rows_loop(0, 33, body, 11)


def prepare(place, mixed_table, state, f1, blocks, gx_rows, total_rows, relax_rows, sum_rows):
    (gx0, gy0, via0, below0, cap0, total0, weights0, f0, x0) = state[:9]
    below1, volt, conduct, surface, spare = state[9:14]
    fine = Level(4, gx0, gy0, via0, below0, cap0, total0, weights0)
    row_block, column_block = place[0], place[1]
    lane = lane_index()
    edge = ((lane == 0) & (column_block == 0)) | ((lane == 64) & (column_block == 3))
    joined = jnp.where(edge, 0.0, 2.0)
    top = layer_index() == LAYERS - 1

    def series(near, far):
        return 2.0 * near * far / (near + far)

    def set_gy(i):
        here = [conduct[i, p] for p in range(4)]
        before = from_left(here[3])
        first = joined * before * here[0] / (before + here[0])
        gy0[i, 0] = first
        for p in range(1, 4):
            gy0[i, p] = series(here[p - 1], here[p])

    def turn_gy(i):
        gy0[i, 4] = from_right(gy0[i, 0])

    for b, block, rim in blocks:

        def place_row(s, block=block, rim=rim, b=b):
            for a, ref in enumerate((volt, cap0, conduct, below0)):
                n = 4 * s + a
                phases = spread(block(n, 0), block(n, 1), rim(n))
                for p in range(4):
                    ref[8 * b + s, p] = phases[p]

        rows_loop(0, 8, place_row, 4)
        loads = spread(block(32, 0), block(32, 1), rim(32))
        for p in range(4):
            values = [jnp.zeros((8, LANES), jnp.float32) for _ in range(SECTIONS)]
            for t in range(LOADS):
                chosen = loads[p] == float(t)
                values = [
                    jnp.where(chosen, mixed_table[t, k], values[k]) for k in range(SECTIONS)
                ]
            for k in range(SECTIONS):
                surface[4 * k + p, 8 * b : 8 * b + 8] = values[k]
        rows_loop(8 * b, 8 * b + 8, set_gy, 8)
        rows_loop(8 * b, 8 * b + 8, turn_gy, 8)
        sum_below(below0, below1, 2, 4 * b, 4 * b + 4)

    def set_gx(i):
        row = 8 * row_block - 16 + i
        inside = jnp.where((row == 0) | (row == 256), 0.0, 1.0).astype(jnp.float32)
        for p in range(4):
            gx0[i, p] = inside * series(conduct[i - 1, p], conduct[i, p])

    def set_source(i):
        centre = [volt[i, p] for p in range(4)]
        for p in range(4):
            leak = total0[i, p] * centre[p] - fine.inflow(
                fine.coeffs(i, p), centre, p, volt[i + 1, p], volt[i - 1, p]
            )
            values = []
            for k in range(SECTIONS):
                drawn = jnp.broadcast_to(surface[4 * k + p, pl.ds(i, 1), :], (LAYERS, LANES))
                values.append(jnp.where(top, drawn, 0.0) - ROW_SUMS[k] * leak)
                f0[i, 4 * k + p] = values[k]
            for k, value in enumerate(fine.weighted(i, p, values)):
                spare[i, 4 * k + p] = value

    for low, high in gx_rows:
        rows_loop(low, high, set_gx, 4)
    for low, high in total_rows:
        rows_loop(low, high, fine.set_total)
        rows_loop(low, high, set_source)
    for low, high in relax_rows:
        fine.relax(x0, spare, f0, low, high)
    for low, high in sum_rows:
        fine.restrict(f1, x0, f0, low, high)


STATE = 14


def own_kernel(place, mixed_table, whole, *refs):
    prepare(
        place,
        mixed_table,
        refs,
        None,
        ((2, lambda n, h: whole[n, h], lambda n: whole[n, 2]),),
        ((17, 24),),
        ((17, 23),),
        ((18, 22),),
        (),
    )


def near_kernel(place, mixed_table, near0, near1, edge_left, edge_right, *refs):
    refs = refs[STATE:]
    late = lane_index() % 32 >= 16
    near = Sides(place, 1, near0, near1)

    def rim_lower(n):
        return jnp.where(late, edge_left[n], edge_right[n])

    def rim_upper(n):
        return jnp.where(
            late, pltpu.roll(edge_left[n], 16, 1), pltpu.roll(edge_right[n], 112, 1)
        )

    prepare(
        place,
        mixed_table,
        refs[:STATE],
        refs[STATE],
        ((1, near.lower, rim_lower), (3, near.upper, rim_upper)),
        ((9, 17), (24, 32)),
        ((9, 17), (23, 31)),
        ((10, 18), (22, 30)),
        ((6, 14),),
    )


def setup_kernel(place, mixed_table, far0, far1, *refs):
    refs = refs[STATE + 1 :]
    state, f1 = refs[:STATE], refs[STATE]
    gx1, gy1, via1, cap1, total1, weights1, x1 = refs[STATE + 1 : STATE + 8]
    gx2, gy2, below2, cap2, f2, go0, go1, spare1 = refs[STATE + 8 :]
    far = Sides(place, 2, far0, far1)
    below1 = state[9]
    prepare(
        place,
        mixed_table,
        state,
        f1,
        (
            (0, far.lower, lambda n: far.lower(n, 2)),
            (4, far.upper, lambda n: far.upper(n, 2)),
        ),
        ((1, 9), (32, 40)),
        ((1, 9), (31, 39)),
        ((2, 10), (30, 38)),
        ((2, 6), (14, 18)),
    )
    fine = Level(4, *state[:7])
    middle = Level(2, gx1, gy1, via1, below1, cap1, total1, weights1)
    coarse = Level(1, gx2, gy2, None, below2, cap2, None, None)
    coarsen(fine, middle, EXT1)
    coarsen(middle, coarse, EXT2)
    sum_below(below1, below2, 1, 0, EXT2)
    rows_loop(1, EXT1 - 1, middle.set_total)
    middle.first_relax(spare1, f1, 2, 18)
    middle.relax(x1, spare1, f1, 3, 17)
    middle.restrict(f2, x1, f1, 2, 8)
    ups, downs = [], []
    for target, first, outer in ((ups, 2, 2), (downs, 4, 6)):
        for j in range(4):
            for k in range(SECTIONS):
                target.append(f2[first + j, k])
        for j in range(2):
            target.extend((gy2[outer + j, 0], below2[outer + j, 0], cap2[outer + j, 0]))
        for j in range(3):
            target.append(gx2[outer + j, 0])
    for n, (up, down) in enumerate(zip(ups, downs)):
        go0[n] = jnp.where(far.odd, down, up)
        go1[n] = jnp.where(far.odd, up, down)


def middle_kernel(place, *refs):
    (gx0, gy0, via0, below0, cap0, total0, weights0, f0, x0) = refs[0:9]
    (gx1, gy1, via1, below1, cap1, total1, weights1, f1, x1) = refs[9:18]
    (gx2, gy2, below2, cap2, f2, got0, got1) = refs[18:25]
    got = Sides(place, 2, got0, got1)
    (x0_out, f1_out, go_side, gxw, gyw, viaw, beloww, weightsw) = refs[25:33]
    (capw, totalw, fw, xa, xb, ya, yb, za, f1_own) = refs[33:42]
    fine = Level(4, gx0, gy0, via0, below0, cap0, total0, weights0)
    middle = Level(2, gx1, gy1, via1, below1, cap1, total1, weights1)
    coarse = Level(1, gxw, gyw, viaw, beloww, capw, totalw, weightsw)
    for j in range(4):
        for k in range(SECTIONS):
            fw[j, k] = got.lower(5 * j + k)
            fw[10 + j, k] = got.upper(5 * j + k)
    for j in range(2):
        for near, source in ((j, got.lower), (12 + j, got.upper)):
            gyw[near, 0] = source(20 + 3 * j)
            gyw[near, 1] = from_right(source(20 + 3 * j))
            beloww[near, 0] = source(21 + 3 * j)
            capw[near, 0] = source(22 + 3 * j)
    for j in range(3):
        gxw[j, 0] = got.lower(26 + j)
        gxw[12 + j, 0] = got.upper(26 + j)
    for j in range(6):
        for k in range(SECTIONS):
            fw[4 + j, k] = f2[2 + j, k]
    for j in range(10):
        gyw[2 + j, 0] = gy2[j, 0]
        gyw[2 + j, 1] = gy2[j, 1]
        beloww[2 + j, 0] = below2[j, 0]
        capw[2 + j, 0] = cap2[j, 0]
    for j in range(1, 10):
        gxw[2 + j, 0] = gx2[j, 0]
    rows_loop(0, WIDE2, coarse.set_total)
    coarse.first_relax(xa, fw, 0, 14)
    coarse.relax(xb, xa, fw, 1, 13)
    coarse.relax(xa, xb, fw, 2, 12)
    coarse.relax(xb, xa, fw, 3, 11)
    middle.correct(ya, x1, xb, 3, 17, 2)
    middle.relax(yb, ya, f1, 4, 16)
    middle.relax(ya, yb, f1, 5, 15)
    fine.correct(x0_out, x0, ya, 10, 30)
    fine.relax(za, x0_out, f0, 11, 29)
    fine.relax(x0_out, za, f0, 12, 28)
    fine.relax(za, x0_out, f0, 13, 27)
    fine.relax(x0_out, za, f0, 14, 26)
    fine.restrict(f1_own, x0_out, f0, 8, 12, -8)
    for j in range(4):
        for n in range(10):
            f1_out[10 * j + n] = f1_own[j, n]
    for j in range(10):
        packs = packed([f1_own[n // 10, n % 10] for n in range(4 * j, 4 * j + 4)])
        for t in range(3):
            go_side[3 * j + t] = packs[t]


def lower_kernel(place, *refs):
    (gx1, gy1, via1, below1, cap1, total1, weights1) = refs[0:7]
    own, got0, got1 = refs[7:10]
    got = Sides(place, 1, got0, got1)
    f1, x1, f2_out = refs[10:13]
    (xa,) = refs[13:14]
    middle = Level(2, gx1, gy1, via1, below1, cap1, total1, weights1)
    for j in range(10):
        for first, source in ((4, got.lower), (12, got.upper)):
            values = unpacked([source(3 * j + t) for t in range(3)])
            for t in range(4):
                n = 4 * j + t
                f1[first + n // 10, n % 10] = values[t]
        for n in range(4 * j, 4 * j + 4):
            f1[8 + n // 10, n % 10] = own[n]
    middle.first_relax(xa, f1, 4, 16)
    middle.relax(x1, xa, f1, 5, 15)
    middle.restrict(f2_out, x1, f1, 3, 7, -3)


def finish_kernel(place, *refs):
    (gx0, gy0, via0, below0, weights0, f0, x0) = refs[0:7]
    (gx1, gy1, via1, below1, weights1, f1, x1) = refs[7:14]
    (gxw, gyw, viaw, beloww, weightsw, own, got0, got1, voltage) = refs[14:23]
    got = Sides(place, 2, got0, got1)
    sections, next_voltage = refs[23:25]
    fw, xa, xb, ya, yb, za, zb, mixed, turn = refs[25:34]
    fine = Level(4, gx0, gy0, via0, below0, None, None, weights0)
    middle = Level(2, gx1, gy1, via1, below1, None, None, weights1)
    coarse = Level(1, gxw, gyw, viaw, beloww, None, None, weightsw)
    for j in range(4):
        for k in range(SECTIONS):
            fw[1 + j, k] = got.lower(j, k)
            fw[5 + j, k] = own[j, k]
            fw[9 + j, k] = got.upper(j, k)
    block = jnp.full((LAYERS, LANES), place[0], jnp.int32)
    for k in range(SECTIONS):
        fw[4, k] = jnp.where(block == 1, got.lower(1, k), fw[4, k])
        fw[9, k] = jnp.where(block == 30, got.upper(2, k), fw[9, k])
    coarse.first_relax(xa, fw, 1, 13)
    coarse.relax(xb, xa, fw, 2, 12)
    coarse.relax(xa, xb, fw, 3, 11)
    coarse.relax(xb, xa, fw, 4, 10)
    middle.correct(ya, x1, xb, 5, 15, 2)
    middle.relax(yb, ya, f1, 6, 14)
    middle.relax(ya, yb, f1, 7, 13)
    fine.correct(za, x0, ya, 14, 26)
    fine.relax(zb, za, f0, 15, 25)
    fine.relax(za, zb, f0, 16, 24)

    def mix(row):
        for p in range(4):
            values = [za[16 + row, 4 * k + p] for k in range(SECTIONS)]
            for j in range(SECTIONS):
                total = TRANSFORM[j][0] * values[0]
                for k in range(1, SECTIONS):
                    total = total + TRANSFORM[j][k] * values[k]
                mixed[p, 8 * j + row] = total

    rows_loop(0, 8, mix)
    result = None
    for p in range(4):
        lane = lax.broadcasted_iota(jnp.int32, (LANES, 256), 0)
        column = lax.broadcasted_iota(jnp.int32, (LANES, 256), 1)
        chooser = jnp.where((lane < 64) & (column == 4 * lane + p), 1.0, 0.0).astype(jnp.bfloat16)
        part = selected(mixed[p].reshape(320, LANES), chooser)
        result = part if result is None else result + part
    for j in range(SECTIONS):
        for row in range(8):
            at = (8 * j + row) * 8
            for h in range(2):
                turn[j, h, pl.ds(row, 8, stride=8), :] = result[
                    at : at + 8, h * 128 : h * 128 + 128
                ]
        for h in range(2):
            sections[j, :, h * 128 : h * 128 + 128] = turn[j, h]
    next_voltage[...] = voltage[...] + sections[SECTIONS - 1]


VMEM = pltpu.MemorySpace.VMEM
SMEM = pltpu.MemorySpace.SMEM


def vregs(*shape):
    return pltpu.VMEM(shape + (LAYERS, LANES), jnp.float32)


def scratch(*shape):
    return pltpu.VMEM(shape + (LAYERS, LANES), jnp.float32)


def call(kernel, inputs, outs, scratches=(), scalars=0, outside=False, aliases=()):
    space = pltpu.MemorySpace.HBM if outside else VMEM
    inputs = [
        value if n < scalars else pltpu.with_memory_space_constraint(value, space)
        for n, value in enumerate(inputs)
    ]
    return pl.pallas_call(
        kernel,
        out_shape=outs,
        in_specs=[pl.BlockSpec(memory_space=SMEM)] * scalars
        + [pl.BlockSpec(memory_space=space)] * (len(inputs) - scalars),
        out_specs=[pl.BlockSpec(memory_space=VMEM)] * len(outs),
        scratch_shapes=list(scratches),
        input_output_aliases=dict(aliases),
        compiler_params=pltpu.CompilerParams(vmem_limit_bytes=12 * 2**20),
    )(*inputs)


def turned(value, axis, count, shift):
    return lax.ppermute(value, axis, [(i, (i + shift) % count) for i in range(count)])


def paired(value, distance):
    rows = lax.axis_size("section") * lax.axis_size("gx")
    columns = lax.axis_size("gy")
    values = value if isinstance(value, tuple) else (value, value)
    result = []
    for which in range(2):
        pairs = []
        for row in range(rows):
            up = (row // distance) % 2 == which
            other = row + distance if up else row - distance
            for column in range(columns):
                target = (other, column)
                if not 0 <= other < rows:
                    target = (row, column ^ 1) if distance == 1 else (row ^ 1, column)
                pairs.append((row * columns + column, target[0] * columns + target[1]))
        result.append(lax.ppermute(values[which], ("section", "gx", "gy"), pairs))
    return result


def local(voltage, capacity, node_class, via_sites, ball_sites, load_type, load_table):
    columns = lax.axis_size("gy")
    volts = voltage.reshape(64, 256)
    own, left, right = call(
        gather_kernel,
        (
            volts,
            capacity.reshape(64, 256),
            node_class.reshape(64, 256),
            via_sites.reshape(56, 256),
            ball_sites,
            load_type,
        ),
        [
            vregs(33, 2),
            pltpu.VMEM((264, 64), jnp.float32),
            pltpu.VMEM((264, 64), jnp.float32),
        ],
        [
            pltpu.VMEM((4, 2, 64, LANES), jnp.float32),
            pltpu.VMEM((64, 256), jnp.float32),
            pltpu.VMEM((64, 256), jnp.float32),
            pltpu.VMEM((64, 256), jnp.int32),
            pltpu.VMEM((56, 256), jnp.int32),
            pltpu.VMEM((8, 256), jnp.int32),
            pltpu.VMEM((8, 256), jnp.int32),
            pltpu.SemaphoreType.DMA((6,)),
            pltpu.VMEM((264, 256), jnp.float32),
        ],
        outside=True,
    )
    place = jnp.stack(
        [
            lax.axis_index("section") * lax.axis_size("gx") + lax.axis_index("gx"),
            lax.axis_index("gy"),
        ]
    ).astype(jnp.int32)
    near = paired(own, 1)
    from_lower = turned(right, "gy", columns, 1)
    from_upper = turned(left, "gy", columns, -1)
    mixed_table = jnp.einsum(
        "tk,jk->tj", load_table, jnp.asarray(INVERSE, jnp.float32), precision=lax.Precision.HIGHEST
    )
    (whole,) = call(rim_kernel, (own, from_lower, from_upper), [vregs(33, 3)])
    far = paired(whole, 2)
    go_right, go_left = call(edge_kernel, (place, *near), [vregs(33), vregs(33)], (), 1)
    edge_left = turned(go_right, "gy", columns, 1)
    edge_right = turned(go_left, "gy", columns, -1)
    state_shapes = [
        vregs(EXT0, 4),
        vregs(EXT0, 5),
        vregs(EXT0, 4),
        vregs(EXT0, 4),
        vregs(EXT0, 4),
        vregs(EXT0, 4),
        vregs(EXT0, 20),
        vregs(EXT0, 20),
        vregs(EXT0, 20),
        vregs(EXT1, 2),
        vregs(EXT0, 4),
        vregs(EXT0, 4),
        pltpu.VMEM((20, EXT0, LANES), jnp.float32),
        vregs(EXT0, 20),
    ]
    state = call(own_kernel, (place, mixed_table, whole), state_shapes, (), 2)
    state = call(
        near_kernel,
        (place, mixed_table, *near, edge_left, edge_right, *state),
        [*state_shapes, vregs(EXT1, 10)],
        (),
        2,
        aliases=[(6 + n, n) for n in range(STATE)],
    )
    state = call(
        setup_kernel,
        (place, mixed_table, *far, *state),
        [
            *state_shapes,
            vregs(EXT1, 10),
            vregs(EXT1, 2),
            vregs(EXT1, 3),
            vregs(EXT1, 2),
            vregs(EXT1, 2),
            vregs(EXT1, 2),
            vregs(EXT1, 10),
            vregs(EXT1, 10),
            vregs(EXT2, 1),
            vregs(EXT2, 2),
            vregs(EXT2, 1),
            vregs(EXT2, 1),
            vregs(EXT2, 5),
            vregs(29),
            vregs(29),
        ],
        [scratch(EXT1, 10)],
        2,
        aliases=[(4 + n, n) for n in range(STATE + 1)],
    )
    fine, below1, f1 = state[:9], state[9], state[STATE]
    gx1, gy1, via1, cap1, total1, weights1, x1 = state[STATE + 1 : STATE + 8]
    middle = (gx1, gy1, via1, below1, cap1, total1, weights1, f1, x1)
    coarse = state[STATE + 8 : STATE + 13]
    got = paired(tuple(state[STATE + 13 :]), 2)
    x0, f1_own, go_side, gxw, gyw, viaw, beloww, weightsw = call(
        middle_kernel,
        (place, *fine, *middle, *coarse, *got),
        [
            vregs(EXT0, 20),
            vregs(40),
            vregs(30),
            vregs(WIDE2 + 1, 1),
            vregs(WIDE2, 2),
            vregs(WIDE2, 1),
            vregs(WIDE2, 1),
            vregs(WIDE2, 5),
        ],
        [
            scratch(WIDE2, 1),
            scratch(WIDE2, 1),
            scratch(WIDE2, 5),
            scratch(WIDE2, 5),
            scratch(WIDE2, 5),
            scratch(EXT1, 10),
            scratch(EXT1, 10),
            scratch(EXT0, 20),
            scratch(4, 10),
        ],
        1,
    )
    got = paired(go_side, 1)
    f1, x1, f2_own = call(
        lower_kernel,
        (place, *middle[:7], f1_own, *got),
        [vregs(EXT1, 10), vregs(EXT1, 10), vregs(4, 5)],
        [scratch(EXT1, 10)],
        1,
    )
    got = paired(f2_own, 2)
    sections, next_voltage = call(
        finish_kernel,
        (
            place,
            *fine[:4],
            *fine[6:8],
            x0,
            *middle[:4],
            middle[6],
            f1,
            x1,
            gxw,
            gyw,
            viaw,
            beloww,
            weightsw,
            f2_own,
            *got,
            volts,
        ),
        [
            jax.ShapeDtypeStruct((SECTIONS, 64, 256), jnp.float32),
            jax.ShapeDtypeStruct((64, 256), jnp.float32),
        ],
        [
            scratch(WIDE2, 5),
            scratch(WIDE2, 5),
            scratch(WIDE2, 5),
            scratch(EXT1, 10),
            scratch(EXT1, 10),
            scratch(EXT0, 20),
            scratch(EXT0, 20),
            scratch(4, 40),
            pltpu.VMEM((SECTIONS, 2, 64, LANES), jnp.float32),
        ],
        1,
    )
    return sections.reshape((SECTIONS,) + voltage.shape), next_voltage.reshape(voltage.shape)


def solution(mesh):
    return jax.shard_map(
        local,
        mesh=mesh,
        in_specs=(
            P(None, ("section", "gx"), "gy"),
            P(None, ("section", "gx"), "gy"),
            P(None, ("section", "gx"), "gy"),
            P(None, ("section", "gx"), "gy"),
            P(("section", "gx"), "gy"),
            P(("section", "gx"), "gy"),
            P(),
        ),
        out_specs=(P(None, None, ("section", "gx"), "gy"), P(None, ("section", "gx"), "gy")),
        check_vma=False,
    )
```

```python
import jax
import jax.numpy as jnp
from jax import lax
from jax.experimental import pallas as pl
from jax.experimental.pallas import tpu as pltpu
from jax.sharding import PartitionSpec as P

SECTIONS = 5
LOADS = 16
LAYERS = 8
LANES = 128
EXT0 = 40
EXT1 = 20
EXT2 = 10
WIDE2 = 14
TILES = 160

node_table = (0.35, 0.55, 0.8, 1.1, 1.5, 2.0, 2.7, 3.6)
via_conductance = 2.5
ball_conductance = 4.0
damping = 0.8
slab_partner = (0, 2, 1, 4, 3)


def pair_times(first, second):
    return (
        first[0] * second[0] - first[1] * second[1],
        first[0] * second[1] + first[1] * second[0],
    )


def pair_over(first, second):
    divisor = second[0] * second[0] + second[1] * second[1]
    return (
        (first[0] * second[0] + first[1] * second[1]) / divisor,
        (first[1] * second[0] - first[0] * second[1]) / divisor,
    )


def pair_minus(first, second):
    return (first[0] - second[0], first[1] - second[1])


def poly_value(coeffs, point):
    total = (0.0, 0.0)
    for c in reversed(coeffs):
        total = pair_times(total, point)
        total = (total[0] + c, total[1])
    return total


def poly_product(first, second):
    result = [0.0] * (len(first) + len(second) - 1)
    for i in range(len(first)):
        for j in range(len(second)):
            result[i + j] = result[i + j] + first[i] * second[j]
    return result


def poly_roots(coeffs):
    leading = coeffs[-1]
    scaled = [c / leading for c in coeffs]
    degree = len(coeffs) - 1
    guesses = []
    current = (1.0, 0.0)
    for k in range(degree):
        guesses.append(current)
        current = pair_times(current, (0.4, 0.9))
    for repeat_index in range(800):
        for k in range(degree):
            divisor = (1.0, 0.0)
            for j in range(degree):
                if j != k:
                    divisor = pair_times(divisor, pair_minus(guesses[k], guesses[j]))
            guesses[k] = pair_minus(guesses[k], pair_over(poly_value(scaled, guesses[k]), divisor))
    return guesses


def matrix_product(first, second):
    return [
        [
            sum((first[i][k] * second[k][j] for k in range(len(second))))
            for j in range(len(second[0]))
        ]
        for i in range(len(first))
    ]


def matrix_inverse(matrix):
    order = len(matrix)
    work = [list(matrix[i]) + [1.0 if i == j else 0.0 for j in range(order)] for i in range(order)]
    for column in range(order):
        pivot = column
        for i in range(column + 1, order):
            if abs(work[i][column]) > abs(work[pivot][column]):
                pivot = i
        work[column], work[pivot] = (work[pivot], work[column])
        factor = work[column][column]
        work[column] = [entry / factor for entry in work[column]]
        for i in range(order):
            if i != column:
                scale_row = work[i][column]
                work[i] = [work[i][j] - scale_row * work[column][j] for j in range(2 * order)]
    return [row[order:] for row in work]


def eigen_vector(matrix, value):
    order = len(matrix)
    size_inner = order - 1
    system = []
    for i in range(size_inner):
        row = []
        for j in range(order):
            entry = (matrix[i][j], 0.0)
            if i == j:
                entry = pair_minus(entry, value)
            row.append(entry)
        row[order - 1] = (-row[order - 1][0], -row[order - 1][1])
        system.append(row)
    for column in range(size_inner):
        pivot = column
        for i in range(column + 1, size_inner):
            left_size = system[i][column][0] ** 2 + system[i][column][1] ** 2
            right_size = system[pivot][column][0] ** 2 + system[pivot][column][1] ** 2
            if left_size > right_size:
                pivot = i
        system[column], system[pivot] = (system[pivot], system[column])
        for i in range(size_inner):
            if i != column:
                factor = pair_over(system[i][column], system[column][column])
                system[i] = [
                    pair_minus(system[i][j], pair_times(factor, system[column][j]))
                    for j in range(order)
                ]
    vector = [pair_over(system[i][order - 1], system[i][i]) for i in range(size_inner)]
    vector.append((1.0, 0.0))
    return vector


def radau_tables():
    section_count = 5
    generator = [1.0]
    for k in range(section_count - 1):
        generator = poly_product(generator, [0.0, 1.0])
    for k in range(section_count):
        generator = poly_product(generator, [-1.0, 1.0])
    for k in range(section_count - 1):
        generator = [j * generator[j] for j in range(1, len(generator))]
    abscissae = sorted((root[0] for root in poly_roots(generator)))
    vander = [[abscissae[i] ** j for j in range(section_count)] for i in range(section_count)]
    integrals = [
        [abscissae[i] ** (j + 1) / (j + 1) for j in range(section_count)]
        for i in range(section_count)
    ]
    butcher = matrix_product(integrals, matrix_inverse(vander))
    inverse = matrix_inverse(butcher)
    coeffs = [0.0] * (section_count + 1)
    coeffs[section_count] = 1.0
    current = [[0.0] * section_count for _ in range(section_count)]
    for k in range(1, section_count + 1):
        current = matrix_product(inverse, current)
        for i in range(section_count):
            current[i][i] = current[i][i] + coeffs[section_count - k + 1]
        applied = matrix_product(inverse, current)
        coeffs[section_count - k] = -sum((applied[i][i] for i in range(section_count))) / k
    eigen_values = poly_roots(coeffs)
    real_pick = 0
    for k in range(section_count):
        if abs(eigen_values[k][1]) < abs(eigen_values[real_pick][1]):
            real_pick = k
    upper_half = [k for k in range(section_count) if eigen_values[k][1] > 1e-09]
    upper_half = sorted(upper_half, key=lambda k: -eigen_values[k][0])
    columns = [[entry[0] for entry in eigen_vector(inverse, (eigen_values[real_pick][0], 0.0))]]
    for k in upper_half:
        vector = eigen_vector(inverse, eigen_values[k])
        columns.append([entry[0] for entry in vector])
        columns.append([entry[1] for entry in vector])
    transform = [[columns[j][i] for j in range(section_count)] for i in range(section_count)]
    inverse_transform = matrix_inverse(transform)
    blocks = matrix_product(matrix_product(inverse_transform, inverse), transform)
    diagonal = [blocks[k][k] for k in range(section_count)]
    coupling = [
        blocks[k][slab_partner[k]] if slab_partner[k] != k else 0.0 for k in range(section_count)
    ]
    return (transform, inverse_transform, diagonal, coupling)


TRANSFORM, INVERSE, DIAGONAL, COUPLING = radau_tables()
SHIFTS = (
    DIAGONAL[0],
    0.5 * (DIAGONAL[1] + DIAGONAL[2]),
    0.5 * (DIAGONAL[3] + DIAGONAL[4]),
)
COUPLES = (0.5 * (COUPLING[1] - COUPLING[2]), 0.5 * (COUPLING[3] - COUPLING[4]))
ROW_SUMS = tuple(sum(row) for row in INVERSE)


def from_right(value):
    return pltpu.roll(value, LANES - 1, 1)


def from_left(value):
    return pltpu.roll(value, 1, 1)


def from_above(value):
    return pltpu.roll(value, LAYERS - 1, 0)


def from_below(value):
    return pltpu.roll(value, 1, 0)


def lane_index():
    return lax.broadcasted_iota(jnp.int32, (LAYERS, LANES), 1)


def layer_index():
    return lax.broadcasted_iota(jnp.int32, (LAYERS, LANES), 0)


def spread(first, second, rim):
    own = lane_index() < 64
    inner = (first, pltpu.roll(first, 64, 1), second, pltpu.roll(second, 64, 1))
    outer = (rim, pltpu.roll(rim, 96, 1), pltpu.roll(rim, 64, 1), pltpu.roll(rim, 32, 1))
    return [jnp.where(own, near, far) for near, far in zip(inner, outer)]


def packed(values):
    lane = lane_index()
    dead = (lane >= 80) & (lane < 112)
    one, two, three, last = values
    tail = jnp.where(lane < 96, pltpu.roll(last, 96, 1), pltpu.roll(last, 32, 1))
    return [
        jnp.where(dead, pltpu.roll(last, 80, 1), one),
        jnp.where(dead, pltpu.roll(last, 48, 1), two),
        jnp.where(dead, tail, three),
    ]


def unpacked(packs):
    lane = lane_index()
    one, two, three = packs
    last = jnp.where(
        lane < 64,
        jnp.where(lane < 32, pltpu.roll(one, 48, 1), pltpu.roll(two, 80, 1)),
        jnp.where(lane < 96, pltpu.roll(three, 96, 1), pltpu.roll(three, 32, 1)),
    )
    return [one, two, three, last]


def rows_loop(low, high, body, unroll=2):
    steps = (high - low) // unroll

    def step(n, carry):
        for j in range(unroll):
            body(low + n * unroll + j)
        return carry

    if steps > 1:
        lax.fori_loop(0, steps, step, 0)
    elif steps == 1:
        step(0, 0)
    for i in range(low + steps * unroll, high):
        body(i)


class Sides:
    def __init__(self, place, distance, first, second):
        self.odd = (place[0] & distance) != 0
        self.first, self.second = first, second

    def lower(self, *at):
        return jnp.where(self.odd, self.first[at], self.second[at])

    def upper(self, *at):
        return jnp.where(self.odd, self.second[at], self.first[at])


class Level:
    def __init__(self, phases, gx, gy, via, below, cap, total, weights):
        self.phases = phases
        self.unroll = 8 // phases
        self.gx, self.gy = gx, gy
        self.via, self.below = via, below
        self.cap, self.total, self.weights = cap, total, weights

    def sides(self, centre, p):
        right = centre[p + 1] if p < self.phases - 1 else from_right(centre[0])
        left = centre[p - 1] if p > 0 else from_left(centre[self.phases - 1])
        return right, left

    def inflow(self, coeffs, centre, p, upper, lower):
        gx_lower, gx_upper, gy_left, gy_right, via, below = coeffs
        right, left = self.sides(centre, p)
        here = centre[p]
        return (
            (gx_upper * upper + gx_lower * lower)
            + (gy_right * right + gy_left * left)
            + (via * from_above(here) + below * from_below(here))
        )

    def coeffs(self, i, p):
        return (
            self.gx[i, p],
            self.gx[i + 1, p],
            self.gy[i, p],
            self.gy[i, p + 1],
            self.via[i, p],
            self.below[i, p],
        )

    def set_total(self, i):
        bottom = layer_index() == 0
        for p in range(self.phases):
            grounded = self.below[i, p]
            below = jnp.where(bottom, 0.0, grounded)
            via = from_above(below)
            total = (
                (self.gx[i, p] + self.gx[i + 1, p])
                + (self.gy[i, p] + self.gy[i, p + 1])
                + (via + grounded)
            )
            self.below[i, p] = below
            self.via[i, p] = via
            self.total[i, p] = total
            cap = self.cap[i, p]
            self.weights[i, p * 5] = damping / (SHIFTS[0] * cap + total)
            for s in range(2):
                direct = SHIFTS[s + 1] * cap + total
                cross = COUPLES[s] * cap
                scale = damping / (direct * direct + cross * cross)
                self.weights[i, p * 5 + 1 + 2 * s] = direct * scale
                self.weights[i, p * 5 + 2 + 2 * s] = -(cross * scale)

    def weighted(self, i, p, values):
        w = [self.weights[i, p * 5 + m] for m in range(5)]
        out = [w[0] * values[0]]
        for s in range(2):
            first, second = values[1 + 2 * s], values[2 + 2 * s]
            out.append(w[1 + 2 * s] * first + w[2 + 2 * s] * second)
            out.append(w[1 + 2 * s] * second - w[2 + 2 * s] * first)
        return out

    def first_relax(self, target, source, low, high):
        def body(i):
            for p in range(self.phases):
                values = [source[i, k * self.phases + p] for k in range(SECTIONS)]
                for k, value in enumerate(self.weighted(i, p, values)):
                    target[i, k * self.phases + p] = value

        rows_loop(low, high, body, self.unroll)

    def gathered(self, iterate, source, i):
        count = self.phases
        centres = [[iterate[i, k * count + p] for p in range(count)] for k in range(SECTIONS)]
        sums = []
        for p in range(count):
            coeffs = self.coeffs(i, p)
            sums.append(
                [
                    source[i, k * count + p]
                    + self.inflow(
                        coeffs,
                        centres[k],
                        p,
                        iterate[i + 1, k * count + p],
                        iterate[i - 1, k * count + p],
                    )
                    for k in range(SECTIONS)
                ]
            )
        return centres, sums

    def relax(self, target, iterate, source, low, high):
        count = self.phases

        def body(i):
            centres, sums = self.gathered(iterate, source, i)
            for p in range(count):
                for k, value in enumerate(self.weighted(i, p, sums[p])):
                    target[i, k * count + p] = (1.0 - damping) * centres[k][p] + value

        rows_loop(low, high, body, self.unroll)

    def residual(self, iterate, source, i):
        centres, sums = self.gathered(iterate, source, i)
        result = []
        for p in range(self.phases):
            cap, total = self.cap[i, p], self.total[i, p]
            x = [centres[k][p] for k in range(SECTIONS)]
            out = [sums[p][0] - (SHIFTS[0] * cap + total) * x[0]]
            for s in range(2):
                direct = SHIFTS[s + 1] * cap + total
                cross = COUPLES[s] * cap
                a, b = 1 + 2 * s, 2 + 2 * s
                out.append(sums[p][a] - (direct * x[a] + cross * x[b]))
                out.append(sums[p][b] - (direct * x[b] - cross * x[a]))
            result.append(out)
        return result

    def restrict(self, target, iterate, source, low, high, shift=0):
        half = self.phases // 2

        def body(row):
            one = self.residual(iterate, source, 2 * row)
            two = self.residual(iterate, source, 2 * row + 1)
            for k in range(SECTIONS):
                for q in range(half):
                    target[row + shift, k * half + q] = (one[2 * q][k] + one[2 * q + 1][k]) + (
                        two[2 * q][k] + two[2 * q + 1][k]
                    )

        rows_loop(low, high, body, self.unroll // 2)

    def correct(self, target, iterate, coarse, low, high, shift=0):
        count, half = self.phases, self.phases // 2

        def body(i):
            row = lax.shift_right_logical(i, 1) + shift
            for k in range(SECTIONS):
                for q in range(half):
                    value = coarse[row, k * half + q]
                    for p in (2 * q, 2 * q + 1):
                        target[i, k * count + p] = iterate[i, k * count + p] + value

        rows_loop(low, high, body, self.unroll)


def coarsen(fine, coarse, rows):
    half = coarse.phases

    def body(row):
        for q in range(half):
            for ref_out, ref_in in ((coarse.cap, fine.cap),):
                ref_out[row, q] = (ref_in[2 * row, 2 * q] + ref_in[2 * row, 2 * q + 1]) + (
                    ref_in[2 * row + 1, 2 * q] + ref_in[2 * row + 1, 2 * q + 1]
                )
        for q in range(half + 1):
            coarse.gy[row, q] = fine.gy[2 * row, 2 * q] + fine.gy[2 * row + 1, 2 * q]

    rows_loop(0, rows, body, 4)

    def body_gx(row):
        for q in range(half):
            coarse.gx[row, q] = fine.gx[2 * row, 2 * q] + fine.gx[2 * row, 2 * q + 1]

    rows_loop(1, rows, body_gx, 4)


def sum_below(fine_below, coarse_below, phases, low, high):
    def body(row):
        for q in range(phases):
            coarse_below[row, q] = (
                fine_below[2 * row, 2 * q] + fine_below[2 * row, 2 * q + 1]
            ) + (fine_below[2 * row + 1, 2 * q] + fine_below[2 * row + 1, 2 * q + 1])

    rows_loop(low, high, body, 4)


def gather_kernel(*refs):
    own, left, right, work = refs[6:10]
    whole = refs[17]
    voltage, capacity, node_class, via, ball, load = refs[10:16]
    copies = [
        pltpu.make_async_copy(source, target, refs[16].at[n])
        for n, (source, target) in enumerate(zip(refs[:6], refs[10:16]))
    ]
    for copy in copies:
        copy.start()
    for copy in copies:
        copy.wait()
    classes = node_class[...]
    conduct = jnp.full(classes.shape, node_table[0], jnp.float32)
    for c in range(1, len(node_table)):
        conduct = jnp.where(classes == c, node_table[c], conduct)
    grounded = jnp.where(ball[...] == 1, ball_conductance, 0.0)
    upright = jnp.where(via[...] == 1, via_conductance, 0.0)
    for h in range(2):
        half = slice(h * 128, h * 128 + 128)
        work[0, h] = voltage[:, half]
        work[1, h] = capacity[:, half]
        work[2, h] = conduct[:, half]
        work[3, h, 0:8] = grounded[:, half]
        work[3, h, 8:64] = upright[:, half]
    for row in range(8):
        for a in range(4):
            at = (row * 4 + a) * 8
            for h in range(2):
                whole[at : at + 8, h * 128 : h * 128 + 128] = work[
                    a, h, pl.ds(row, 8, stride=8), :
                ]
    whole[256:264] = load[...].astype(jnp.float32)
    left[...] = whole[:, :64]
    right[...] = whole[:, 192:]
    column = lax.broadcasted_iota(jnp.int32, (256, 256), 0)
    slot = lax.broadcasted_iota(jnp.int32, (256, 256), 1)
    wanted = 4 * (slot % 64) + slot // 64
    result = selected(whole[...], jnp.where(column == wanted, 1.0, 0.0).astype(jnp.bfloat16))
    for n in range(33):
        for h in range(2):
            own[n, h] = result[8 * n : 8 * n + 8, 128 * h : 128 * h + 128]


def three_parts(value):
    high = value.astype(jnp.bfloat16)
    rest = value - high.astype(jnp.float32)
    middle = rest.astype(jnp.bfloat16)
    low = (rest - middle.astype(jnp.float32)).astype(jnp.bfloat16)
    return high, middle, low


def selected(value, chooser):
    high, middle, low = (
        jnp.dot(part, chooser, preferred_element_type=jnp.float32) for part in three_parts(value)
    )
    return high + (middle + low)


def rim_kernel(own, from_lower, from_upper, whole):
    column = lax.broadcasted_iota(jnp.int32, (64, LANES), 0)
    slot = lax.broadcasted_iota(jnp.int32, (64, LANES), 1)
    group, place = slot // 32, slot % 32
    below = (place >= 16) & (column == 4 * (place - 16) + (group + 1) % 4)
    above = (place < 16) & (column == 4 * place + (group + 2) % 4)
    result = selected(from_lower[...], jnp.where(below, 1.0, 0.0).astype(jnp.bfloat16))
    result = result + selected(
        from_upper[...], jnp.where(above, 1.0, 0.0).astype(jnp.bfloat16)
    )
    for n in range(33):
        whole[n, 2] = result[8 * n : 8 * n + 8]
        for h in range(2):
            whole[n, h] = own[n, h]


def edge_kernel(place, near0, near1, go_right, go_left):
    lane = lane_index()
    group = lane // 32
    late = lane % 32 >= 16
    near = Sides(place, 1, near0, near1)

    def chosen(one, two, three, four):
        return jnp.where(
            group < 2, jnp.where(group == 0, one, two), jnp.where(group == 2, three, four)
        )

    def body(n):
        rights, lefts = [], []
        for block in (near.lower, near.upper):
            first, second = block(n, 0), block(n, 1)
            first_far, first_near = pltpu.roll(first, 64, 1), pltpu.roll(first, 32, 1)
            second_far = pltpu.roll(second, 96, 1)
            rights.append(chosen(first_near, second, second_far, first_far))
            lefts.append(chosen(second, second_far, first_far, first_near))
        go_right[n] = jnp.where(late, rights[0], pltpu.roll(rights[1], 112, 1))
        go_left[n] = jnp.where(late, pltpu.roll(lefts[1], 16, 1), lefts[0])

    rows_loop(0, 33, body, 11)


def prepare(place, mixed_table, state, f1, blocks, gx_rows, total_rows, relax_rows, sum_rows):
    (gx0, gy0, via0, below0, cap0, total0, weights0, f0, x0) = state[:9]
    below1, volt, conduct, surface, spare = state[9:14]
    fine = Level(4, gx0, gy0, via0, below0, cap0, total0, weights0)
    row_block, column_block = place[0], place[1]
    lane = lane_index()
    edge = ((lane == 0) & (column_block == 0)) | ((lane == 64) & (column_block == 3))
    joined = jnp.where(edge, 0.0, 2.0)
    top = layer_index() == LAYERS - 1

    def series(near, far):
        return 2.0 * near * far / (near + far)

    def set_gy(i):
        here = [conduct[i, p] for p in range(4)]
        before = from_left(here[3])
        first = joined * before * here[0] / (before + here[0])
        gy0[i, 0] = first
        for p in range(1, 4):
            gy0[i, p] = series(here[p - 1], here[p])

    def turn_gy(i):
        gy0[i, 4] = from_right(gy0[i, 0])

    for b, block, rim in blocks:

        def place_row(s, block=block, rim=rim, b=b):
            for a, ref in enumerate((volt, cap0, conduct, below0)):
                n = 4 * s + a
                phases = spread(block(n, 0), block(n, 1), rim(n))
                for p in range(4):
                    ref[8 * b + s, p] = phases[p]

        rows_loop(0, 8, place_row, 4)
        loads = spread(block(32, 0), block(32, 1), rim(32))
        for p in range(4):
            values = [jnp.zeros((8, LANES), jnp.float32) for _ in range(SECTIONS)]
            for t in range(LOADS):
                chosen = loads[p] == float(t)
                values = [
                    jnp.where(chosen, mixed_table[SECTIONS * t + k], values[k]) for k in range(SECTIONS)
                ]
            for k in range(SECTIONS):
                at = 8 * b * TILES + (4 * k + p) * LAYERS + LAYERS - 1
                surface[pl.ds(at, 8, stride=TILES), :] = values[k]
        rows_loop(8 * b, 8 * b + 8, set_gy, 8)
        rows_loop(8 * b, 8 * b + 8, turn_gy, 8)
        sum_below(below0, below1, 2, 4 * b, 4 * b + 4)

    def set_gx(i):
        row = 8 * row_block - 16 + i
        twice = jnp.where((row == 0) | (row == 256), 0.0, 2.0)
        for p in range(4):
            near, far = conduct[i - 1, p], conduct[i, p]
            gx0[i, p] = twice * near * far / (near + far)

    def set_source(i):
        centre = [volt[i, p] for p in range(4)]
        for p in range(4):
            leak = total0[i, p] * centre[p] - fine.inflow(
                fine.coeffs(i, p), centre, p, volt[i + 1, p], volt[i - 1, p]
            )
            values = []
            for k in range(SECTIONS):
                at = pl.multiple_of(i * TILES + (4 * k + p) * LAYERS, LAYERS)
                drawn = surface[pl.ds(at, LAYERS), :]
                values.append(jnp.where(top, drawn, 0.0) - ROW_SUMS[k] * leak)
                f0[i, 4 * k + p] = values[k]
            for k, value in enumerate(fine.weighted(i, p, values)):
                spare[i, 4 * k + p] = value

    def set_row(i):
        fine.set_total(i)
        set_source(i)

    for low, high in gx_rows:
        rows_loop(low, high, set_gx, 4)
    for low, high in total_rows:
        rows_loop(low, high, set_row)
    for low, high in relax_rows:
        fine.relax(x0, spare, f0, low, high)
    for low, high in sum_rows:
        fine.restrict(f1, x0, f0, low, high)


STATE = 14


def own_kernel(place, mixed_table, whole, *refs):
    prepare(
        place,
        mixed_table,
        refs,
        None,
        ((2, lambda n, h: whole[n, h], lambda n: whole[n, 2]),),
        ((17, 24),),
        ((17, 23),),
        ((18, 22),),
        (),
    )


def near_kernel(place, mixed_table, near0, near1, edge_left, edge_right, *refs):
    refs = refs[STATE:]
    late = lane_index() % 32 >= 16
    near = Sides(place, 1, near0, near1)

    def rim_lower(n):
        return jnp.where(late, edge_left[n], edge_right[n])

    def rim_upper(n):
        return jnp.where(
            late, pltpu.roll(edge_left[n], 16, 1), pltpu.roll(edge_right[n], 112, 1)
        )

    prepare(
        place,
        mixed_table,
        refs[:STATE],
        refs[STATE],
        ((1, near.lower, rim_lower), (3, near.upper, rim_upper)),
        ((9, 17), (24, 32)),
        ((9, 17), (23, 31)),
        ((10, 18), (22, 30)),
        ((6, 14),),
    )


def setup_kernel(place, mixed_table, far0, far1, *refs):
    refs = refs[STATE + 1 :]
    state, f1 = refs[:STATE], refs[STATE]
    gx1, gy1, via1, cap1, total1, weights1, x1 = refs[STATE + 1 : STATE + 8]
    gx2, gy2, below2, cap2, f2, go0, go1, spare1 = refs[STATE + 8 :]
    far = Sides(place, 2, far0, far1)
    below1 = state[9]
    prepare(
        place,
        mixed_table,
        state,
        f1,
        (
            (0, far.lower, lambda n: far.lower(n, 2)),
            (4, far.upper, lambda n: far.upper(n, 2)),
        ),
        ((2, 9), (32, 39)),
        ((2, 9), (31, 38)),
        ((3, 10), (30, 37)),
        ((2, 6), (14, 18)),
    )
    fine = Level(4, *state[:7])
    middle = Level(2, gx1, gy1, via1, below1, cap1, total1, weights1)
    coarse = Level(1, gx2, gy2, None, below2, cap2, None, None)
    coarsen(fine, middle, EXT1)
    coarsen(middle, coarse, EXT2)
    sum_below(below1, below2, 1, 0, EXT2)
    rows_loop(2, EXT1 - 2, middle.set_total, 4)
    middle.first_relax(spare1, f1, 2, 18)
    middle.relax(x1, spare1, f1, 3, 17)
    middle.restrict(f2, x1, f1, 2, 8)
    ups, downs = [], []
    for target, first, outer in ((ups, 2, 2), (downs, 4, 6)):
        for j in range(4):
            for k in range(SECTIONS):
                target.append(f2[first + j, k])
        for j in range(2):
            target.extend((gy2[outer + j, 0], below2[outer + j, 0], cap2[outer + j, 0]))
        for j in range(3):
            target.append(gx2[outer + j, 0])
    for n, (up, down) in enumerate(zip(ups, downs)):
        go0[n] = jnp.where(far.odd, down, up)
        go1[n] = jnp.where(far.odd, up, down)


def middle_kernel(place, *refs):
    (gx0, gy0, via0, below0, cap0, total0, weights0, f0, x0) = refs[0:9]
    (gx1, gy1, via1, below1, cap1, total1, weights1, f1, x1) = refs[9:18]
    (gx2, gy2, below2, cap2, f2, got0, got1) = refs[18:25]
    got = Sides(place, 2, got0, got1)
    (x0_out, f1_out, go_side, gxw, gyw, viaw, beloww, weightsw) = refs[25:33]
    (capw, totalw, fw, xa, xb, ya, yb, za, f1_own) = refs[33:42]
    fine = Level(4, gx0, gy0, via0, below0, cap0, total0, weights0)
    middle = Level(2, gx1, gy1, via1, below1, cap1, total1, weights1)
    coarse = Level(1, gxw, gyw, viaw, beloww, capw, totalw, weightsw)
    for j in range(4):
        for k in range(SECTIONS):
            fw[j, k] = got.lower(5 * j + k)
            fw[10 + j, k] = got.upper(5 * j + k)
    for j in range(2):
        for near, source in ((j, got.lower), (12 + j, got.upper)):
            gyw[near, 0] = source(20 + 3 * j)
            gyw[near, 1] = from_right(source(20 + 3 * j))
            beloww[near, 0] = source(21 + 3 * j)
            capw[near, 0] = source(22 + 3 * j)
    for j in range(3):
        gxw[j, 0] = got.lower(26 + j)
        gxw[12 + j, 0] = got.upper(26 + j)
    for j in range(6):
        for k in range(SECTIONS):
            fw[4 + j, k] = f2[2 + j, k]
    for j in range(10):
        gyw[2 + j, 0] = gy2[j, 0]
        gyw[2 + j, 1] = gy2[j, 1]
        beloww[2 + j, 0] = below2[j, 0]
        capw[2 + j, 0] = cap2[j, 0]
    for j in range(1, 10):
        gxw[2 + j, 0] = gx2[j, 0]
    rows_loop(0, WIDE2, coarse.set_total)
    coarse.first_relax(xa, fw, 0, 14)
    coarse.relax(xb, xa, fw, 1, 13)
    coarse.relax(xa, xb, fw, 2, 12)
    coarse.relax(xb, xa, fw, 3, 11)
    middle.correct(ya, x1, xb, 3, 17, 2)
    middle.relax(yb, ya, f1, 4, 16)
    middle.relax(ya, yb, f1, 5, 15)
    fine.correct(x0_out, x0, ya, 10, 30)
    fine.relax(za, x0_out, f0, 11, 29)
    fine.relax(x0_out, za, f0, 12, 28)
    fine.relax(za, x0_out, f0, 13, 27)
    fine.relax(x0_out, za, f0, 14, 26)
    fine.restrict(f1_own, x0_out, f0, 8, 12, -8)
    for j in range(4):
        for n in range(10):
            f1_out[10 * j + n] = f1_own[j, n]
    for j in range(10):
        packs = packed([f1_own[n // 10, n % 10] for n in range(4 * j, 4 * j + 4)])
        for t in range(3):
            go_side[3 * j + t] = packs[t]


def lower_kernel(place, *refs):
    (gx1, gy1, via1, below1, cap1, total1, weights1) = refs[0:7]
    own, got0, got1 = refs[7:10]
    got = Sides(place, 1, got0, got1)
    f1, x1, f2_out = refs[10:13]
    (xa,) = refs[13:14]
    middle = Level(2, gx1, gy1, via1, below1, cap1, total1, weights1)
    for j in range(10):
        for first, source in ((4, got.lower), (12, got.upper)):
            values = unpacked([source(3 * j + t) for t in range(3)])
            for t in range(4):
                n = 4 * j + t
                f1[first + n // 10, n % 10] = values[t]
        for n in range(4 * j, 4 * j + 4):
            f1[8 + n // 10, n % 10] = own[n]
    middle.first_relax(xa, f1, 4, 16)
    middle.relax(x1, xa, f1, 5, 15)
    middle.restrict(f2_out, x1, f1, 3, 7, -3)


def finish_kernel(place, *refs):
    (gx0, gy0, via0, below0, weights0, f0, x0) = refs[0:7]
    (gx1, gy1, via1, below1, weights1, f1, x1) = refs[7:14]
    (gxw, gyw, viaw, beloww, weightsw, own, got0, got1, voltage) = refs[14:23]
    got = Sides(place, 2, got0, got1)
    sections, next_voltage = refs[23:25]
    fw, xa, xb, ya, yb, za, zb, mixed, turn = refs[25:34]
    fine = Level(4, gx0, gy0, via0, below0, None, None, weights0)
    middle = Level(2, gx1, gy1, via1, below1, None, None, weights1)
    coarse = Level(1, gxw, gyw, viaw, beloww, None, None, weightsw)
    for j in range(4):
        for k in range(SECTIONS):
            fw[1 + j, k] = got.lower(j, k)
            fw[5 + j, k] = own[j, k]
            fw[9 + j, k] = got.upper(j, k)
    block = place[0]
    for k in range(SECTIONS):
        fw[4, k] = jnp.where(block == 1, got.lower(1, k), fw[4, k])
        fw[9, k] = jnp.where(block == 30, got.upper(2, k), fw[9, k])
    coarse.first_relax(xa, fw, 1, 13)
    coarse.relax(xb, xa, fw, 2, 12)
    coarse.relax(xa, xb, fw, 3, 11)
    coarse.relax(xb, xa, fw, 4, 10)
    middle.correct(ya, x1, xb, 5, 15, 2)
    middle.relax(yb, ya, f1, 6, 14)
    middle.relax(ya, yb, f1, 7, 13)
    fine.correct(za, x0, ya, 14, 26)
    fine.relax(zb, za, f0, 15, 25)
    fine.relax(za, zb, f0, 16, 24)

    def mix(row):
        for p in range(4):
            values = [za[16 + row, 4 * k + p] for k in range(SECTIONS)]
            for j in range(SECTIONS):
                total = TRANSFORM[j][0] * values[0]
                for k in range(1, SECTIONS):
                    total = total + TRANSFORM[j][k] * values[k]
                mixed[p, 8 * j + row] = total

    rows_loop(0, 8, mix)
    result = None
    for p in range(4):
        lane = lax.broadcasted_iota(jnp.int32, (LANES, 256), 0)
        column = lax.broadcasted_iota(jnp.int32, (LANES, 256), 1)
        chooser = jnp.where((lane < 64) & (column == 4 * lane + p), 1.0, 0.0).astype(jnp.bfloat16)
        part = selected(mixed[p].reshape(320, LANES), chooser)
        result = part if result is None else result + part
    for j in range(SECTIONS):
        for row in range(8):
            at = (8 * j + row) * 8
            for h in range(2):
                turn[j, h, pl.ds(row, 8, stride=8), :] = result[
                    at : at + 8, h * 128 : h * 128 + 128
                ]
        for h in range(2):
            sections[j, :, h * 128 : h * 128 + 128] = turn[j, h]
    next_voltage[...] = voltage[...] + sections[SECTIONS - 1]


VMEM = pltpu.MemorySpace.VMEM


def vregs(*shape):
    return pltpu.VMEM(shape + (LAYERS, LANES), jnp.float32)


def scratch(*shape):
    return pltpu.VMEM(shape + (LAYERS, LANES), jnp.float32)


def call(kernel, inputs, outs, scratches=(), outside=False, aliases=()):
    space = pltpu.MemorySpace.HBM if outside else VMEM
    inputs = [pltpu.with_memory_space_constraint(value, space) for value in inputs]
    return pl.pallas_call(
        kernel,
        out_shape=outs,
        in_specs=[pl.BlockSpec(memory_space=space)] * len(inputs),
        out_specs=[pl.BlockSpec(memory_space=VMEM)] * len(outs),
        scratch_shapes=list(scratches),
        input_output_aliases=dict(aliases),
        compiler_params=pltpu.CompilerParams(vmem_limit_bytes=12 * 2**20),
    )(*inputs)


def turned(value, axis, count, shift):
    return lax.ppermute(value, axis, [(i, (i + shift) % count) for i in range(count)])


def paired(value, distance):
    rows = lax.axis_size("section") * lax.axis_size("gx")
    columns = lax.axis_size("gy")
    values = value if isinstance(value, tuple) else (value, value)
    result = [None, None]
    for which in (1, 0):
        pairs = []
        for row in range(rows):
            up = (row // distance) % 2 == which
            other = row + distance if up else row - distance
            for column in range(columns):
                target = (other, column)
                if not 0 <= other < rows:
                    target = (row, column ^ 1) if distance == 1 else (row ^ 1, column)
                pairs.append((row * columns + column, target[0] * columns + target[1]))
        result[which] = lax.ppermute(values[which], ("section", "gx", "gy"), pairs)
    return result


def local(voltage, capacity, node_class, via_sites, ball_sites, load_type, load_table):
    columns = lax.axis_size("gy")
    volts = voltage.reshape(64, 256)
    own, left, right = call(
        gather_kernel,
        (
            volts,
            capacity.reshape(64, 256),
            node_class.reshape(64, 256),
            via_sites.reshape(56, 256),
            ball_sites,
            load_type,
        ),
        [
            vregs(33, 2),
            pltpu.VMEM((264, 64), jnp.float32),
            pltpu.VMEM((264, 64), jnp.float32),
        ],
        [
            pltpu.VMEM((4, 2, 64, LANES), jnp.float32),
            pltpu.VMEM((64, 256), jnp.float32),
            pltpu.VMEM((64, 256), jnp.float32),
            pltpu.VMEM((64, 256), jnp.int32),
            pltpu.VMEM((56, 256), jnp.int32),
            pltpu.VMEM((8, 256), jnp.int32),
            pltpu.VMEM((8, 256), jnp.int32),
            pltpu.SemaphoreType.DMA((6,)),
            pltpu.VMEM((264, 256), jnp.float32),
        ],
        outside=True,
    )
    mixed_table = jnp.einsum(
        "tk,jk->tj", load_table, jnp.asarray(INVERSE, jnp.float32), precision=lax.Precision.HIGHEST
    )
    row_block = lax.axis_index("section") * lax.axis_size("gx") + lax.axis_index("gx")
    place = jnp.stack(
        [
            jnp.full((LAYERS, LANES), number, jnp.int32)
            for number in (row_block, lax.axis_index("gy"))
        ]
    )
    mixed_table = jnp.broadcast_to(
        mixed_table.reshape(LOADS * SECTIONS, 1, 1), (LOADS * SECTIONS, LAYERS, LANES)
    )
    near = paired(own, 1)
    from_lower = turned(right, "gy", columns, 1)
    from_upper = turned(left, "gy", columns, -1)
    (whole,) = call(rim_kernel, (own, from_lower, from_upper), [vregs(33, 3)])
    far = paired(whole, 2)
    go_right, go_left = call(edge_kernel, (place, *near), [vregs(33), vregs(33)])
    edge_left = turned(go_right, "gy", columns, 1)
    edge_right = turned(go_left, "gy", columns, -1)
    state_shapes = [
        vregs(EXT0, 4),
        vregs(EXT0, 5),
        vregs(EXT0, 4),
        vregs(EXT0, 4),
        vregs(EXT0, 4),
        vregs(EXT0, 4),
        vregs(EXT0, 20),
        vregs(EXT0, 20),
        vregs(EXT0, 20),
        vregs(EXT1, 2),
        vregs(EXT0, 4),
        vregs(EXT0, 4),
        pltpu.VMEM((EXT0 * TILES, LANES), jnp.float32),
        vregs(EXT0, 20),
    ]
    state = call(own_kernel, (place, mixed_table, whole), state_shapes)
    state = call(
        near_kernel,
        (place, mixed_table, *near, edge_left, edge_right, *state),
        [*state_shapes, vregs(EXT1, 10)],
        aliases=[(6 + n, n) for n in range(STATE)],
    )
    state = call(
        setup_kernel,
        (place, mixed_table, *far, *state),
        [
            *state_shapes,
            vregs(EXT1, 10),
            vregs(EXT1, 2),
            vregs(EXT1, 3),
            vregs(EXT1, 2),
            vregs(EXT1, 2),
            vregs(EXT1, 2),
            vregs(EXT1, 10),
            vregs(EXT1, 10),
            vregs(EXT2, 1),
            vregs(EXT2, 2),
            vregs(EXT2, 1),
            vregs(EXT2, 1),
            vregs(EXT2, 5),
            vregs(29),
            vregs(29),
        ],
        [scratch(EXT1, 10)],
        aliases=[(4 + n, n) for n in range(STATE + 1)],
    )
    fine, below1, f1 = state[:9], state[9], state[STATE]
    gx1, gy1, via1, cap1, total1, weights1, x1 = state[STATE + 1 : STATE + 8]
    middle = (gx1, gy1, via1, below1, cap1, total1, weights1, f1, x1)
    coarse = state[STATE + 8 : STATE + 13]
    got = paired(tuple(state[STATE + 13 :]), 2)
    x0, f1_own, go_side, gxw, gyw, viaw, beloww, weightsw = call(
        middle_kernel,
        (place, *fine, *middle, *coarse, *got),
        [
            vregs(EXT0, 20),
            vregs(40),
            vregs(30),
            vregs(WIDE2 + 1, 1),
            vregs(WIDE2, 2),
            vregs(WIDE2, 1),
            vregs(WIDE2, 1),
            vregs(WIDE2, 5),
        ],
        [
            scratch(WIDE2, 1),
            scratch(WIDE2, 1),
            scratch(WIDE2, 5),
            scratch(WIDE2, 5),
            scratch(WIDE2, 5),
            scratch(EXT1, 10),
            scratch(EXT1, 10),
            scratch(EXT0, 20),
            scratch(4, 10),
        ],
    )
    got = paired(go_side, 1)
    f1, x1, f2_own = call(
        lower_kernel,
        (place, *middle[:7], f1_own, *got),
        [vregs(EXT1, 10), vregs(EXT1, 10), vregs(4, 5)],
        [scratch(EXT1, 10)],
    )
    got = paired(f2_own, 2)
    sections, next_voltage = call(
        finish_kernel,
        (
            place,
            *fine[:4],
            *fine[6:8],
            x0,
            *middle[:4],
            middle[6],
            f1,
            x1,
            gxw,
            gyw,
            viaw,
            beloww,
            weightsw,
            f2_own,
            *got,
            volts,
        ),
        [
            jax.ShapeDtypeStruct((SECTIONS, 64, 256), jnp.float32),
            jax.ShapeDtypeStruct((64, 256), jnp.float32),
        ],
        [
            scratch(WIDE2, 5),
            scratch(WIDE2, 5),
            scratch(WIDE2, 5),
            scratch(EXT1, 10),
            scratch(EXT1, 10),
            scratch(EXT0, 20),
            scratch(EXT0, 20),
            scratch(4, 40),
            pltpu.VMEM((SECTIONS, 2, 64, LANES), jnp.float32),
        ],
    )
    return sections.reshape((SECTIONS,) + voltage.shape), next_voltage.reshape(voltage.shape)


def solution(mesh):
    return jax.shard_map(
        local,
        mesh=mesh,
        in_specs=(
            P(None, ("section", "gx"), "gy"),
            P(None, ("section", "gx"), "gy"),
            P(None, ("section", "gx"), "gy"),
            P(None, ("section", "gx"), "gy"),
            P(("section", "gx"), "gy"),
            P(("section", "gx"), "gy"),
            P(),
        ),
        out_specs=(P(None, None, ("section", "gx"), "gy"), P(None, ("section", "gx"), "gy")),
        check_vma=False,
    )
```

```python
import jax
import jax.numpy as jnp
from jax import lax
from jax.experimental import pallas as pl
from jax.experimental.pallas import tpu as pltpu
from jax.sharding import PartitionSpec as P

SECTIONS = 5
LOADS = 16
LAYERS = 8
LANES = 128
EXT0 = 40
EXT1 = 20
EXT2 = 10
WIDE2 = 14
TILES = 160

node_table = (0.35, 0.55, 0.8, 1.1, 1.5, 2.0, 2.7, 3.6)
via_conductance = 2.5
ball_conductance = 4.0
damping = 0.8
slab_partner = (0, 2, 1, 4, 3)


def pair_times(first, second):
    return (
        first[0] * second[0] - first[1] * second[1],
        first[0] * second[1] + first[1] * second[0],
    )


def pair_over(first, second):
    divisor = second[0] * second[0] + second[1] * second[1]
    return (
        (first[0] * second[0] + first[1] * second[1]) / divisor,
        (first[1] * second[0] - first[0] * second[1]) / divisor,
    )


def pair_minus(first, second):
    return (first[0] - second[0], first[1] - second[1])


def poly_value(coeffs, point):
    total = (0.0, 0.0)
    for c in reversed(coeffs):
        total = pair_times(total, point)
        total = (total[0] + c, total[1])
    return total


def poly_product(first, second):
    result = [0.0] * (len(first) + len(second) - 1)
    for i in range(len(first)):
        for j in range(len(second)):
            result[i + j] = result[i + j] + first[i] * second[j]
    return result


def poly_roots(coeffs):
    leading = coeffs[-1]
    scaled = [c / leading for c in coeffs]
    degree = len(coeffs) - 1
    guesses = []
    current = (1.0, 0.0)
    for k in range(degree):
        guesses.append(current)
        current = pair_times(current, (0.4, 0.9))
    for repeat_index in range(800):
        for k in range(degree):
            divisor = (1.0, 0.0)
            for j in range(degree):
                if j != k:
                    divisor = pair_times(divisor, pair_minus(guesses[k], guesses[j]))
            guesses[k] = pair_minus(guesses[k], pair_over(poly_value(scaled, guesses[k]), divisor))
    return guesses


def matrix_product(first, second):
    return [
        [
            sum((first[i][k] * second[k][j] for k in range(len(second))))
            for j in range(len(second[0]))
        ]
        for i in range(len(first))
    ]


def matrix_inverse(matrix):
    order = len(matrix)
    work = [list(matrix[i]) + [1.0 if i == j else 0.0 for j in range(order)] for i in range(order)]
    for column in range(order):
        pivot = column
        for i in range(column + 1, order):
            if abs(work[i][column]) > abs(work[pivot][column]):
                pivot = i
        work[column], work[pivot] = (work[pivot], work[column])
        factor = work[column][column]
        work[column] = [entry / factor for entry in work[column]]
        for i in range(order):
            if i != column:
                scale_row = work[i][column]
                work[i] = [work[i][j] - scale_row * work[column][j] for j in range(2 * order)]
    return [row[order:] for row in work]


def eigen_vector(matrix, value):
    order = len(matrix)
    size_inner = order - 1
    system = []
    for i in range(size_inner):
        row = []
        for j in range(order):
            entry = (matrix[i][j], 0.0)
            if i == j:
                entry = pair_minus(entry, value)
            row.append(entry)
        row[order - 1] = (-row[order - 1][0], -row[order - 1][1])
        system.append(row)
    for column in range(size_inner):
        pivot = column
        for i in range(column + 1, size_inner):
            left_size = system[i][column][0] ** 2 + system[i][column][1] ** 2
            right_size = system[pivot][column][0] ** 2 + system[pivot][column][1] ** 2
            if left_size > right_size:
                pivot = i
        system[column], system[pivot] = (system[pivot], system[column])
        for i in range(size_inner):
            if i != column:
                factor = pair_over(system[i][column], system[column][column])
                system[i] = [
                    pair_minus(system[i][j], pair_times(factor, system[column][j]))
                    for j in range(order)
                ]
    vector = [pair_over(system[i][order - 1], system[i][i]) for i in range(size_inner)]
    vector.append((1.0, 0.0))
    return vector


def radau_tables():
    section_count = 5
    generator = [1.0]
    for k in range(section_count - 1):
        generator = poly_product(generator, [0.0, 1.0])
    for k in range(section_count):
        generator = poly_product(generator, [-1.0, 1.0])
    for k in range(section_count - 1):
        generator = [j * generator[j] for j in range(1, len(generator))]
    abscissae = sorted((root[0] for root in poly_roots(generator)))
    vander = [[abscissae[i] ** j for j in range(section_count)] for i in range(section_count)]
    integrals = [
        [abscissae[i] ** (j + 1) / (j + 1) for j in range(section_count)]
        for i in range(section_count)
    ]
    butcher = matrix_product(integrals, matrix_inverse(vander))
    inverse = matrix_inverse(butcher)
    coeffs = [0.0] * (section_count + 1)
    coeffs[section_count] = 1.0
    current = [[0.0] * section_count for _ in range(section_count)]
    for k in range(1, section_count + 1):
        current = matrix_product(inverse, current)
        for i in range(section_count):
            current[i][i] = current[i][i] + coeffs[section_count - k + 1]
        applied = matrix_product(inverse, current)
        coeffs[section_count - k] = -sum((applied[i][i] for i in range(section_count))) / k
    eigen_values = poly_roots(coeffs)
    real_pick = 0
    for k in range(section_count):
        if abs(eigen_values[k][1]) < abs(eigen_values[real_pick][1]):
            real_pick = k
    upper_half = [k for k in range(section_count) if eigen_values[k][1] > 1e-09]
    upper_half = sorted(upper_half, key=lambda k: -eigen_values[k][0])
    columns = [[entry[0] for entry in eigen_vector(inverse, (eigen_values[real_pick][0], 0.0))]]
    for k in upper_half:
        vector = eigen_vector(inverse, eigen_values[k])
        columns.append([entry[0] for entry in vector])
        columns.append([entry[1] for entry in vector])
    transform = [[columns[j][i] for j in range(section_count)] for i in range(section_count)]
    inverse_transform = matrix_inverse(transform)
    blocks = matrix_product(matrix_product(inverse_transform, inverse), transform)
    diagonal = [blocks[k][k] for k in range(section_count)]
    coupling = [
        blocks[k][slab_partner[k]] if slab_partner[k] != k else 0.0 for k in range(section_count)
    ]
    return (transform, inverse_transform, diagonal, coupling)


TRANSFORM, INVERSE, DIAGONAL, COUPLING = radau_tables()
SHIFTS = (
    DIAGONAL[0],
    0.5 * (DIAGONAL[1] + DIAGONAL[2]),
    0.5 * (DIAGONAL[3] + DIAGONAL[4]),
)
COUPLES = (0.5 * (COUPLING[1] - COUPLING[2]), 0.5 * (COUPLING[3] - COUPLING[4]))
ROW_SUMS = tuple(sum(row) for row in INVERSE)


def from_right(value):
    return pltpu.roll(value, LANES - 1, 1)


def from_left(value):
    return pltpu.roll(value, 1, 1)


def from_above(value):
    return pltpu.roll(value, LAYERS - 1, 0)


def from_below(value):
    return pltpu.roll(value, 1, 0)


def lane_index():
    return lax.broadcasted_iota(jnp.int32, (LAYERS, LANES), 1)


def layer_index():
    return lax.broadcasted_iota(jnp.int32, (LAYERS, LANES), 0)


def spread(first, second, rim):
    own = lane_index() < 64
    inner = (first, pltpu.roll(first, 64, 1), second, pltpu.roll(second, 64, 1))
    outer = (rim, pltpu.roll(rim, 96, 1), pltpu.roll(rim, 64, 1), pltpu.roll(rim, 32, 1))
    return [jnp.where(own, near, far) for near, far in zip(inner, outer)]


def packed(values):
    lane = lane_index()
    result = []
    for q in range(5):
        carrier = values[q]
        for e in range(3):
            spare, at = values[5 + e], 72 + 16 * e
            if q < 4:
                part = pltpu.roll(spare, at - 16 * q, 1)
            else:
                part = jnp.where(
                    lane < at + 8,
                    pltpu.roll(spare, at - 64, 1),
                    pltpu.roll(spare, (at + 8 - 120) % LANES, 1),
                )
            carrier = jnp.where((lane >= at) & (lane < at + 16), part, carrier)
        result.append(carrier)
    return result


def unpacked(packs):
    lane = lane_index()
    result = list(packs)
    for e in range(3):
        at = 72 + 16 * e
        value = jnp.where(
            lane < 96,
            pltpu.roll(packs[4], (64 - at) % LANES, 1),
            pltpu.roll(packs[4], (120 - at - 8) % LANES, 1),
        )
        for q in range(4):
            part = pltpu.roll(packs[q], (16 * q - at) % LANES, 1)
            value = jnp.where((lane >= 16 * q) & (lane < 16 * q + 16), part, value)
        result.append(value)
    return result


def rows_loop(low, high, body, unroll=2):
    steps = (high - low) // unroll

    def step(n, carry):
        for j in range(unroll):
            body(low + n * unroll + j)
        return carry

    if steps > 1:
        lax.fori_loop(0, steps, step, 0)
    elif steps == 1:
        step(0, 0)
    for i in range(low + steps * unroll, high):
        body(i)


class Sides:
    def __init__(self, place, distance, first, second):
        self.odd = (place[0] & distance) != 0
        self.first, self.second = first, second

    def lower(self, *at):
        return jnp.where(self.odd, self.first[at], self.second[at])

    def upper(self, *at):
        return jnp.where(self.odd, self.second[at], self.first[at])


class Level:
    def __init__(self, phases, gx, gy, via, below, cap, total, weights):
        self.phases = phases
        self.unroll = 8 // phases
        self.gx, self.gy = gx, gy
        self.via, self.below = via, below
        self.cap, self.total, self.weights = cap, total, weights

    def sides(self, centre, p):
        right = centre[p + 1] if p < self.phases - 1 else from_right(centre[0])
        left = centre[p - 1] if p > 0 else from_left(centre[self.phases - 1])
        return right, left

    def inflow(self, coeffs, centre, p, upper, lower):
        gx_lower, gx_upper, gy_left, gy_right, via, below = coeffs
        right, left = self.sides(centre, p)
        here = centre[p]
        return (
            (gx_upper * upper + gx_lower * lower)
            + (gy_right * right + gy_left * left)
            + (via * from_above(here) + below * from_below(here))
        )

    def coeffs(self, i, p):
        return (
            self.gx[i, p],
            self.gx[i + 1, p],
            self.gy[i, p],
            self.gy[i, p + 1],
            self.via[i, p],
            self.below[i, p],
        )

    def set_total(self, i):
        bottom = layer_index() == 0
        for p in range(self.phases):
            grounded = self.below[i, p]
            below = jnp.where(bottom, 0.0, grounded)
            via = from_above(below)
            total = (
                (self.gx[i, p] + self.gx[i + 1, p])
                + (self.gy[i, p] + self.gy[i, p + 1])
                + (via + grounded)
            )
            self.below[i, p] = below
            self.via[i, p] = via
            self.total[i, p] = total
            cap = self.cap[i, p]
            self.weights[i, p * 5] = damping / (SHIFTS[0] * cap + total)
            for s in range(2):
                direct = SHIFTS[s + 1] * cap + total
                cross = COUPLES[s] * cap
                scale = damping / (direct * direct + cross * cross)
                self.weights[i, p * 5 + 1 + 2 * s] = direct * scale
                self.weights[i, p * 5 + 2 + 2 * s] = -(cross * scale)

    def weighted(self, i, p, values):
        w = [self.weights[i, p * 5 + m] for m in range(5)]
        out = [w[0] * values[0]]
        for s in range(2):
            first, second = values[1 + 2 * s], values[2 + 2 * s]
            out.append(w[1 + 2 * s] * first + w[2 + 2 * s] * second)
            out.append(w[1 + 2 * s] * second - w[2 + 2 * s] * first)
        return out

    def first_relax(self, target, source, low, high):
        def body(i):
            for p in range(self.phases):
                values = [source[i, k * self.phases + p] for k in range(SECTIONS)]
                for k, value in enumerate(self.weighted(i, p, values)):
                    target[i, k * self.phases + p] = value

        rows_loop(low, high, body, self.unroll)

    def gathered(self, iterate, source, i):
        count = self.phases
        centres = [[iterate[i, k * count + p] for p in range(count)] for k in range(SECTIONS)]
        sums = []
        for p in range(count):
            coeffs = self.coeffs(i, p)
            sums.append(
                [
                    source[i, k * count + p]
                    + self.inflow(
                        coeffs,
                        centres[k],
                        p,
                        iterate[i + 1, k * count + p],
                        iterate[i - 1, k * count + p],
                    )
                    for k in range(SECTIONS)
                ]
            )
        return centres, sums

    def relax(self, target, iterate, source, low, high):
        count = self.phases

        def body(i):
            centres, sums = self.gathered(iterate, source, i)
            for p in range(count):
                for k, value in enumerate(self.weighted(i, p, sums[p])):
                    target[i, k * count + p] = (1.0 - damping) * centres[k][p] + value

        rows_loop(low, high, body, self.unroll)

    def residual(self, iterate, source, i):
        centres, sums = self.gathered(iterate, source, i)
        result = []
        for p in range(self.phases):
            cap, total = self.cap[i, p], self.total[i, p]
            x = [centres[k][p] for k in range(SECTIONS)]
            out = [sums[p][0] - (SHIFTS[0] * cap + total) * x[0]]
            for s in range(2):
                direct = SHIFTS[s + 1] * cap + total
                cross = COUPLES[s] * cap
                a, b = 1 + 2 * s, 2 + 2 * s
                out.append(sums[p][a] - (direct * x[a] + cross * x[b]))
                out.append(sums[p][b] - (direct * x[b] - cross * x[a]))
            result.append(out)
        return result

    def restrict(self, target, iterate, source, low, high, shift=0):
        half = self.phases // 2

        def body(row):
            one = self.residual(iterate, source, 2 * row)
            two = self.residual(iterate, source, 2 * row + 1)
            for k in range(SECTIONS):
                for q in range(half):
                    target[row + shift, k * half + q] = (one[2 * q][k] + one[2 * q + 1][k]) + (
                        two[2 * q][k] + two[2 * q + 1][k]
                    )

        rows_loop(low, high, body, self.unroll // 2)

    def correct(self, target, iterate, coarse, low, high, shift=0):
        count, half = self.phases, self.phases // 2

        def body(i):
            row = lax.shift_right_logical(i, 1) + shift
            for k in range(SECTIONS):
                for q in range(half):
                    value = coarse[row, k * half + q]
                    for p in (2 * q, 2 * q + 1):
                        target[i, k * count + p] = iterate[i, k * count + p] + value

        rows_loop(low, high, body, self.unroll)


def coarsen(fine, coarse, rows):
    half = coarse.phases

    def body(row):
        for q in range(half):
            for ref_out, ref_in in ((coarse.cap, fine.cap),):
                ref_out[row, q] = (ref_in[2 * row, 2 * q] + ref_in[2 * row, 2 * q + 1]) + (
                    ref_in[2 * row + 1, 2 * q] + ref_in[2 * row + 1, 2 * q + 1]
                )
        for q in range(half + 1):
            coarse.gy[row, q] = fine.gy[2 * row, 2 * q] + fine.gy[2 * row + 1, 2 * q]

    rows_loop(0, rows, body, 4)

    def body_gx(row):
        for q in range(half):
            coarse.gx[row, q] = fine.gx[2 * row, 2 * q] + fine.gx[2 * row, 2 * q + 1]

    rows_loop(1, rows, body_gx, 4)


def sum_below(fine_below, coarse_below, phases, low, high):
    def body(row):
        for q in range(phases):
            coarse_below[row, q] = (
                fine_below[2 * row, 2 * q] + fine_below[2 * row, 2 * q + 1]
            ) + (fine_below[2 * row + 1, 2 * q] + fine_below[2 * row + 1, 2 * q + 1])

    rows_loop(low, high, body, 4)


def gather_kernel(*refs):
    own, left, right, work = refs[6:10]
    whole = refs[17]
    voltage, capacity, node_class, via, ball, load = refs[10:16]
    copies = [
        pltpu.make_async_copy(source, target, refs[16].at[n])
        for n, (source, target) in enumerate(zip(refs[:6], refs[10:16]))
    ]
    for copy in copies:
        copy.start()
    for copy in copies:
        copy.wait()
    classes = node_class[...]
    conduct = jnp.full(classes.shape, node_table[0], jnp.float32)
    for c in range(1, len(node_table)):
        conduct = jnp.where(classes == c, node_table[c], conduct)
    grounded = jnp.where(ball[...] == 1, ball_conductance, 0.0)
    upright = jnp.where(via[...] == 1, via_conductance, 0.0)
    for h in range(2):
        half = slice(h * 128, h * 128 + 128)
        work[0, h] = voltage[:, half]
        work[1, h] = capacity[:, half]
        work[2, h] = conduct[:, half]
        work[3, h, 0:8] = grounded[:, half]
        work[3, h, 8:64] = upright[:, half]
    for row in range(8):
        for a in range(4):
            at = (row * 4 + a) * 8
            for h in range(2):
                whole[at : at + 8, h * 128 : h * 128 + 128] = work[
                    a, h, pl.ds(row, 8, stride=8), :
                ]
    whole[256:264] = load[...].astype(jnp.float32)
    left[...] = whole[:, :64]
    right[...] = whole[:, 192:]
    column = lax.broadcasted_iota(jnp.int32, (256, 256), 0)
    slot = lax.broadcasted_iota(jnp.int32, (256, 256), 1)
    wanted = 4 * (slot % 64) + slot // 64
    result = selected(whole[...], jnp.where(column == wanted, 1.0, 0.0).astype(jnp.bfloat16))
    for n in range(33):
        for h in range(2):
            own[n, h] = result[8 * n : 8 * n + 8, 128 * h : 128 * h + 128]


def three_parts(value):
    high = value.astype(jnp.bfloat16)
    rest = value - high.astype(jnp.float32)
    middle = rest.astype(jnp.bfloat16)
    low = (rest - middle.astype(jnp.float32)).astype(jnp.bfloat16)
    return high, middle, low


def selected(value, chooser):
    high, middle, low = (
        jnp.dot(part, chooser, preferred_element_type=jnp.float32) for part in three_parts(value)
    )
    return high + (middle + low)


def rim_kernel(own, from_lower, from_upper, whole):
    column = lax.broadcasted_iota(jnp.int32, (64, LANES), 0)
    slot = lax.broadcasted_iota(jnp.int32, (64, LANES), 1)
    group, place = slot // 32, slot % 32
    below = (place >= 16) & (column == 4 * (place - 16) + (group + 1) % 4)
    above = (place < 16) & (column == 4 * place + (group + 2) % 4)
    result = selected(from_lower[...], jnp.where(below, 1.0, 0.0).astype(jnp.bfloat16))
    result = result + selected(
        from_upper[...], jnp.where(above, 1.0, 0.0).astype(jnp.bfloat16)
    )
    for n in range(33):
        whole[n, 2] = result[8 * n : 8 * n + 8]
        for h in range(2):
            whole[n, h] = own[n, h]


def edge_kernel(place, near0, near1, go_right, go_left):
    lane = lane_index()
    group = lane // 32
    late = lane % 32 >= 16
    near = Sides(place, 1, near0, near1)

    def chosen(one, two, three, four):
        return jnp.where(
            group < 2, jnp.where(group == 0, one, two), jnp.where(group == 2, three, four)
        )

    def body(n):
        rights, lefts = [], []
        for block in (near.lower, near.upper):
            first, second = block(n, 0), block(n, 1)
            first_far, first_near = pltpu.roll(first, 64, 1), pltpu.roll(first, 32, 1)
            second_far = pltpu.roll(second, 96, 1)
            rights.append(chosen(first_near, second, second_far, first_far))
            lefts.append(chosen(second, second_far, first_far, first_near))
        go_right[n] = jnp.where(late, rights[0], pltpu.roll(rights[1], 112, 1))
        go_left[n] = jnp.where(late, pltpu.roll(lefts[1], 16, 1), lefts[0])

    rows_loop(0, 33, body, 11)


def prepare(place, mixed_table, state, f1, blocks, gx_rows, total_rows, relax_rows, sum_rows):
    (gx0, gy0, via0, below0, cap0, total0, weights0, f0, x0) = state[:9]
    below1, volt, conduct, surface, spare = state[9:14]
    fine = Level(4, gx0, gy0, via0, below0, cap0, total0, weights0)
    row_block, column_block = place[0], place[1]
    lane = lane_index()
    edge = ((lane == 0) & (column_block == 0)) | ((lane == 64) & (column_block == 3))
    joined = jnp.where(edge, 0.0, 2.0)
    top = layer_index() == LAYERS - 1

    def series(near, far):
        return 2.0 * near * far / (near + far)

    def set_gy(i):
        here = [conduct[i, p] for p in range(4)]
        before = from_left(here[3])
        first = joined * before * here[0] / (before + here[0])
        gy0[i, 0] = first
        for p in range(1, 4):
            gy0[i, p] = series(here[p - 1], here[p])

    def turn_gy(i):
        gy0[i, 4] = from_right(gy0[i, 0])

    for b, block, rim in blocks:

        def place_row(s, block=block, rim=rim, b=b):
            for a, ref in enumerate((volt, cap0, conduct, below0)):
                n = 4 * s + a
                phases = spread(block(n, 0), block(n, 1), rim(n))
                for p in range(4):
                    ref[8 * b + s, p] = phases[p]

        rows_loop(0, 8, place_row, 4)
        loads = spread(block(32, 0), block(32, 1), rim(32))
        for p in range(4):
            values = [jnp.zeros((8, LANES), jnp.float32) for _ in range(SECTIONS)]
            for t in range(LOADS):
                chosen = loads[p] == float(t)
                values = [
                    jnp.where(chosen, mixed_table[SECTIONS * t + k], values[k]) for k in range(SECTIONS)
                ]
            for k in range(SECTIONS):
                at = 8 * b * TILES + (4 * k + p) * LAYERS + LAYERS - 1
                surface[pl.ds(at, 8, stride=TILES), :] = values[k]
        rows_loop(8 * b, 8 * b + 8, set_gy, 8)
        rows_loop(8 * b, 8 * b + 8, turn_gy, 8)
        sum_below(below0, below1, 2, 4 * b, 4 * b + 4)

    def set_gx(i):
        row = 8 * row_block - 16 + i
        twice = jnp.where((row == 0) | (row == 256), 0.0, 2.0)
        for p in range(4):
            near, far = conduct[i - 1, p], conduct[i, p]
            gx0[i, p] = twice * near * far / (near + far)

    def set_source(i):
        centre = [volt[i, p] for p in range(4)]
        for p in range(4):
            leak = total0[i, p] * centre[p] - fine.inflow(
                fine.coeffs(i, p), centre, p, volt[i + 1, p], volt[i - 1, p]
            )
            values = []
            for k in range(SECTIONS):
                at = pl.multiple_of(i * TILES + (4 * k + p) * LAYERS, LAYERS)
                drawn = surface[pl.ds(at, LAYERS), :]
                values.append(jnp.where(top, drawn, 0.0) - ROW_SUMS[k] * leak)
                f0[i, 4 * k + p] = values[k]
            for k, value in enumerate(fine.weighted(i, p, values)):
                spare[i, 4 * k + p] = value

    def set_row(i):
        fine.set_total(i)
        set_source(i)

    for low, high in gx_rows:
        rows_loop(low, high, set_gx, 4)
    for low, high in total_rows:
        rows_loop(low, high, set_row)
    for low, high in relax_rows:
        fine.relax(x0, spare, f0, low, high)
    for low, high in sum_rows:
        fine.restrict(f1, x0, f0, low, high)


STATE = 14


def own_kernel(place, mixed_table, whole, *refs):
    prepare(
        place,
        mixed_table,
        refs,
        None,
        ((2, lambda n, h: whole[n, h], lambda n: whole[n, 2]),),
        ((17, 24),),
        ((17, 23),),
        ((18, 22),),
        (),
    )


def near_kernel(place, mixed_table, near0, near1, edge_left, edge_right, *refs):
    refs = refs[STATE:]
    late = lane_index() % 32 >= 16
    near = Sides(place, 1, near0, near1)

    def rim_lower(n):
        return jnp.where(late, edge_left[n], edge_right[n])

    def rim_upper(n):
        return jnp.where(
            late, pltpu.roll(edge_left[n], 16, 1), pltpu.roll(edge_right[n], 112, 1)
        )

    prepare(
        place,
        mixed_table,
        refs[:STATE],
        refs[STATE],
        ((1, near.lower, rim_lower), (3, near.upper, rim_upper)),
        ((9, 17), (24, 32)),
        ((9, 17), (23, 31)),
        ((10, 18), (22, 30)),
        ((6, 14),),
    )


def setup_kernel(place, mixed_table, far0, far1, *refs):
    refs = refs[STATE + 1 :]
    state, f1 = refs[:STATE], refs[STATE]
    gx1, gy1, via1, cap1, total1, weights1, x1 = refs[STATE + 1 : STATE + 8]
    gx2, gy2, below2, cap2, f2, go1, go0, spare1 = refs[STATE + 8 :]
    far = Sides(place, 2, far0, far1)
    below1 = state[9]
    prepare(
        place,
        mixed_table,
        state,
        f1,
        (
            (0, far.lower, lambda n: far.lower(n, 2)),
            (4, far.upper, lambda n: far.upper(n, 2)),
        ),
        ((2, 9), (32, 39)),
        ((2, 9), (31, 38)),
        ((3, 10), (30, 37)),
        ((2, 6), (14, 18)),
    )
    fine = Level(4, *state[:7])
    middle = Level(2, gx1, gy1, via1, below1, cap1, total1, weights1)
    coarse = Level(1, gx2, gy2, None, below2, cap2, None, None)
    coarsen(fine, middle, EXT1)
    coarsen(middle, coarse, EXT2)
    sum_below(below1, below2, 1, 0, EXT2)
    rows_loop(2, EXT1 - 2, middle.set_total, 4)
    middle.first_relax(spare1, f1, 2, 18)
    middle.relax(x1, spare1, f1, 3, 17)
    middle.restrict(f2, x1, f1, 2, 8)
    ups, downs = [], []
    for target, first, outer in ((ups, 2, 2), (downs, 4, 6)):
        for j in range(4):
            for k in range(SECTIONS):
                target.append(f2[first + j, k])
        for j in range(2):
            target.extend((gy2[outer + j, 0], below2[outer + j, 0], cap2[outer + j, 0]))
        for j in range(3):
            target.append(gx2[outer + j, 0])
    for n, (up, down) in enumerate(zip(ups, downs)):
        go0[n] = jnp.where(far.odd, down, up)
        go1[n] = jnp.where(far.odd, up, down)


def middle_kernel(place, *refs):
    (gx0, gy0, via0, below0, cap0, total0, weights0, f0, x0) = refs[0:9]
    (gx1, gy1, via1, below1, cap1, total1, weights1, f1, x1) = refs[9:18]
    (gx2, gy2, below2, cap2, f2, got1, got0) = refs[18:25]
    got = Sides(place, 2, got0, got1)
    (x0_out, f1_out, go_side, gxw, gyw, viaw, beloww, weightsw) = refs[25:33]
    (capw, totalw, fw, xa, xb, ya, yb, za, f1_own) = refs[33:42]
    fine = Level(4, gx0, gy0, via0, below0, cap0, total0, weights0)
    middle = Level(2, gx1, gy1, via1, below1, cap1, total1, weights1)
    coarse = Level(1, gxw, gyw, viaw, beloww, capw, totalw, weightsw)
    for j in range(4):
        for k in range(SECTIONS):
            fw[j, k] = got.lower(5 * j + k)
            fw[10 + j, k] = got.upper(5 * j + k)
    for j in range(2):
        for near, source in ((j, got.lower), (12 + j, got.upper)):
            gyw[near, 0] = source(20 + 3 * j)
            gyw[near, 1] = from_right(source(20 + 3 * j))
            beloww[near, 0] = source(21 + 3 * j)
            capw[near, 0] = source(22 + 3 * j)
    for j in range(3):
        gxw[j, 0] = got.lower(26 + j)
        gxw[12 + j, 0] = got.upper(26 + j)
    for j in range(6):
        for k in range(SECTIONS):
            fw[4 + j, k] = f2[2 + j, k]
    for j in range(10):
        gyw[2 + j, 0] = gy2[j, 0]
        gyw[2 + j, 1] = gy2[j, 1]
        beloww[2 + j, 0] = below2[j, 0]
        capw[2 + j, 0] = cap2[j, 0]
    for j in range(1, 10):
        gxw[2 + j, 0] = gx2[j, 0]
    rows_loop(0, WIDE2, coarse.set_total, 7)
    coarse.first_relax(xa, fw, 0, 14)
    coarse.relax(xb, xa, fw, 1, 13)
    coarse.relax(xa, xb, fw, 2, 12)
    coarse.relax(xb, xa, fw, 3, 11)
    middle.correct(ya, x1, xb, 3, 17, 2)
    middle.relax(yb, ya, f1, 4, 16)
    middle.relax(ya, yb, f1, 5, 15)
    fine.correct(x0_out, x0, ya, 10, 30)
    fine.relax(za, x0_out, f0, 11, 29)
    fine.relax(x0_out, za, f0, 12, 28)
    fine.relax(za, x0_out, f0, 13, 27)
    fine.relax(x0_out, za, f0, 14, 26)
    fine.restrict(f1_own, x0_out, f0, 8, 12, -8)
    for j in range(4):
        for n in range(10):
            f1_out[10 * j + n] = f1_own[j, n]
    for j in range(5):
        packs = packed([f1_own[n // 10, n % 10] for n in range(8 * j, 8 * j + 8)])
        for t in range(5):
            go_side[5 * j + t] = packs[t]


def lower_kernel(place, *refs):
    (gx1, gy1, via1, below1, cap1, total1, weights1) = refs[0:7]
    own, got0, got1 = refs[7:10]
    got = Sides(place, 1, got0, got1)
    f1, x1, f2_out = refs[10:13]
    (xa,) = refs[13:14]
    middle = Level(2, gx1, gy1, via1, below1, cap1, total1, weights1)
    for j in range(5):
        for first, source in ((4, got.lower), (12, got.upper)):
            values = unpacked([source(5 * j + t) for t in range(5)])
            for t in range(8):
                n = 8 * j + t
                f1[first + n // 10, n % 10] = values[t]
        for n in range(8 * j, 8 * j + 8):
            f1[8 + n // 10, n % 10] = own[n]
    middle.first_relax(xa, f1, 4, 16)
    middle.relax(x1, xa, f1, 5, 15)
    middle.restrict(f2_out, x1, f1, 3, 7, -3)


def finish_kernel(place, *refs):
    (gx0, gy0, via0, below0, weights0, f0, x0) = refs[0:7]
    (gx1, gy1, via1, below1, weights1, f1, x1) = refs[7:14]
    (gxw, gyw, viaw, beloww, weightsw, own, got0, got1, voltage) = refs[14:23]
    got = Sides(place, 2, got0, got1)
    sections, next_voltage = refs[23:25]
    fw, xa, xb, ya, yb, za, zb, mixed, turn, after, done = refs[25:36]
    fine = Level(4, gx0, gy0, via0, below0, None, None, weights0)
    middle = Level(2, gx1, gy1, via1, below1, None, None, weights1)
    coarse = Level(1, gxw, gyw, viaw, beloww, None, None, weightsw)
    for j in range(4):
        for k in range(SECTIONS):
            fw[1 + j, k] = got.lower(j, k)
            fw[5 + j, k] = own[j, k]
            fw[9 + j, k] = got.upper(j, k)
    block = place[0]
    for k in range(SECTIONS):
        fw[4, k] = jnp.where(block == 1, got.lower(1, k), fw[4, k])
        fw[9, k] = jnp.where(block == 30, got.upper(2, k), fw[9, k])
    coarse.first_relax(xa, fw, 1, 13)
    coarse.relax(xb, xa, fw, 2, 12)
    coarse.relax(xa, xb, fw, 3, 11)
    coarse.relax(xb, xa, fw, 4, 10)
    middle.correct(ya, x1, xb, 5, 15, 2)
    middle.relax(yb, ya, f1, 6, 14)
    middle.relax(ya, yb, f1, 7, 13)
    fine.correct(za, x0, ya, 14, 26)
    fine.relax(zb, za, f0, 15, 25)
    fine.relax(za, zb, f0, 16, 24)

    half = lane_index() < 64

    def mix(row):
        phases = []
        for p in range(4):
            values = [za[16 + row, 4 * k + p] for k in range(SECTIONS)]
            sums = []
            for j in range(SECTIONS):
                total = TRANSFORM[j][0] * values[0]
                for k in range(1, SECTIONS):
                    total = total + TRANSFORM[j][k] * values[k]
                sums.append(total)
            phases.append(sums)
        for h in range(2):
            for j in range(SECTIONS):
                mixed[h, 8 * j + row] = jnp.where(
                    half, phases[2 * h][j], pltpu.roll(phases[2 * h + 1][j], 64, 1)
                )

    rows_loop(0, 8, mix)
    slot = lax.broadcasted_iota(jnp.int32, (256, 256), 0)
    column = lax.broadcasted_iota(jnp.int32, (256, 256), 1)
    chooser = jnp.where(column == 4 * (slot % 64) + slot // 64, 1.0, 0.0).astype(jnp.bfloat16)
    result = selected(
        jnp.concatenate([mixed[h].reshape(320, LANES) for h in range(2)], axis=1), chooser
    )
    started = []

    def send(source, target):
        started.append(pltpu.make_async_copy(source, target, done.at[len(started)]))
        started[-1].start()

    for j in (4, 0, 1, 2, 3):
        for h in range(2):
            cut = slice(h * 128, h * 128 + 128)
            for row in range(8):
                at = (8 * j + row) * 8
                turn[j, h, pl.ds(row, 8, stride=8), :] = result[at : at + 8, cut]
            if j == 4:
                after[h] = voltage[:, cut] + turn[j, h]
                send(after.at[h], next_voltage.at[:, cut])
            send(turn.at[j, h], sections.at[j, :, cut])
    for copy in started:
        copy.wait()


VMEM = pltpu.MemorySpace.VMEM


def vregs(*shape):
    return pltpu.VMEM(shape + (LAYERS, LANES), jnp.float32)


def scratch(*shape):
    return pltpu.VMEM(shape + (LAYERS, LANES), jnp.float32)


def call(kernel, inputs, outs, scratches=(), outside=False, aliases=(), out_space=None):
    space = pltpu.MemorySpace.HBM if outside else VMEM
    inputs = [pltpu.with_memory_space_constraint(value, space) for value in inputs]
    return pl.pallas_call(
        kernel,
        out_shape=outs,
        in_specs=[pl.BlockSpec(memory_space=space)] * len(inputs),
        out_specs=[pl.BlockSpec(memory_space=out_space or VMEM)] * len(outs),
        scratch_shapes=list(scratches),
        input_output_aliases=dict(aliases),
        compiler_params=pltpu.CompilerParams(vmem_limit_bytes=12 * 2**20),
    )(*inputs)


def turned(value, axis, count, shift):
    return lax.ppermute(value, axis, [(i, (i + shift) % count) for i in range(count)])


def paired(value, distance):
    rows = lax.axis_size("section") * lax.axis_size("gx")
    columns = lax.axis_size("gy")
    values = value if isinstance(value, tuple) else (value, value)
    result = [None, None]
    for which in (1, 0):
        pairs = []
        for row in range(rows):
            up = (row // distance) % 2 == which
            other = row + distance if up else row - distance
            for column in range(columns):
                target = (other, column)
                if not 0 <= other < rows:
                    target = (row, column ^ 1) if distance == 1 else (row ^ 1, column)
                pairs.append((row * columns + column, target[0] * columns + target[1]))
        result[which] = lax.ppermute(values[which], ("section", "gx", "gy"), pairs)
    return result


def local(voltage, capacity, node_class, via_sites, ball_sites, load_type, load_table):
    columns = lax.axis_size("gy")
    volts = voltage.reshape(64, 256)
    own, left, right = call(
        gather_kernel,
        (
            volts,
            capacity.reshape(64, 256),
            node_class.reshape(64, 256),
            via_sites.reshape(56, 256),
            ball_sites,
            load_type,
        ),
        [
            vregs(33, 2),
            pltpu.VMEM((264, 64), jnp.float32),
            pltpu.VMEM((264, 64), jnp.float32),
        ],
        [
            pltpu.VMEM((4, 2, 64, LANES), jnp.float32),
            pltpu.VMEM((64, 256), jnp.float32),
            pltpu.VMEM((64, 256), jnp.float32),
            pltpu.VMEM((64, 256), jnp.int32),
            pltpu.VMEM((56, 256), jnp.int32),
            pltpu.VMEM((8, 256), jnp.int32),
            pltpu.VMEM((8, 256), jnp.int32),
            pltpu.SemaphoreType.DMA((6,)),
            pltpu.VMEM((264, 256), jnp.float32),
        ],
        outside=True,
    )
    mixed_table = jnp.einsum(
        "tk,jk->tj", load_table, jnp.asarray(INVERSE, jnp.float32), precision=lax.Precision.HIGHEST
    )
    row_block = lax.axis_index("section") * lax.axis_size("gx") + lax.axis_index("gx")
    place = jnp.stack(
        [
            jnp.full((LAYERS, LANES), number, jnp.int32)
            for number in (row_block, lax.axis_index("gy"))
        ]
    )
    mixed_table = jnp.broadcast_to(
        mixed_table.reshape(LOADS * SECTIONS, 1, 1), (LOADS * SECTIONS, LAYERS, LANES)
    )
    near = paired(own, 1)
    from_lower = turned(right, "gy", columns, 1)
    from_upper = turned(left, "gy", columns, -1)
    (whole,) = call(rim_kernel, (own, from_lower, from_upper), [vregs(33, 3)])
    far = paired(whole, 2)
    go_right, go_left = call(edge_kernel, (place, *near), [vregs(33), vregs(33)])
    edge_left = turned(go_right, "gy", columns, 1)
    edge_right = turned(go_left, "gy", columns, -1)
    state_shapes = [
        vregs(EXT0, 4),
        vregs(EXT0, 5),
        vregs(EXT0, 4),
        vregs(EXT0, 4),
        vregs(EXT0, 4),
        vregs(EXT0, 4),
        vregs(EXT0, 20),
        vregs(EXT0, 20),
        vregs(EXT0, 20),
        vregs(EXT1, 2),
        vregs(EXT0, 4),
        vregs(EXT0, 4),
        pltpu.VMEM((EXT0 * TILES, LANES), jnp.float32),
        vregs(EXT0, 20),
    ]
    state = call(own_kernel, (place, mixed_table, whole), state_shapes)
    state = call(
        near_kernel,
        (place, mixed_table, *near, edge_left, edge_right, *state),
        [*state_shapes, vregs(EXT1, 10)],
        aliases=[(6 + n, n) for n in range(STATE)],
    )
    state = call(
        setup_kernel,
        (place, mixed_table, *far, *state),
        [
            *state_shapes,
            vregs(EXT1, 10),
            vregs(EXT1, 2),
            vregs(EXT1, 3),
            vregs(EXT1, 2),
            vregs(EXT1, 2),
            vregs(EXT1, 2),
            vregs(EXT1, 10),
            vregs(EXT1, 10),
            vregs(EXT2, 1),
            vregs(EXT2, 2),
            vregs(EXT2, 1),
            vregs(EXT2, 1),
            vregs(EXT2, 5),
            vregs(29),
            vregs(29),
        ],
        [scratch(EXT1, 10)],
        aliases=[(4 + n, n) for n in range(STATE + 1)],
    )
    fine, below1, f1 = state[:9], state[9], state[STATE]
    gx1, gy1, via1, cap1, total1, weights1, x1 = state[STATE + 1 : STATE + 8]
    middle = (gx1, gy1, via1, below1, cap1, total1, weights1, f1, x1)
    coarse = state[STATE + 8 : STATE + 13]
    got = paired(tuple(reversed(state[STATE + 13 :])), 2)
    x0, f1_own, go_side, gxw, gyw, viaw, beloww, weightsw = call(
        middle_kernel,
        (place, *fine, *middle, *coarse, *reversed(got)),
        [
            vregs(EXT0, 20),
            vregs(40),
            vregs(25),
            vregs(WIDE2 + 1, 1),
            vregs(WIDE2, 2),
            vregs(WIDE2, 1),
            vregs(WIDE2, 1),
            vregs(WIDE2, 5),
        ],
        [
            scratch(WIDE2, 1),
            scratch(WIDE2, 1),
            scratch(WIDE2, 5),
            scratch(WIDE2, 5),
            scratch(WIDE2, 5),
            scratch(EXT1, 10),
            scratch(EXT1, 10),
            scratch(EXT0, 20),
            scratch(4, 10),
        ],
    )
    got = paired(go_side, 1)
    f1, x1, f2_own = call(
        lower_kernel,
        (place, *middle[:7], f1_own, *got),
        [vregs(EXT1, 10), vregs(EXT1, 10), vregs(4, 5)],
        [scratch(EXT1, 10)],
    )
    got = paired(f2_own, 2)
    sections, next_voltage = call(
        finish_kernel,
        (
            place,
            *fine[:4],
            *fine[6:8],
            x0,
            *middle[:4],
            middle[6],
            f1,
            x1,
            gxw,
            gyw,
            viaw,
            beloww,
            weightsw,
            f2_own,
            *got,
            volts,
        ),
        [
            jax.ShapeDtypeStruct((SECTIONS, 64, 256), jnp.float32),
            jax.ShapeDtypeStruct((64, 256), jnp.float32),
        ],
        [
            scratch(WIDE2, 5),
            scratch(WIDE2, 5),
            scratch(WIDE2, 5),
            scratch(EXT1, 10),
            scratch(EXT1, 10),
            scratch(EXT0, 20),
            scratch(EXT0, 20),
            scratch(2, 40),
            pltpu.VMEM((SECTIONS, 2, 64, LANES), jnp.float32),
            pltpu.VMEM((2, 64, LANES), jnp.float32),
            pltpu.SemaphoreType.DMA((12,)),
        ],
        out_space=pltpu.MemorySpace.HBM,
    )
    return sections.reshape((SECTIONS,) + voltage.shape), next_voltage.reshape(voltage.shape)


def solution(mesh):
    return jax.shard_map(
        local,
        mesh=mesh,
        in_specs=(
            P(None, ("section", "gx"), "gy"),
            P(None, ("section", "gx"), "gy"),
            P(None, ("section", "gx"), "gy"),
            P(None, ("section", "gx"), "gy"),
            P(("section", "gx"), "gy"),
            P(("section", "gx"), "gy"),
            P(),
        ),
        out_specs=(P(None, None, ("section", "gx"), "gy"), P(None, ("section", "gx"), "gy")),
        check_vma=False,
    )
```

```python
import jax
import jax.numpy as jnp
from jax import lax
from jax.experimental import pallas as pl
from jax.experimental.pallas import tpu as pltpu
from jax.sharding import PartitionSpec as P

SECTIONS = 5
LOADS = 16
LAYERS = 8
LANES = 128
EXT0 = 40
EXT1 = 20
EXT2 = 10
WIDE2 = 14
TILES = 160

node_table = (0.35, 0.55, 0.8, 1.1, 1.5, 2.0, 2.7, 3.6)
via_conductance = 2.5
ball_conductance = 4.0
damping = 0.8
slab_partner = (0, 2, 1, 4, 3)


def pair_times(first, second):
    return (
        first[0] * second[0] - first[1] * second[1],
        first[0] * second[1] + first[1] * second[0],
    )


def pair_over(first, second):
    divisor = second[0] * second[0] + second[1] * second[1]
    return (
        (first[0] * second[0] + first[1] * second[1]) / divisor,
        (first[1] * second[0] - first[0] * second[1]) / divisor,
    )


def pair_minus(first, second):
    return (first[0] - second[0], first[1] - second[1])


def poly_value(coeffs, point):
    total = (0.0, 0.0)
    for c in reversed(coeffs):
        total = pair_times(total, point)
        total = (total[0] + c, total[1])
    return total


def poly_product(first, second):
    result = [0.0] * (len(first) + len(second) - 1)
    for i in range(len(first)):
        for j in range(len(second)):
            result[i + j] = result[i + j] + first[i] * second[j]
    return result


def poly_roots(coeffs):
    leading = coeffs[-1]
    scaled = [c / leading for c in coeffs]
    degree = len(coeffs) - 1
    guesses = []
    current = (1.0, 0.0)
    for k in range(degree):
        guesses.append(current)
        current = pair_times(current, (0.4, 0.9))
    for repeat_index in range(800):
        for k in range(degree):
            divisor = (1.0, 0.0)
            for j in range(degree):
                if j != k:
                    divisor = pair_times(divisor, pair_minus(guesses[k], guesses[j]))
            guesses[k] = pair_minus(guesses[k], pair_over(poly_value(scaled, guesses[k]), divisor))
    return guesses


def matrix_product(first, second):
    return [
        [
            sum((first[i][k] * second[k][j] for k in range(len(second))))
            for j in range(len(second[0]))
        ]
        for i in range(len(first))
    ]


def matrix_inverse(matrix):
    order = len(matrix)
    work = [list(matrix[i]) + [1.0 if i == j else 0.0 for j in range(order)] for i in range(order)]
    for column in range(order):
        pivot = column
        for i in range(column + 1, order):
            if abs(work[i][column]) > abs(work[pivot][column]):
                pivot = i
        work[column], work[pivot] = (work[pivot], work[column])
        factor = work[column][column]
        work[column] = [entry / factor for entry in work[column]]
        for i in range(order):
            if i != column:
                scale_row = work[i][column]
                work[i] = [work[i][j] - scale_row * work[column][j] for j in range(2 * order)]
    return [row[order:] for row in work]


def eigen_vector(matrix, value):
    order = len(matrix)
    size_inner = order - 1
    system = []
    for i in range(size_inner):
        row = []
        for j in range(order):
            entry = (matrix[i][j], 0.0)
            if i == j:
                entry = pair_minus(entry, value)
            row.append(entry)
        row[order - 1] = (-row[order - 1][0], -row[order - 1][1])
        system.append(row)
    for column in range(size_inner):
        pivot = column
        for i in range(column + 1, size_inner):
            left_size = system[i][column][0] ** 2 + system[i][column][1] ** 2
            right_size = system[pivot][column][0] ** 2 + system[pivot][column][1] ** 2
            if left_size > right_size:
                pivot = i
        system[column], system[pivot] = (system[pivot], system[column])
        for i in range(size_inner):
            if i != column:
                factor = pair_over(system[i][column], system[column][column])
                system[i] = [
                    pair_minus(system[i][j], pair_times(factor, system[column][j]))
                    for j in range(order)
                ]
    vector = [pair_over(system[i][order - 1], system[i][i]) for i in range(size_inner)]
    vector.append((1.0, 0.0))
    return vector


def radau_tables():
    section_count = 5
    generator = [1.0]
    for k in range(section_count - 1):
        generator = poly_product(generator, [0.0, 1.0])
    for k in range(section_count):
        generator = poly_product(generator, [-1.0, 1.0])
    for k in range(section_count - 1):
        generator = [j * generator[j] for j in range(1, len(generator))]
    abscissae = sorted((root[0] for root in poly_roots(generator)))
    vander = [[abscissae[i] ** j for j in range(section_count)] for i in range(section_count)]
    integrals = [
        [abscissae[i] ** (j + 1) / (j + 1) for j in range(section_count)]
        for i in range(section_count)
    ]
    butcher = matrix_product(integrals, matrix_inverse(vander))
    inverse = matrix_inverse(butcher)
    coeffs = [0.0] * (section_count + 1)
    coeffs[section_count] = 1.0
    current = [[0.0] * section_count for _ in range(section_count)]
    for k in range(1, section_count + 1):
        current = matrix_product(inverse, current)
        for i in range(section_count):
            current[i][i] = current[i][i] + coeffs[section_count - k + 1]
        applied = matrix_product(inverse, current)
        coeffs[section_count - k] = -sum((applied[i][i] for i in range(section_count))) / k
    eigen_values = poly_roots(coeffs)
    real_pick = 0
    for k in range(section_count):
        if abs(eigen_values[k][1]) < abs(eigen_values[real_pick][1]):
            real_pick = k
    upper_half = [k for k in range(section_count) if eigen_values[k][1] > 1e-09]
    upper_half = sorted(upper_half, key=lambda k: -eigen_values[k][0])
    columns = [[entry[0] for entry in eigen_vector(inverse, (eigen_values[real_pick][0], 0.0))]]
    for k in upper_half:
        vector = eigen_vector(inverse, eigen_values[k])
        columns.append([entry[0] for entry in vector])
        columns.append([entry[1] for entry in vector])
    transform = [[columns[j][i] for j in range(section_count)] for i in range(section_count)]
    inverse_transform = matrix_inverse(transform)
    blocks = matrix_product(matrix_product(inverse_transform, inverse), transform)
    diagonal = [blocks[k][k] for k in range(section_count)]
    coupling = [
        blocks[k][slab_partner[k]] if slab_partner[k] != k else 0.0 for k in range(section_count)
    ]
    return (transform, inverse_transform, diagonal, coupling)


TRANSFORM, INVERSE, DIAGONAL, COUPLING = radau_tables()
SHIFTS = (
    DIAGONAL[0],
    0.5 * (DIAGONAL[1] + DIAGONAL[2]),
    0.5 * (DIAGONAL[3] + DIAGONAL[4]),
)
COUPLES = (0.5 * (COUPLING[1] - COUPLING[2]), 0.5 * (COUPLING[3] - COUPLING[4]))
ROW_SUMS = tuple(sum(row) for row in INVERSE)


def from_right(value):
    return pltpu.roll(value, LANES - 1, 1)


def from_left(value):
    return pltpu.roll(value, 1, 1)


def from_above(value):
    return pltpu.roll(value, LAYERS - 1, 0)


def from_below(value):
    return pltpu.roll(value, 1, 0)


def lane_index():
    return lax.broadcasted_iota(jnp.int32, (LAYERS, LANES), 1)


def layer_index():
    return lax.broadcasted_iota(jnp.int32, (LAYERS, LANES), 0)


def spread(first, second, rim):
    own = lane_index() < 64
    inner = (first, pltpu.roll(first, 64, 1), second, pltpu.roll(second, 64, 1))
    outer = (rim, pltpu.roll(rim, 96, 1), pltpu.roll(rim, 64, 1), pltpu.roll(rim, 32, 1))
    return [jnp.where(own, near, far) for near, far in zip(inner, outer)]


def packed(values):
    lane = lane_index()
    result = []
    for q in range(5):
        carrier = values[q]
        for e in range(3):
            spare, at = values[5 + e], 72 + 16 * e
            if q < 4:
                part = pltpu.roll(spare, at - 16 * q, 1)
            else:
                part = jnp.where(
                    lane < at + 8,
                    pltpu.roll(spare, at - 64, 1),
                    pltpu.roll(spare, (at + 8 - 120) % LANES, 1),
                )
            carrier = jnp.where((lane >= at) & (lane < at + 16), part, carrier)
        result.append(carrier)
    return result


def unpacked(packs):
    lane = lane_index()
    result = list(packs)
    for e in range(3):
        at = 72 + 16 * e
        value = jnp.where(
            lane < 96,
            pltpu.roll(packs[4], (64 - at) % LANES, 1),
            pltpu.roll(packs[4], (120 - at - 8) % LANES, 1),
        )
        for q in range(4):
            part = pltpu.roll(packs[q], (16 * q - at) % LANES, 1)
            value = jnp.where((lane >= 16 * q) & (lane < 16 * q + 16), part, value)
        result.append(value)
    return result


def rows_loop(low, high, body, unroll=2):
    steps = (high - low) // unroll

    def step(n, carry):
        for j in range(unroll):
            body(low + n * unroll + j)
        return carry

    if steps > 1:
        lax.fori_loop(0, steps, step, 0)
    elif steps == 1:
        step(0, 0)
    for i in range(low + steps * unroll, high):
        body(i)


class Sides:
    def __init__(self, place, distance, first, second):
        self.odd = (place[0] & distance) != 0
        self.first, self.second = first, second

    def lower(self, *at):
        return jnp.where(self.odd, self.first[at], self.second[at])

    def upper(self, *at):
        return jnp.where(self.odd, self.second[at], self.first[at])


class Level:
    def __init__(self, phases, gx, gy, via, below, cap, total, weights):
        self.phases = phases
        self.unroll = 8 // phases
        self.gx, self.gy = gx, gy
        self.via, self.below = via, below
        self.cap, self.total, self.weights = cap, total, weights

    def sides(self, centre, p):
        right = centre[p + 1] if p < self.phases - 1 else from_right(centre[0])
        left = centre[p - 1] if p > 0 else from_left(centre[self.phases - 1])
        return right, left

    def inflow(self, coeffs, centre, p, upper, lower):
        gx_lower, gx_upper, gy_left, gy_right, via, below = coeffs
        right, left = self.sides(centre, p)
        here = centre[p]
        return (
            (gx_upper * upper + gx_lower * lower)
            + (gy_right * right + gy_left * left)
            + (via * from_above(here) + below * from_below(here))
        )

    def coeffs(self, i, p):
        return (
            self.gx[i, p],
            self.gx[i + 1, p],
            self.gy[i, p],
            self.gy[i, p + 1],
            self.via[i, p],
            self.below[i, p],
        )

    def set_total(self, i):
        bottom = layer_index() == 0
        for p in range(self.phases):
            grounded = self.below[i, p]
            below = jnp.where(bottom, 0.0, grounded)
            via = from_above(below)
            total = (
                (self.gx[i, p] + self.gx[i + 1, p])
                + (self.gy[i, p] + self.gy[i, p + 1])
                + (via + grounded)
            )
            self.below[i, p] = below
            self.via[i, p] = via
            self.total[i, p] = total
            cap = self.cap[i, p]
            self.weights[i, p * 5] = damping / (SHIFTS[0] * cap + total)
            for s in range(2):
                direct = SHIFTS[s + 1] * cap + total
                cross = COUPLES[s] * cap
                scale = damping / (direct * direct + cross * cross)
                self.weights[i, p * 5 + 1 + 2 * s] = direct * scale
                self.weights[i, p * 5 + 2 + 2 * s] = -(cross * scale)

    def weighted(self, i, p, values):
        w = [self.weights[i, p * 5 + m] for m in range(5)]
        out = [w[0] * values[0]]
        for s in range(2):
            first, second = values[1 + 2 * s], values[2 + 2 * s]
            out.append(w[1 + 2 * s] * first + w[2 + 2 * s] * second)
            out.append(w[1 + 2 * s] * second - w[2 + 2 * s] * first)
        return out

    def first_relax(self, target, source, low, high):
        def body(i):
            for p in range(self.phases):
                values = [source[i, k * self.phases + p] for k in range(SECTIONS)]
                for k, value in enumerate(self.weighted(i, p, values)):
                    target[i, k * self.phases + p] = value

        rows_loop(low, high, body, self.unroll)

    def gathered(self, iterate, source, i):
        count = self.phases
        centres = [[iterate[i, k * count + p] for p in range(count)] for k in range(SECTIONS)]
        sums = []
        for p in range(count):
            coeffs = self.coeffs(i, p)
            sums.append(
                [
                    source[i, k * count + p]
                    + self.inflow(
                        coeffs,
                        centres[k],
                        p,
                        iterate[i + 1, k * count + p],
                        iterate[i - 1, k * count + p],
                    )
                    for k in range(SECTIONS)
                ]
            )
        return centres, sums

    def relax(self, target, iterate, source, low, high):
        count = self.phases

        def body(i):
            centres, sums = self.gathered(iterate, source, i)
            for p in range(count):
                for k, value in enumerate(self.weighted(i, p, sums[p])):
                    target[i, k * count + p] = (1.0 - damping) * centres[k][p] + value

        rows_loop(low, high, body, self.unroll)

    def residual(self, iterate, source, i):
        centres, sums = self.gathered(iterate, source, i)
        result = []
        for p in range(self.phases):
            cap, total = self.cap[i, p], self.total[i, p]
            x = [centres[k][p] for k in range(SECTIONS)]
            out = [sums[p][0] - (SHIFTS[0] * cap + total) * x[0]]
            for s in range(2):
                direct = SHIFTS[s + 1] * cap + total
                cross = COUPLES[s] * cap
                a, b = 1 + 2 * s, 2 + 2 * s
                out.append(sums[p][a] - (direct * x[a] + cross * x[b]))
                out.append(sums[p][b] - (direct * x[b] - cross * x[a]))
            result.append(out)
        return result

    def restrict(self, target, iterate, source, low, high, shift=0):
        half = self.phases // 2

        def body(row):
            one = self.residual(iterate, source, 2 * row)
            two = self.residual(iterate, source, 2 * row + 1)
            for k in range(SECTIONS):
                for q in range(half):
                    target[row + shift, k * half + q] = (one[2 * q][k] + one[2 * q + 1][k]) + (
                        two[2 * q][k] + two[2 * q + 1][k]
                    )

        rows_loop(low, high, body, self.unroll // 2)

    def correct(self, target, iterate, coarse, low, high, shift=0):
        count, half = self.phases, self.phases // 2

        def body(i):
            row = lax.shift_right_logical(i, 1) + shift
            for k in range(SECTIONS):
                for q in range(half):
                    value = coarse[row, k * half + q]
                    for p in (2 * q, 2 * q + 1):
                        target[i, k * count + p] = iterate[i, k * count + p] + value

        rows_loop(low, high, body, self.unroll)


def coarsen(fine, coarse, rows):
    half = coarse.phases

    def body(row):
        for q in range(half):
            for ref_out, ref_in in ((coarse.cap, fine.cap),):
                ref_out[row, q] = (ref_in[2 * row, 2 * q] + ref_in[2 * row, 2 * q + 1]) + (
                    ref_in[2 * row + 1, 2 * q] + ref_in[2 * row + 1, 2 * q + 1]
                )
        for q in range(half + 1):
            coarse.gy[row, q] = fine.gy[2 * row, 2 * q] + fine.gy[2 * row + 1, 2 * q]

    rows_loop(0, rows, body, 4)

    def body_gx(row):
        for q in range(half):
            coarse.gx[row, q] = fine.gx[2 * row, 2 * q] + fine.gx[2 * row, 2 * q + 1]

    rows_loop(1, rows, body_gx, 4)


def sum_below(fine_below, coarse_below, phases, low, high):
    def body(row):
        for q in range(phases):
            coarse_below[row, q] = (
                fine_below[2 * row, 2 * q] + fine_below[2 * row, 2 * q + 1]
            ) + (fine_below[2 * row + 1, 2 * q] + fine_below[2 * row + 1, 2 * q + 1])

    rows_loop(low, high, body, 4)


def gather_kernel(*refs):
    own, left, right, work = refs[6:10]
    whole = refs[17]
    voltage, capacity, node_class, via, ball, load = refs[10:16]
    copies = [
        pltpu.make_async_copy(source, target, refs[16].at[n])
        for n, (source, target) in enumerate(zip(refs[:6], refs[10:16]))
    ]
    for copy in copies:
        copy.start()
    for copy in copies:
        copy.wait()
    classes = node_class[...]
    conduct = jnp.full(classes.shape, node_table[0], jnp.float32)
    for c in range(1, len(node_table)):
        conduct = jnp.where(classes == c, node_table[c], conduct)
    grounded = jnp.where(ball[...] == 1, ball_conductance, 0.0)
    upright = jnp.where(via[...] == 1, via_conductance, 0.0)
    for h in range(2):
        half = slice(h * 128, h * 128 + 128)
        work[0, h] = voltage[:, half]
        work[1, h] = capacity[:, half]
        work[2, h] = conduct[:, half]
        work[3, h, 0:8] = grounded[:, half]
        work[3, h, 8:64] = upright[:, half]
    for row in range(8):
        for a in range(4):
            at = (row * 4 + a) * 8
            for h in range(2):
                whole[at : at + 8, h * 128 : h * 128 + 128] = work[
                    a, h, pl.ds(row, 8, stride=8), :
                ]
    whole[256:264] = load[...].astype(jnp.float32)
    left[...] = whole[:, :64]
    right[...] = whole[:, 192:]
    column = lax.broadcasted_iota(jnp.int32, (256, 256), 0)
    slot = lax.broadcasted_iota(jnp.int32, (256, 256), 1)
    wanted = 4 * (slot % 64) + slot // 64
    result = selected(whole[...], jnp.where(column == wanted, 1.0, 0.0).astype(jnp.bfloat16))
    for n in range(33):
        for h in range(2):
            own[n, h] = result[8 * n : 8 * n + 8, 128 * h : 128 * h + 128]


def three_parts(value):
    high = value.astype(jnp.bfloat16)
    rest = value - high.astype(jnp.float32)
    middle = rest.astype(jnp.bfloat16)
    low = (rest - middle.astype(jnp.float32)).astype(jnp.bfloat16)
    return high, middle, low


def selected(value, chooser):
    high, middle, low = (
        jnp.dot(part, chooser, preferred_element_type=jnp.float32) for part in three_parts(value)
    )
    return high + (middle + low)


def rim_kernel(own, from_lower, from_upper, whole):
    column = lax.broadcasted_iota(jnp.int32, (64, LANES), 0)
    slot = lax.broadcasted_iota(jnp.int32, (64, LANES), 1)
    group, place = slot // 32, slot % 32
    below = (place >= 16) & (column == 4 * (place - 16) + (group + 1) % 4)
    above = (place < 16) & (column == 4 * place + (group + 2) % 4)
    result = selected(from_lower[...], jnp.where(below, 1.0, 0.0).astype(jnp.bfloat16))
    result = result + selected(
        from_upper[...], jnp.where(above, 1.0, 0.0).astype(jnp.bfloat16)
    )
    for n in range(33):
        whole[n, 2] = result[8 * n : 8 * n + 8]
        for h in range(2):
            whole[n, h] = own[n, h]


def edge_kernel(place, near0, near1, go_right, go_left):
    lane = lane_index()
    group = lane // 32
    late = lane % 32 >= 16
    near = Sides(place, 1, near0, near1)

    def chosen(one, two, three, four):
        return jnp.where(
            group < 2, jnp.where(group == 0, one, two), jnp.where(group == 2, three, four)
        )

    def body(n):
        rights, lefts = [], []
        for block in (near.lower, near.upper):
            first, second = block(n, 0), block(n, 1)
            first_far, first_near = pltpu.roll(first, 64, 1), pltpu.roll(first, 32, 1)
            second_far = pltpu.roll(second, 96, 1)
            rights.append(chosen(first_near, second, second_far, first_far))
            lefts.append(chosen(second, second_far, first_far, first_near))
        go_right[n] = jnp.where(late, rights[0], pltpu.roll(rights[1], 112, 1))
        go_left[n] = jnp.where(late, pltpu.roll(lefts[1], 16, 1), lefts[0])

    rows_loop(0, 33, body, 11)


def prepare(
    place, mixed_table, state, f1, blocks, gx_rows, total_rows, relax_rows, sum_rows, unroll=8
):
    (gx0, gy0, via0, below0, cap0, total0, weights0, f0, x0) = state[:9]
    below1, volt, conduct, surface, spare = state[9:14]
    fine = Level(4, gx0, gy0, via0, below0, cap0, total0, weights0)
    row_block, column_block = place[0], place[1]
    lane = lane_index()
    edge = ((lane == 0) & (column_block == 0)) | ((lane == 64) & (column_block == 3))
    joined = jnp.where(edge, 0.0, 2.0)
    top = layer_index() == LAYERS - 1

    def series(near, far):
        return 2.0 * near * far / (near + far)

    def set_gy(i):
        here = [conduct[i, p] for p in range(4)]
        before = from_left(here[3])
        first = joined * before * here[0] / (before + here[0])
        gy0[i, 0] = first
        for p in range(1, 4):
            gy0[i, p] = series(here[p - 1], here[p])

    def turn_gy(i):
        gy0[i, 4] = from_right(gy0[i, 0])

    for b, block, rim in blocks:

        def place_row(s, block=block, rim=rim, b=b):
            for a, ref in enumerate((volt, cap0, conduct, below0)):
                n = 4 * s + a
                phases = spread(block(n, 0), block(n, 1), rim(n))
                for p in range(4):
                    ref[8 * b + s, p] = phases[p]

        rows_loop(0, 8, place_row, unroll)
        loads = spread(block(32, 0), block(32, 1), rim(32))
        for p in range(4):
            values = [jnp.zeros((8, LANES), jnp.float32) for _ in range(SECTIONS)]
            for t in range(LOADS):
                chosen = loads[p] == float(t)
                values = [
                    jnp.where(chosen, mixed_table[SECTIONS * t + k], values[k]) for k in range(SECTIONS)
                ]
            for k in range(SECTIONS):
                at = 8 * b * TILES + (4 * k + p) * LAYERS + LAYERS - 1
                surface[pl.ds(at, 8, stride=TILES), :] = values[k]
        rows_loop(8 * b, 8 * b + 8, set_gy, 8)
        rows_loop(8 * b, 8 * b + 8, turn_gy, 8)
        sum_below(below0, below1, 2, 4 * b, 4 * b + 4)

    def set_gx(i):
        row = 8 * row_block - 16 + i
        twice = jnp.where((row == 0) | (row == 256), 0.0, 2.0)
        for p in range(4):
            near, far = conduct[i - 1, p], conduct[i, p]
            gx0[i, p] = twice * near * far / (near + far)

    def set_source(i):
        centre = [volt[i, p] for p in range(4)]
        for p in range(4):
            leak = total0[i, p] * centre[p] - fine.inflow(
                fine.coeffs(i, p), centre, p, volt[i + 1, p], volt[i - 1, p]
            )
            values = []
            for k in range(SECTIONS):
                at = pl.multiple_of(i * TILES + (4 * k + p) * LAYERS, LAYERS)
                drawn = surface[pl.ds(at, LAYERS), :]
                values.append(jnp.where(top, drawn, 0.0) - ROW_SUMS[k] * leak)
                f0[i, 4 * k + p] = values[k]
            for k, value in enumerate(fine.weighted(i, p, values)):
                spare[i, 4 * k + p] = value

    def set_row(i):
        fine.set_total(i)
        set_source(i)

    for low, high in gx_rows:
        rows_loop(low, high, set_gx, 8)
    for low, high in total_rows:
        rows_loop(low, high, set_row, 4)
    for low, high in relax_rows:
        fine.relax(x0, spare, f0, low, high)
    for low, high in sum_rows:
        fine.restrict(f1, x0, f0, low, high)


STATE = 14


def own_kernel(place, mixed_table, whole, *refs):
    prepare(
        place,
        mixed_table,
        refs,
        None,
        ((2, lambda n, h: whole[n, h], lambda n: whole[n, 2]),),
        ((17, 24),),
        ((17, 23),),
        ((18, 22),),
        (),
    )


def near_kernel(place, mixed_table, near0, near1, edge_left, edge_right, *refs):
    refs = refs[STATE:]
    late = lane_index() % 32 >= 16
    near = Sides(place, 1, near0, near1)

    def rim_lower(n):
        return jnp.where(late, edge_left[n], edge_right[n])

    def rim_upper(n):
        return jnp.where(
            late, pltpu.roll(edge_left[n], 16, 1), pltpu.roll(edge_right[n], 112, 1)
        )

    prepare(
        place,
        mixed_table,
        refs[:STATE],
        refs[STATE],
        ((1, near.lower, rim_lower), (3, near.upper, rim_upper)),
        ((9, 17), (24, 32)),
        ((9, 17), (23, 31)),
        ((10, 18), (22, 30)),
        ((6, 14),),
        4,
    )


def setup_kernel(place, mixed_table, far0, far1, *refs):
    refs = refs[STATE + 1 :]
    state, f1 = refs[:STATE], refs[STATE]
    gx1, gy1, via1, cap1, total1, weights1, x1 = refs[STATE + 1 : STATE + 8]
    gx2, gy2, below2, cap2, f2, go1, go0, spare1 = refs[STATE + 8 :]
    far = Sides(place, 2, far0, far1)
    below1 = state[9]
    prepare(
        place,
        mixed_table,
        state,
        f1,
        (
            (0, far.lower, lambda n: far.lower(n, 2)),
            (4, far.upper, lambda n: far.upper(n, 2)),
        ),
        ((2, 9), (32, 39)),
        ((2, 9), (31, 38)),
        ((3, 10), (30, 37)),
        ((2, 6), (14, 18)),
    )
    fine = Level(4, *state[:7])
    middle = Level(2, gx1, gy1, via1, below1, cap1, total1, weights1)
    coarse = Level(1, gx2, gy2, None, below2, cap2, None, None)
    coarsen(fine, middle, EXT1)
    coarsen(middle, coarse, EXT2)
    sum_below(below1, below2, 1, 0, EXT2)
    rows_loop(2, EXT1 - 2, middle.set_total, 4)
    middle.first_relax(spare1, f1, 2, 18)
    middle.relax(x1, spare1, f1, 3, 17)
    middle.restrict(f2, x1, f1, 2, 8)
    ups, downs = [], []
    for target, first, outer in ((ups, 2, 2), (downs, 4, 6)):
        for j in range(4):
            for k in range(SECTIONS):
                target.append(f2[first + j, k])
        for j in range(2):
            target.extend((gy2[outer + j, 0], below2[outer + j, 0], cap2[outer + j, 0]))
        for j in range(3):
            target.append(gx2[outer + j, 0])
    for n, (up, down) in enumerate(zip(ups, downs)):
        go0[n] = jnp.where(far.odd, down, up)
        go1[n] = jnp.where(far.odd, up, down)


def middle_kernel(place, *refs):
    (gx0, gy0, via0, below0, cap0, total0, weights0, f0, x0) = refs[0:9]
    (gx1, gy1, via1, below1, cap1, total1, weights1, f1, x1) = refs[9:18]
    (gx2, gy2, below2, cap2, f2, got1, got0) = refs[18:25]
    got = Sides(place, 2, got0, got1)
    (x0_out, f1_out, go_side, gxw, gyw, viaw, beloww, weightsw) = refs[25:33]
    (capw, totalw, fw, xa, xb, ya, yb, za, f1_own) = refs[33:42]
    fine = Level(4, gx0, gy0, via0, below0, cap0, total0, weights0)
    middle = Level(2, gx1, gy1, via1, below1, cap1, total1, weights1)
    coarse = Level(1, gxw, gyw, viaw, beloww, capw, totalw, weightsw)
    for j in range(4):
        for k in range(SECTIONS):
            fw[j, k] = got.lower(5 * j + k)
            fw[10 + j, k] = got.upper(5 * j + k)
    for j in range(2):
        for near, source in ((j, got.lower), (12 + j, got.upper)):
            gyw[near, 0] = source(20 + 3 * j)
            gyw[near, 1] = from_right(source(20 + 3 * j))
            beloww[near, 0] = source(21 + 3 * j)
            capw[near, 0] = source(22 + 3 * j)
    for j in range(3):
        gxw[j, 0] = got.lower(26 + j)
        gxw[12 + j, 0] = got.upper(26 + j)
    for j in range(6):
        for k in range(SECTIONS):
            fw[4 + j, k] = f2[2 + j, k]
    for j in range(10):
        gyw[2 + j, 0] = gy2[j, 0]
        gyw[2 + j, 1] = gy2[j, 1]
        beloww[2 + j, 0] = below2[j, 0]
        capw[2 + j, 0] = cap2[j, 0]
    for j in range(1, 10):
        gxw[2 + j, 0] = gx2[j, 0]
    rows_loop(0, WIDE2, coarse.set_total, 7)
    coarse.first_relax(xa, fw, 0, 14)
    coarse.relax(xb, xa, fw, 1, 13)
    coarse.relax(xa, xb, fw, 2, 12)
    coarse.relax(xb, xa, fw, 3, 11)
    middle.correct(ya, x1, xb, 3, 17, 2)
    middle.relax(yb, ya, f1, 4, 16)
    middle.relax(ya, yb, f1, 5, 15)
    fine.correct(x0_out, x0, ya, 10, 30)
    fine.relax(za, x0_out, f0, 11, 29)
    fine.relax(x0_out, za, f0, 12, 28)
    fine.relax(za, x0_out, f0, 13, 27)
    fine.relax(x0_out, za, f0, 14, 26)
    fine.restrict(f1_own, x0_out, f0, 8, 12, -8)
    for j in range(4):
        for n in range(10):
            f1_out[10 * j + n] = f1_own[j, n]
    for j in range(5):
        packs = packed([f1_own[n // 10, n % 10] for n in range(8 * j, 8 * j + 8)])
        for t in range(5):
            go_side[5 * j + t] = packs[t]


def lower_kernel(place, *refs):
    (gx1, gy1, via1, below1, cap1, total1, weights1) = refs[0:7]
    own, got0, got1 = refs[7:10]
    got = Sides(place, 1, got0, got1)
    f1, x1, f2_out = refs[10:13]
    (xa,) = refs[13:14]
    middle = Level(2, gx1, gy1, via1, below1, cap1, total1, weights1)
    for j in range(5):
        for first, source in ((4, got.lower), (12, got.upper)):
            values = unpacked([source(5 * j + t) for t in range(5)])
            for t in range(8):
                n = 8 * j + t
                f1[first + n // 10, n % 10] = values[t]
        for n in range(8 * j, 8 * j + 8):
            f1[8 + n // 10, n % 10] = own[n]
    middle.first_relax(xa, f1, 4, 16)
    middle.relax(x1, xa, f1, 5, 15)
    middle.restrict(f2_out, x1, f1, 3, 7, -3)


def finish_kernel(place, *refs):
    (gx0, gy0, via0, below0, weights0, f0, x0) = refs[0:7]
    (gx1, gy1, via1, below1, weights1, f1, x1) = refs[7:14]
    (gxw, gyw, viaw, beloww, weightsw, own, got0, got1, voltage) = refs[14:23]
    got = Sides(place, 2, got0, got1)
    sections, next_voltage = refs[23:25]
    fw, xa, xb, ya, yb, za, zb, mixed, turn, after, done = refs[25:36]
    fine = Level(4, gx0, gy0, via0, below0, None, None, weights0)
    middle = Level(2, gx1, gy1, via1, below1, None, None, weights1)
    coarse = Level(1, gxw, gyw, viaw, beloww, None, None, weightsw)
    for j in range(4):
        for k in range(SECTIONS):
            fw[1 + j, k] = got.lower(j, k)
            fw[5 + j, k] = own[j, k]
            fw[9 + j, k] = got.upper(j, k)
    block = place[0]
    for k in range(SECTIONS):
        fw[4, k] = jnp.where(block == 1, got.lower(1, k), fw[4, k])
        fw[9, k] = jnp.where(block == 30, got.upper(2, k), fw[9, k])
    coarse.first_relax(xa, fw, 1, 13)
    coarse.relax(xb, xa, fw, 2, 12)
    coarse.relax(xa, xb, fw, 3, 11)
    coarse.relax(xb, xa, fw, 4, 10)
    middle.correct(ya, x1, xb, 5, 15, 2)
    middle.relax(yb, ya, f1, 6, 14)
    middle.relax(ya, yb, f1, 7, 13)
    fine.correct(za, x0, ya, 14, 26)
    fine.relax(zb, za, f0, 15, 25)
    fine.relax(za, zb, f0, 16, 24)

    half = lane_index() < 64

    def mix(row):
        phases = []
        for p in range(4):
            values = [za[16 + row, 4 * k + p] for k in range(SECTIONS)]
            sums = []
            for j in range(SECTIONS):
                total = TRANSFORM[j][0] * values[0]
                for k in range(1, SECTIONS):
                    total = total + TRANSFORM[j][k] * values[k]
                sums.append(total)
            phases.append(sums)
        for h in range(2):
            for j in range(SECTIONS):
                mixed[h, 8 * j + row] = jnp.where(
                    half, phases[2 * h][j], pltpu.roll(phases[2 * h + 1][j], 64, 1)
                )

    rows_loop(0, 8, mix)
    slot = lax.broadcasted_iota(jnp.int32, (256, 256), 0)
    column = lax.broadcasted_iota(jnp.int32, (256, 256), 1)
    chooser = jnp.where(column == 4 * (slot % 64) + slot // 64, 1.0, 0.0).astype(jnp.bfloat16)
    result = selected(
        jnp.concatenate([mixed[h].reshape(320, LANES) for h in range(2)], axis=1), chooser
    )
    started = []

    def send(source, target):
        started.append(pltpu.make_async_copy(source, target, done.at[len(started)]))
        started[-1].start()

    for j in (4, 0, 1, 2, 3):
        for h in range(2):
            cut = slice(h * 128, h * 128 + 128)
            for row in range(8):
                at = (8 * j + row) * 8
                turn[j, h, pl.ds(row, 8, stride=8), :] = result[at : at + 8, cut]
            if j == 4:
                after[h] = voltage[:, cut] + turn[j, h]
                send(after.at[h], next_voltage.at[:, cut])
            send(turn.at[j, h], sections.at[j, :, cut])
    for copy in started:
        copy.wait()


VMEM = pltpu.MemorySpace.VMEM


def vregs(*shape):
    return pltpu.VMEM(shape + (LAYERS, LANES), jnp.float32)


def scratch(*shape):
    return pltpu.VMEM(shape + (LAYERS, LANES), jnp.float32)


def call(kernel, inputs, outs, scratches=(), outside=False, aliases=(), out_space=None):
    space = pltpu.MemorySpace.HBM if outside else VMEM
    inputs = [pltpu.with_memory_space_constraint(value, space) for value in inputs]
    return pl.pallas_call(
        kernel,
        out_shape=outs,
        in_specs=[pl.BlockSpec(memory_space=space)] * len(inputs),
        out_specs=[pl.BlockSpec(memory_space=out_space or VMEM)] * len(outs),
        scratch_shapes=list(scratches),
        input_output_aliases=dict(aliases),
        compiler_params=pltpu.CompilerParams(vmem_limit_bytes=12 * 2**20),
    )(*inputs)


def turned(value, axis, count, shift):
    return lax.ppermute(value, axis, [(i, (i + shift) % count) for i in range(count)])


def paired(value, distance):
    rows = lax.axis_size("section") * lax.axis_size("gx")
    columns = lax.axis_size("gy")
    values = value if isinstance(value, tuple) else (value, value)
    result = [None, None]
    for which in (1, 0):
        pairs = []
        for row in range(rows):
            up = (row // distance) % 2 == which
            other = row + distance if up else row - distance
            for column in range(columns):
                target = (other, column)
                if not 0 <= other < rows:
                    target = (row, column ^ 1) if distance == 1 else (row ^ 1, column)
                pairs.append((row * columns + column, target[0] * columns + target[1]))
        result[which] = lax.ppermute(values[which], ("section", "gx", "gy"), pairs)
    return result


def local(voltage, capacity, node_class, via_sites, ball_sites, load_type, load_table):
    columns = lax.axis_size("gy")
    volts = voltage.reshape(64, 256)
    own, left, right = call(
        gather_kernel,
        (
            volts,
            capacity.reshape(64, 256),
            node_class.reshape(64, 256),
            via_sites.reshape(56, 256),
            ball_sites,
            load_type,
        ),
        [
            vregs(33, 2),
            pltpu.VMEM((264, 64), jnp.float32),
            pltpu.VMEM((264, 64), jnp.float32),
        ],
        [
            pltpu.VMEM((4, 2, 64, LANES), jnp.float32),
            pltpu.VMEM((64, 256), jnp.float32),
            pltpu.VMEM((64, 256), jnp.float32),
            pltpu.VMEM((64, 256), jnp.int32),
            pltpu.VMEM((56, 256), jnp.int32),
            pltpu.VMEM((8, 256), jnp.int32),
            pltpu.VMEM((8, 256), jnp.int32),
            pltpu.SemaphoreType.DMA((6,)),
            pltpu.VMEM((264, 256), jnp.float32),
        ],
        outside=True,
    )
    mixed_table = jnp.einsum(
        "tk,jk->tj", load_table, jnp.asarray(INVERSE, jnp.float32), precision=lax.Precision.HIGHEST
    )
    row_block = lax.axis_index("section") * lax.axis_size("gx") + lax.axis_index("gx")
    place = jnp.stack(
        [
            jnp.full((LAYERS, LANES), number, jnp.int32)
            for number in (row_block, lax.axis_index("gy"))
        ]
    )
    mixed_table = jnp.broadcast_to(
        mixed_table.reshape(LOADS * SECTIONS, 1, 1), (LOADS * SECTIONS, LAYERS, LANES)
    )
    near = paired(own, 1)
    from_lower = turned(right, "gy", columns, 1)
    from_upper = turned(left, "gy", columns, -1)
    (whole,) = call(rim_kernel, (own, from_lower, from_upper), [vregs(33, 3)])
    far = paired(whole, 2)
    go_right, go_left = call(edge_kernel, (place, *near), [vregs(33), vregs(33)])
    edge_left = turned(go_right, "gy", columns, 1)
    edge_right = turned(go_left, "gy", columns, -1)
    state_shapes = [
        vregs(EXT0, 4),
        vregs(EXT0, 5),
        vregs(EXT0, 4),
        vregs(EXT0, 4),
        vregs(EXT0, 4),
        vregs(EXT0, 4),
        vregs(EXT0, 20),
        vregs(EXT0, 20),
        vregs(EXT0, 20),
        vregs(EXT1, 2),
        vregs(EXT0, 4),
        vregs(EXT0, 4),
        pltpu.VMEM((EXT0 * TILES, LANES), jnp.float32),
        vregs(EXT0, 20),
    ]
    state = call(own_kernel, (place, mixed_table, whole), state_shapes)
    state = call(
        near_kernel,
        (place, mixed_table, *near, edge_left, edge_right, *state),
        [*state_shapes, vregs(EXT1, 10)],
        aliases=[(6 + n, n) for n in range(STATE)],
    )
    state = call(
        setup_kernel,
        (place, mixed_table, *far, *state),
        [
            *state_shapes,
            vregs(EXT1, 10),
            vregs(EXT1, 2),
            vregs(EXT1, 3),
            vregs(EXT1, 2),
            vregs(EXT1, 2),
            vregs(EXT1, 2),
            vregs(EXT1, 10),
            vregs(EXT1, 10),
            vregs(EXT2, 1),
            vregs(EXT2, 2),
            vregs(EXT2, 1),
            vregs(EXT2, 1),
            vregs(EXT2, 5),
            vregs(29),
            vregs(29),
        ],
        [scratch(EXT1, 10)],
        aliases=[(4 + n, n) for n in range(STATE + 1)],
    )
    fine, below1, f1 = state[:9], state[9], state[STATE]
    gx1, gy1, via1, cap1, total1, weights1, x1 = state[STATE + 1 : STATE + 8]
    middle = (gx1, gy1, via1, below1, cap1, total1, weights1, f1, x1)
    coarse = state[STATE + 8 : STATE + 13]
    got = paired(tuple(reversed(state[STATE + 13 :])), 2)
    x0, f1_own, go_side, gxw, gyw, viaw, beloww, weightsw = call(
        middle_kernel,
        (place, *fine, *middle, *coarse, *reversed(got)),
        [
            vregs(EXT0, 20),
            vregs(40),
            vregs(25),
            vregs(WIDE2 + 1, 1),
            vregs(WIDE2, 2),
            vregs(WIDE2, 1),
            vregs(WIDE2, 1),
            vregs(WIDE2, 5),
        ],
        [
            scratch(WIDE2, 1),
            scratch(WIDE2, 1),
            scratch(WIDE2, 5),
            scratch(WIDE2, 5),
            scratch(WIDE2, 5),
            scratch(EXT1, 10),
            scratch(EXT1, 10),
            scratch(EXT0, 20),
            scratch(4, 10),
        ],
    )
    got = paired(go_side, 1)
    f1, x1, f2_own = call(
        lower_kernel,
        (place, *middle[:7], f1_own, *got),
        [vregs(EXT1, 10), vregs(EXT1, 10), vregs(4, 5)],
        [scratch(EXT1, 10)],
    )
    got = paired(f2_own, 2)
    sections, next_voltage = call(
        finish_kernel,
        (
            place,
            *fine[:4],
            *fine[6:8],
            x0,
            *middle[:4],
            middle[6],
            f1,
            x1,
            gxw,
            gyw,
            viaw,
            beloww,
            weightsw,
            f2_own,
            *got,
            volts,
        ),
        [
            jax.ShapeDtypeStruct((SECTIONS, 64, 256), jnp.float32),
            jax.ShapeDtypeStruct((64, 256), jnp.float32),
        ],
        [
            scratch(WIDE2, 5),
            scratch(WIDE2, 5),
            scratch(WIDE2, 5),
            scratch(EXT1, 10),
            scratch(EXT1, 10),
            scratch(EXT0, 20),
            scratch(EXT0, 20),
            scratch(2, 40),
            pltpu.VMEM((SECTIONS, 2, 64, LANES), jnp.float32),
            pltpu.VMEM((2, 64, LANES), jnp.float32),
            pltpu.SemaphoreType.DMA((12,)),
        ],
        out_space=pltpu.MemorySpace.HBM,
    )
    return sections.reshape((SECTIONS,) + voltage.shape), next_voltage.reshape(voltage.shape)


def solution(mesh):
    return jax.shard_map(
        local,
        mesh=mesh,
        in_specs=(
            P(None, ("section", "gx"), "gy"),
            P(None, ("section", "gx"), "gy"),
            P(None, ("section", "gx"), "gy"),
            P(None, ("section", "gx"), "gy"),
            P(("section", "gx"), "gy"),
            P(("section", "gx"), "gy"),
            P(),
        ),
        out_specs=(P(None, None, ("section", "gx"), "gy"), P(None, ("section", "gx"), "gy")),
        check_vma=False,
    )
```

```python
import jax
import jax.numpy as jnp
from jax import lax
from jax.experimental import pallas as pl
from jax.experimental.pallas import tpu as pltpu
from jax.sharding import PartitionSpec as P

SECTIONS = 5
LOADS = 16
LAYERS = 8
LANES = 128
EXT0 = 40
EXT1 = 20
EXT2 = 10
WIDE2 = 14
TILES = 160

node_table = (0.35, 0.55, 0.8, 1.1, 1.5, 2.0, 2.7, 3.6)
via_conductance = 2.5
ball_conductance = 4.0
damping = 0.8
slab_partner = (0, 2, 1, 4, 3)


def pair_times(first, second):
    return (
        first[0] * second[0] - first[1] * second[1],
        first[0] * second[1] + first[1] * second[0],
    )


def pair_over(first, second):
    divisor = second[0] * second[0] + second[1] * second[1]
    return (
        (first[0] * second[0] + first[1] * second[1]) / divisor,
        (first[1] * second[0] - first[0] * second[1]) / divisor,
    )


def pair_minus(first, second):
    return (first[0] - second[0], first[1] - second[1])


def poly_value(coeffs, point):
    total = (0.0, 0.0)
    for c in reversed(coeffs):
        total = pair_times(total, point)
        total = (total[0] + c, total[1])
    return total


def poly_product(first, second):
    result = [0.0] * (len(first) + len(second) - 1)
    for i in range(len(first)):
        for j in range(len(second)):
            result[i + j] = result[i + j] + first[i] * second[j]
    return result


def poly_roots(coeffs):
    leading = coeffs[-1]
    scaled = [c / leading for c in coeffs]
    degree = len(coeffs) - 1
    guesses = []
    current = (1.0, 0.0)
    for k in range(degree):
        guesses.append(current)
        current = pair_times(current, (0.4, 0.9))
    for repeat_index in range(800):
        for k in range(degree):
            divisor = (1.0, 0.0)
            for j in range(degree):
                if j != k:
                    divisor = pair_times(divisor, pair_minus(guesses[k], guesses[j]))
            guesses[k] = pair_minus(guesses[k], pair_over(poly_value(scaled, guesses[k]), divisor))
    return guesses


def matrix_product(first, second):
    return [
        [
            sum((first[i][k] * second[k][j] for k in range(len(second))))
            for j in range(len(second[0]))
        ]
        for i in range(len(first))
    ]


def matrix_inverse(matrix):
    order = len(matrix)
    work = [list(matrix[i]) + [1.0 if i == j else 0.0 for j in range(order)] for i in range(order)]
    for column in range(order):
        pivot = column
        for i in range(column + 1, order):
            if abs(work[i][column]) > abs(work[pivot][column]):
                pivot = i
        work[column], work[pivot] = (work[pivot], work[column])
        factor = work[column][column]
        work[column] = [entry / factor for entry in work[column]]
        for i in range(order):
            if i != column:
                scale_row = work[i][column]
                work[i] = [work[i][j] - scale_row * work[column][j] for j in range(2 * order)]
    return [row[order:] for row in work]


def eigen_vector(matrix, value):
    order = len(matrix)
    size_inner = order - 1
    system = []
    for i in range(size_inner):
        row = []
        for j in range(order):
            entry = (matrix[i][j], 0.0)
            if i == j:
                entry = pair_minus(entry, value)
            row.append(entry)
        row[order - 1] = (-row[order - 1][0], -row[order - 1][1])
        system.append(row)
    for column in range(size_inner):
        pivot = column
        for i in range(column + 1, size_inner):
            left_size = system[i][column][0] ** 2 + system[i][column][1] ** 2
            right_size = system[pivot][column][0] ** 2 + system[pivot][column][1] ** 2
            if left_size > right_size:
                pivot = i
        system[column], system[pivot] = (system[pivot], system[column])
        for i in range(size_inner):
            if i != column:
                factor = pair_over(system[i][column], system[column][column])
                system[i] = [
                    pair_minus(system[i][j], pair_times(factor, system[column][j]))
                    for j in range(order)
                ]
    vector = [pair_over(system[i][order - 1], system[i][i]) for i in range(size_inner)]
    vector.append((1.0, 0.0))
    return vector


def radau_tables():
    section_count = 5
    generator = [1.0]
    for k in range(section_count - 1):
        generator = poly_product(generator, [0.0, 1.0])
    for k in range(section_count):
        generator = poly_product(generator, [-1.0, 1.0])
    for k in range(section_count - 1):
        generator = [j * generator[j] for j in range(1, len(generator))]
    abscissae = sorted((root[0] for root in poly_roots(generator)))
    vander = [[abscissae[i] ** j for j in range(section_count)] for i in range(section_count)]
    integrals = [
        [abscissae[i] ** (j + 1) / (j + 1) for j in range(section_count)]
        for i in range(section_count)
    ]
    butcher = matrix_product(integrals, matrix_inverse(vander))
    inverse = matrix_inverse(butcher)
    coeffs = [0.0] * (section_count + 1)
    coeffs[section_count] = 1.0
    current = [[0.0] * section_count for _ in range(section_count)]
    for k in range(1, section_count + 1):
        current = matrix_product(inverse, current)
        for i in range(section_count):
            current[i][i] = current[i][i] + coeffs[section_count - k + 1]
        applied = matrix_product(inverse, current)
        coeffs[section_count - k] = -sum((applied[i][i] for i in range(section_count))) / k
    eigen_values = poly_roots(coeffs)
    real_pick = 0
    for k in range(section_count):
        if abs(eigen_values[k][1]) < abs(eigen_values[real_pick][1]):
            real_pick = k
    upper_half = [k for k in range(section_count) if eigen_values[k][1] > 1e-09]
    upper_half = sorted(upper_half, key=lambda k: -eigen_values[k][0])
    columns = [[entry[0] for entry in eigen_vector(inverse, (eigen_values[real_pick][0], 0.0))]]
    for k in upper_half:
        vector = eigen_vector(inverse, eigen_values[k])
        columns.append([entry[0] for entry in vector])
        columns.append([entry[1] for entry in vector])
    transform = [[columns[j][i] for j in range(section_count)] for i in range(section_count)]
    inverse_transform = matrix_inverse(transform)
    blocks = matrix_product(matrix_product(inverse_transform, inverse), transform)
    diagonal = [blocks[k][k] for k in range(section_count)]
    coupling = [
        blocks[k][slab_partner[k]] if slab_partner[k] != k else 0.0 for k in range(section_count)
    ]
    return (transform, inverse_transform, diagonal, coupling)


TRANSFORM, INVERSE, DIAGONAL, COUPLING = radau_tables()
SHIFTS = (
    DIAGONAL[0],
    0.5 * (DIAGONAL[1] + DIAGONAL[2]),
    0.5 * (DIAGONAL[3] + DIAGONAL[4]),
)
COUPLES = (0.5 * (COUPLING[1] - COUPLING[2]), 0.5 * (COUPLING[3] - COUPLING[4]))
ROW_SUMS = tuple(sum(row) for row in INVERSE)


def from_right(value):
    return pltpu.roll(value, LANES - 1, 1)


def from_left(value):
    return pltpu.roll(value, 1, 1)


def from_above(value):
    return pltpu.roll(value, LAYERS - 1, 0)


def from_below(value):
    return pltpu.roll(value, 1, 0)


def lane_index():
    return lax.broadcasted_iota(jnp.int32, (LAYERS, LANES), 1)


def layer_index():
    return lax.broadcasted_iota(jnp.int32, (LAYERS, LANES), 0)


def spread(first, second, rim):
    own = lane_index() < 64
    inner = (first, pltpu.roll(first, 64, 1), second, pltpu.roll(second, 64, 1))
    outer = (rim, pltpu.roll(rim, 96, 1), pltpu.roll(rim, 64, 1), pltpu.roll(rim, 32, 1))
    return [jnp.where(own, near, far) for near, far in zip(inner, outer)]


def packed(values):
    lane = lane_index()
    result = []
    for q in range(5):
        carrier = values[q]
        for e in range(3):
            spare, at = values[5 + e], 72 + 16 * e
            if q < 4:
                part = pltpu.roll(spare, at - 16 * q, 1)
            else:
                part = jnp.where(
                    lane < at + 8,
                    pltpu.roll(spare, at - 64, 1),
                    pltpu.roll(spare, (at + 8 - 120) % LANES, 1),
                )
            carrier = jnp.where((lane >= at) & (lane < at + 16), part, carrier)
        result.append(carrier)
    return result


def unpacked(packs):
    lane = lane_index()
    result = list(packs)
    for e in range(3):
        at = 72 + 16 * e
        value = jnp.where(
            lane < 96,
            pltpu.roll(packs[4], (64 - at) % LANES, 1),
            pltpu.roll(packs[4], (120 - at - 8) % LANES, 1),
        )
        for q in range(4):
            part = pltpu.roll(packs[q], (16 * q - at) % LANES, 1)
            value = jnp.where((lane >= 16 * q) & (lane < 16 * q + 16), part, value)
        result.append(value)
    return result


def rows_loop(low, high, body, unroll=2):
    steps = (high - low) // unroll

    def step(n, carry):
        for j in range(unroll):
            body(low + n * unroll + j)
        return carry

    if steps > 1:
        lax.fori_loop(0, steps, step, 0)
    elif steps == 1:
        step(0, 0)
    for i in range(low + steps * unroll, high):
        body(i)


class Sides:
    def __init__(self, place, distance, first, second):
        self.odd = (place[0] & distance) != 0
        self.first, self.second = first, second

    def lower(self, *at):
        return jnp.where(self.odd, self.first[at], self.second[at])

    def upper(self, *at):
        return jnp.where(self.odd, self.second[at], self.first[at])


class Level:
    def __init__(self, phases, gx, gy, via, below, cap, total, weights):
        self.phases = phases
        self.unroll = 8 // phases
        self.gx, self.gy = gx, gy
        self.via, self.below = via, below
        self.cap, self.total, self.weights = cap, total, weights

    def sides(self, centre, p):
        right = centre[p + 1] if p < self.phases - 1 else from_right(centre[0])
        left = centre[p - 1] if p > 0 else from_left(centre[self.phases - 1])
        return right, left

    def inflow(self, coeffs, centre, p, upper, lower):
        gx_lower, gx_upper, gy_left, gy_right, via, below = coeffs
        right, left = self.sides(centre, p)
        here = centre[p]
        return (
            (gx_upper * upper + gx_lower * lower)
            + (gy_right * right + gy_left * left)
            + (via * from_above(here) + below * from_below(here))
        )

    def coeffs(self, i, p):
        return (
            self.gx[i, p],
            self.gx[i + 1, p],
            self.gy[i, p],
            self.gy[i, p + 1],
            self.via[i, p],
            self.below[i, p],
        )

    def set_total(self, i):
        bottom = layer_index() == 0
        for p in range(self.phases):
            grounded = self.below[i, p]
            below = jnp.where(bottom, 0.0, grounded)
            via = from_above(below)
            total = (
                (self.gx[i, p] + self.gx[i + 1, p])
                + (self.gy[i, p] + self.gy[i, p + 1])
                + (via + grounded)
            )
            self.below[i, p] = below
            self.via[i, p] = via
            self.total[i, p] = total
            cap = self.cap[i, p]
            self.weights[i, p * 5] = damping / (SHIFTS[0] * cap + total)
            for s in range(2):
                direct = SHIFTS[s + 1] * cap + total
                cross = COUPLES[s] * cap
                scale = damping / (direct * direct + cross * cross)
                self.weights[i, p * 5 + 1 + 2 * s] = direct * scale
                self.weights[i, p * 5 + 2 + 2 * s] = -(cross * scale)

    def weighted(self, i, p, values):
        w = [self.weights[i, p * 5 + m] for m in range(5)]
        out = [w[0] * values[0]]
        for s in range(2):
            first, second = values[1 + 2 * s], values[2 + 2 * s]
            out.append(w[1 + 2 * s] * first + w[2 + 2 * s] * second)
            out.append(w[1 + 2 * s] * second - w[2 + 2 * s] * first)
        return out

    def first_relax(self, target, source, low, high):
        def body(i):
            for p in range(self.phases):
                values = [source[i, k * self.phases + p] for k in range(SECTIONS)]
                for k, value in enumerate(self.weighted(i, p, values)):
                    target[i, k * self.phases + p] = value

        rows_loop(low, high, body, self.unroll)

    def gathered(self, iterate, source, i):
        count = self.phases
        centres = [[iterate[i, k * count + p] for p in range(count)] for k in range(SECTIONS)]
        sums = []
        for p in range(count):
            coeffs = self.coeffs(i, p)
            sums.append(
                [
                    source[i, k * count + p]
                    + self.inflow(
                        coeffs,
                        centres[k],
                        p,
                        iterate[i + 1, k * count + p],
                        iterate[i - 1, k * count + p],
                    )
                    for k in range(SECTIONS)
                ]
            )
        return centres, sums

    def relax(self, target, iterate, source, low, high):
        count = self.phases

        def body(i):
            centres, sums = self.gathered(iterate, source, i)
            for p in range(count):
                for k, value in enumerate(self.weighted(i, p, sums[p])):
                    target[i, k * count + p] = (1.0 - damping) * centres[k][p] + value

        rows_loop(low, high, body, self.unroll)

    def residual(self, iterate, source, i):
        centres, sums = self.gathered(iterate, source, i)
        result = []
        for p in range(self.phases):
            cap, total = self.cap[i, p], self.total[i, p]
            x = [centres[k][p] for k in range(SECTIONS)]
            out = [sums[p][0] - (SHIFTS[0] * cap + total) * x[0]]
            for s in range(2):
                direct = SHIFTS[s + 1] * cap + total
                cross = COUPLES[s] * cap
                a, b = 1 + 2 * s, 2 + 2 * s
                out.append(sums[p][a] - (direct * x[a] + cross * x[b]))
                out.append(sums[p][b] - (direct * x[b] - cross * x[a]))
            result.append(out)
        return result

    def restrict(self, target, iterate, source, low, high, shift=0):
        half = self.phases // 2

        def body(row):
            one = self.residual(iterate, source, 2 * row)
            two = self.residual(iterate, source, 2 * row + 1)
            for k in range(SECTIONS):
                for q in range(half):
                    target[row + shift, k * half + q] = (one[2 * q][k] + one[2 * q + 1][k]) + (
                        two[2 * q][k] + two[2 * q + 1][k]
                    )

        rows_loop(low, high, body, 2)

    def correct(self, target, iterate, coarse, low, high, shift=0):
        count, half = self.phases, self.phases // 2

        def body(i):
            row = lax.shift_right_logical(i, 1) + shift
            for k in range(SECTIONS):
                for q in range(half):
                    value = coarse[row, k * half + q]
                    for p in (2 * q, 2 * q + 1):
                        target[i, k * count + p] = iterate[i, k * count + p] + value

        rows_loop(low, high, body, self.unroll)


def coarsen(fine, coarse, rows):
    half = coarse.phases

    def body(row):
        for q in range(half):
            for ref_out, ref_in in ((coarse.cap, fine.cap),):
                ref_out[row, q] = (ref_in[2 * row, 2 * q] + ref_in[2 * row, 2 * q + 1]) + (
                    ref_in[2 * row + 1, 2 * q] + ref_in[2 * row + 1, 2 * q + 1]
                )
        for q in range(half + 1):
            coarse.gy[row, q] = fine.gy[2 * row, 2 * q] + fine.gy[2 * row + 1, 2 * q]

    rows_loop(0, rows, body, 4)

    def body_gx(row):
        for q in range(half):
            coarse.gx[row, q] = fine.gx[2 * row, 2 * q] + fine.gx[2 * row, 2 * q + 1]

    rows_loop(1, rows, body_gx, 4)


def sum_below(fine_below, coarse_below, phases, low, high):
    def body(row):
        for q in range(phases):
            coarse_below[row, q] = (
                fine_below[2 * row, 2 * q] + fine_below[2 * row, 2 * q + 1]
            ) + (fine_below[2 * row + 1, 2 * q] + fine_below[2 * row + 1, 2 * q + 1])

    rows_loop(low, high, body, 4)


def gather_kernel(*refs):
    own, left, right, work = refs[6:10]
    whole = refs[17]
    voltage, capacity, node_class, via, ball, load = refs[10:16]
    copies = [
        pltpu.make_async_copy(source, target, refs[16].at[n])
        for n, (source, target) in enumerate(zip(refs[:6], refs[10:16]))
    ]
    for copy in copies:
        copy.start()
    for copy in copies:
        copy.wait()
    classes = node_class[...]
    conduct = jnp.full(classes.shape, node_table[0], jnp.float32)
    for c in range(1, len(node_table)):
        conduct = jnp.where(classes == c, node_table[c], conduct)
    grounded = jnp.where(ball[...] == 1, ball_conductance, 0.0)
    upright = jnp.where(via[...] == 1, via_conductance, 0.0)
    for h in range(2):
        half = slice(h * 128, h * 128 + 128)
        work[0, h] = voltage[:, half]
        work[1, h] = capacity[:, half]
        work[2, h] = conduct[:, half]
        work[3, h, 0:8] = grounded[:, half]
        work[3, h, 8:64] = upright[:, half]
    for row in range(8):
        for a in range(4):
            at = (row * 4 + a) * 8
            for h in range(2):
                whole[at : at + 8, h * 128 : h * 128 + 128] = work[
                    a, h, pl.ds(row, 8, stride=8), :
                ]
    whole[256:264] = load[...].astype(jnp.float32)
    left[...] = whole[:, :64]
    right[...] = whole[:, 192:]
    column = lax.broadcasted_iota(jnp.int32, (256, 256), 0)
    slot = lax.broadcasted_iota(jnp.int32, (256, 256), 1)
    wanted = 4 * (slot % 64) + slot // 64
    result = selected(whole[...], jnp.where(column == wanted, 1.0, 0.0).astype(jnp.bfloat16))
    for n in range(33):
        for h in range(2):
            own[n, h] = result[8 * n : 8 * n + 8, 128 * h : 128 * h + 128]


def three_parts(value):
    high = value.astype(jnp.bfloat16)
    rest = value - high.astype(jnp.float32)
    middle = rest.astype(jnp.bfloat16)
    low = (rest - middle.astype(jnp.float32)).astype(jnp.bfloat16)
    return high, middle, low


def selected(value, chooser):
    high, middle, low = (
        jnp.dot(part, chooser, preferred_element_type=jnp.float32) for part in three_parts(value)
    )
    return high + (middle + low)


def rim_kernel(own, from_lower, from_upper, whole):
    column = lax.broadcasted_iota(jnp.int32, (64, LANES), 0)
    slot = lax.broadcasted_iota(jnp.int32, (64, LANES), 1)
    group, place = slot // 32, slot % 32
    below = (place >= 16) & (column == 4 * (place - 16) + (group + 1) % 4)
    above = (place < 16) & (column == 4 * place + (group + 2) % 4)
    result = selected(from_lower[...], jnp.where(below, 1.0, 0.0).astype(jnp.bfloat16))
    result = result + selected(
        from_upper[...], jnp.where(above, 1.0, 0.0).astype(jnp.bfloat16)
    )
    for n in range(33):
        whole[n, 2] = result[8 * n : 8 * n + 8]
        for h in range(2):
            whole[n, h] = own[n, h]


def edge_kernel(place, near0, near1, go_right, go_left):
    lane = lane_index()
    group = lane // 32
    late = lane % 32 >= 16
    near = Sides(place, 1, near0, near1)

    def chosen(one, two, three, four):
        return jnp.where(
            group < 2, jnp.where(group == 0, one, two), jnp.where(group == 2, three, four)
        )

    def body(n):
        rights, lefts = [], []
        for block in (near.lower, near.upper):
            first, second = block(n, 0), block(n, 1)
            first_far, first_near = pltpu.roll(first, 64, 1), pltpu.roll(first, 32, 1)
            second_far = pltpu.roll(second, 96, 1)
            rights.append(chosen(first_near, second, second_far, first_far))
            lefts.append(chosen(second, second_far, first_far, first_near))
        go_right[n] = jnp.where(late, rights[0], pltpu.roll(rights[1], 112, 1))
        go_left[n] = jnp.where(late, pltpu.roll(lefts[1], 16, 1), lefts[0])

    rows_loop(0, 33, body, 11)


def prepare(
    place, mixed_table, state, f1, blocks, gx_rows, total_rows, relax_rows, sum_rows, unroll=8
):
    (gx0, gy0, via0, below0, cap0, total0, weights0, f0, x0) = state[:9]
    below1, volt, conduct, surface, spare = state[9:14]
    fine = Level(4, gx0, gy0, via0, below0, cap0, total0, weights0)
    row_block, column_block = place[0], place[1]
    lane = lane_index()
    edge = ((lane == 0) & (column_block == 0)) | ((lane == 64) & (column_block == 3))
    joined = jnp.where(edge, 0.0, 2.0)
    top = layer_index() == LAYERS - 1

    def series(near, far):
        return 2.0 * near * far / (near + far)

    def set_gy(i):
        here = [conduct[i, p] for p in range(4)]
        before = from_left(here[3])
        first = joined * before * here[0] / (before + here[0])
        gy0[i, 0] = first
        for p in range(1, 4):
            gy0[i, p] = series(here[p - 1], here[p])

    def turn_gy(i):
        gy0[i, 4] = from_right(gy0[i, 0])

    for b, block, rim in blocks:

        def place_row(s, block=block, rim=rim, b=b):
            for a, ref in enumerate((volt, cap0, conduct, below0)):
                n = 4 * s + a
                phases = spread(block(n, 0), block(n, 1), rim(n))
                for p in range(4):
                    ref[8 * b + s, p] = phases[p]

        rows_loop(0, 8, place_row, unroll)
        loads = spread(block(32, 0), block(32, 1), rim(32))
        for p in range(4):
            values = [jnp.zeros((8, LANES), jnp.float32) for _ in range(SECTIONS)]
            for t in range(LOADS):
                chosen = loads[p] == float(t)
                values = [
                    jnp.where(chosen, mixed_table[SECTIONS * t + k], values[k]) for k in range(SECTIONS)
                ]
            for k in range(SECTIONS):
                at = 8 * b * TILES + (4 * k + p) * LAYERS + LAYERS - 1
                surface[pl.ds(at, 8, stride=TILES), :] = values[k]
        rows_loop(8 * b, 8 * b + 8, set_gy, 8)
        rows_loop(8 * b, 8 * b + 8, turn_gy, 8)
        sum_below(below0, below1, 2, 4 * b, 4 * b + 4)

    def set_gx(i):
        row = 8 * row_block - 16 + i
        twice = jnp.where((row == 0) | (row == 256), 0.0, 2.0)
        for p in range(4):
            near, far = conduct[i - 1, p], conduct[i, p]
            gx0[i, p] = twice * near * far / (near + far)

    def set_source(i):
        centre = [volt[i, p] for p in range(4)]
        for p in range(4):
            leak = total0[i, p] * centre[p] - fine.inflow(
                fine.coeffs(i, p), centre, p, volt[i + 1, p], volt[i - 1, p]
            )
            values = []
            for k in range(SECTIONS):
                at = pl.multiple_of(i * TILES + (4 * k + p) * LAYERS, LAYERS)
                drawn = surface[pl.ds(at, LAYERS), :]
                values.append(jnp.where(top, drawn, 0.0) - ROW_SUMS[k] * leak)
                f0[i, 4 * k + p] = values[k]
            for k, value in enumerate(fine.weighted(i, p, values)):
                spare[i, 4 * k + p] = value

    def set_row(i):
        fine.set_total(i)
        set_source(i)

    for low, high in gx_rows:
        rows_loop(low, high, set_gx, 8)
    for low, high in total_rows:
        rows_loop(low, high, set_row, 4)
    for low, high in relax_rows:
        fine.relax(x0, spare, f0, low, high)
    for low, high in sum_rows:
        fine.restrict(f1, x0, f0, low, high)


STATE = 14


def own_kernel(place, mixed_table, whole, *refs):
    prepare(
        place,
        mixed_table,
        refs,
        None,
        ((2, lambda n, h: whole[n, h], lambda n: whole[n, 2]),),
        ((17, 24),),
        ((17, 23),),
        ((18, 22),),
        (),
    )


def near_kernel(place, mixed_table, near0, near1, edge_left, edge_right, *refs):
    refs = refs[STATE:]
    late = lane_index() % 32 >= 16
    near = Sides(place, 1, near0, near1)

    def rim_lower(n):
        return jnp.where(late, edge_left[n], edge_right[n])

    def rim_upper(n):
        return jnp.where(
            late, pltpu.roll(edge_left[n], 16, 1), pltpu.roll(edge_right[n], 112, 1)
        )

    prepare(
        place,
        mixed_table,
        refs[:STATE],
        refs[STATE],
        ((1, near.lower, rim_lower), (3, near.upper, rim_upper)),
        ((9, 17), (24, 32)),
        ((9, 17), (23, 31)),
        ((10, 18), (22, 30)),
        ((6, 14),),
        4,
    )


def setup_kernel(place, mixed_table, far0, far1, *refs):
    refs = refs[STATE + 1 :]
    state, f1 = refs[:STATE], refs[STATE]
    gx1, gy1, via1, cap1, total1, weights1, x1 = refs[STATE + 1 : STATE + 8]
    gx2, gy2, below2, cap2, f2, go1, go0, spare1 = refs[STATE + 8 :]
    far = Sides(place, 2, far0, far1)
    below1 = state[9]
    prepare(
        place,
        mixed_table,
        state,
        f1,
        (
            (0, far.lower, lambda n: far.lower(n, 2)),
            (4, far.upper, lambda n: far.upper(n, 2)),
        ),
        ((2, 9), (32, 39)),
        ((2, 9), (31, 38)),
        ((3, 10), (30, 37)),
        ((2, 6), (14, 18)),
    )
    fine = Level(4, *state[:7])
    middle = Level(2, gx1, gy1, via1, below1, cap1, total1, weights1)
    coarse = Level(1, gx2, gy2, None, below2, cap2, None, None)
    coarsen(fine, middle, EXT1)
    coarsen(middle, coarse, EXT2)
    sum_below(below1, below2, 1, 0, EXT2)
    rows_loop(2, EXT1 - 2, middle.set_total, 4)
    middle.first_relax(spare1, f1, 2, 18)
    middle.relax(x1, spare1, f1, 3, 17)
    middle.restrict(f2, x1, f1, 2, 8)
    ups, downs = [], []
    for target, first, outer in ((ups, 2, 2), (downs, 4, 6)):
        for j in range(4):
            for k in range(SECTIONS):
                target.append(f2[first + j, k])
        for j in range(2):
            target.extend((gy2[outer + j, 0], below2[outer + j, 0], cap2[outer + j, 0]))
        for j in range(3):
            target.append(gx2[outer + j, 0])
    for n, (up, down) in enumerate(zip(ups, downs)):
        go0[n] = jnp.where(far.odd, down, up)
        go1[n] = jnp.where(far.odd, up, down)


def middle_kernel(place, *refs):
    (gx0, gy0, via0, below0, cap0, total0, weights0, f0, x0) = refs[0:9]
    (gx1, gy1, via1, below1, cap1, total1, weights1, f1, x1) = refs[9:18]
    (gx2, gy2, below2, cap2, f2, got1, got0) = refs[18:25]
    got = Sides(place, 2, got0, got1)
    (x0_out, f1_out, go_side, gxw, gyw, viaw, beloww, weightsw) = refs[25:33]
    (capw, totalw, fw, xa, xb, ya, yb, za, f1_own) = refs[33:42]
    fine = Level(4, gx0, gy0, via0, below0, cap0, total0, weights0)
    middle = Level(2, gx1, gy1, via1, below1, cap1, total1, weights1)
    coarse = Level(1, gxw, gyw, viaw, beloww, capw, totalw, weightsw)
    for j in range(4):
        for k in range(SECTIONS):
            fw[j, k] = got.lower(5 * j + k)
            fw[10 + j, k] = got.upper(5 * j + k)
    for j in range(2):
        for near, source in ((j, got.lower), (12 + j, got.upper)):
            gyw[near, 0] = source(20 + 3 * j)
            gyw[near, 1] = from_right(source(20 + 3 * j))
            beloww[near, 0] = source(21 + 3 * j)
            capw[near, 0] = source(22 + 3 * j)
    for j in range(3):
        gxw[j, 0] = got.lower(26 + j)
        gxw[12 + j, 0] = got.upper(26 + j)
    for j in range(6):
        for k in range(SECTIONS):
            fw[4 + j, k] = f2[2 + j, k]
    for j in range(10):
        gyw[2 + j, 0] = gy2[j, 0]
        gyw[2 + j, 1] = gy2[j, 1]
        beloww[2 + j, 0] = below2[j, 0]
        capw[2 + j, 0] = cap2[j, 0]
    for j in range(1, 10):
        gxw[2 + j, 0] = gx2[j, 0]
    rows_loop(0, WIDE2, coarse.set_total, 7)
    coarse.first_relax(xa, fw, 0, 14)
    coarse.relax(xb, xa, fw, 1, 13)
    coarse.relax(xa, xb, fw, 2, 12)
    coarse.relax(xb, xa, fw, 3, 11)
    middle.correct(ya, x1, xb, 3, 17, 2)
    middle.relax(yb, ya, f1, 4, 16)
    middle.relax(ya, yb, f1, 5, 15)
    fine.correct(x0_out, x0, ya, 10, 30)
    fine.relax(za, x0_out, f0, 11, 29)
    fine.relax(x0_out, za, f0, 12, 28)
    fine.relax(za, x0_out, f0, 13, 27)
    fine.relax(x0_out, za, f0, 14, 26)
    fine.restrict(f1_own, x0_out, f0, 8, 12, -8)
    for j in range(4):
        for n in range(10):
            f1_out[10 * j + n] = f1_own[j, n]
    for j in range(5):
        packs = packed([f1_own[n // 10, n % 10] for n in range(8 * j, 8 * j + 8)])
        for t in range(5):
            go_side[5 * j + t] = packs[t]


def lower_kernel(place, *refs):
    (gx1, gy1, via1, below1, cap1, total1, weights1) = refs[0:7]
    own, got0, got1 = refs[7:10]
    got = Sides(place, 1, got0, got1)
    f1, x1, f2_out = refs[10:13]
    (xa,) = refs[13:14]
    middle = Level(2, gx1, gy1, via1, below1, cap1, total1, weights1)
    for j in range(5):
        for first, source in ((4, got.lower), (12, got.upper)):
            values = unpacked([source(5 * j + t) for t in range(5)])
            for t in range(8):
                n = 8 * j + t
                f1[first + n // 10, n % 10] = values[t]
        for n in range(8 * j, 8 * j + 8):
            f1[8 + n // 10, n % 10] = own[n]
    middle.first_relax(xa, f1, 4, 16)
    middle.relax(x1, xa, f1, 5, 15)
    middle.restrict(f2_out, x1, f1, 3, 7, -3)


def finish_kernel(place, *refs):
    (gx0, gy0, via0, below0, weights0, f0, x0) = refs[0:7]
    (gx1, gy1, via1, below1, weights1, f1, x1) = refs[7:14]
    (gxw, gyw, viaw, beloww, weightsw, own, got0, got1, voltage) = refs[14:23]
    got = Sides(place, 2, got0, got1)
    sections, next_voltage = refs[23:25]
    fw, xa, xb, ya, yb, za, zb, mixed, turn, after, done = refs[25:36]
    fine = Level(4, gx0, gy0, via0, below0, None, None, weights0)
    middle = Level(2, gx1, gy1, via1, below1, None, None, weights1)
    coarse = Level(1, gxw, gyw, viaw, beloww, None, None, weightsw)
    for j in range(4):
        for k in range(SECTIONS):
            fw[1 + j, k] = got.lower(j, k)
            fw[5 + j, k] = own[j, k]
            fw[9 + j, k] = got.upper(j, k)
    block = place[0]
    for k in range(SECTIONS):
        fw[4, k] = jnp.where(block == 1, got.lower(1, k), fw[4, k])
        fw[9, k] = jnp.where(block == 30, got.upper(2, k), fw[9, k])
    coarse.first_relax(xa, fw, 1, 13)
    coarse.relax(xb, xa, fw, 2, 12)
    coarse.relax(xa, xb, fw, 3, 11)
    coarse.relax(xb, xa, fw, 4, 10)
    middle.correct(ya, x1, xb, 5, 15, 2)
    middle.relax(yb, ya, f1, 6, 14)
    middle.relax(ya, yb, f1, 7, 13)
    fine.correct(za, x0, ya, 14, 26)
    fine.relax(zb, za, f0, 15, 25)
    fine.relax(za, zb, f0, 16, 24)

    half = lane_index() < 64

    def mix(row):
        phases = []
        for p in range(4):
            values = [za[16 + row, 4 * k + p] for k in range(SECTIONS)]
            sums = []
            for j in range(SECTIONS):
                total = TRANSFORM[j][0] * values[0]
                for k in range(1, SECTIONS):
                    total = total + TRANSFORM[j][k] * values[k]
                sums.append(total)
            phases.append(sums)
        for h in range(2):
            for j in range(SECTIONS):
                mixed[h, 8 * j + row] = jnp.where(
                    half, phases[2 * h][j], pltpu.roll(phases[2 * h + 1][j], 64, 1)
                )

    rows_loop(0, 8, mix)
    slot = lax.broadcasted_iota(jnp.int32, (256, 256), 0)
    column = lax.broadcasted_iota(jnp.int32, (256, 256), 1)
    chooser = jnp.where(column == 4 * (slot % 64) + slot // 64, 1.0, 0.0).astype(jnp.bfloat16)
    result = selected(
        jnp.concatenate([mixed[h].reshape(320, LANES) for h in range(2)], axis=1), chooser
    )
    started = []

    def send(source, target):
        started.append(pltpu.make_async_copy(source, target, done.at[len(started)]))
        started[-1].start()

    for j in (4, 0, 1, 2, 3):
        for h in range(2):
            cut = slice(h * 128, h * 128 + 128)
            for row in range(8):
                at = (8 * j + row) * 8
                turn[j, h, pl.ds(row, 8, stride=8), :] = result[at : at + 8, cut]
            if j == 4:
                after[h] = voltage[:, cut] + turn[j, h]
                send(after.at[h], next_voltage.at[:, cut])
            send(turn.at[j, h], sections.at[j, :, cut])
    for copy in started:
        copy.wait()


VMEM = pltpu.MemorySpace.VMEM


def vregs(*shape):
    return pltpu.VMEM(shape + (LAYERS, LANES), jnp.float32)


def scratch(*shape):
    return pltpu.VMEM(shape + (LAYERS, LANES), jnp.float32)


def call(kernel, inputs, outs, scratches=(), outside=False, aliases=(), out_space=None):
    space = pltpu.MemorySpace.HBM if outside else VMEM
    inputs = [pltpu.with_memory_space_constraint(value, space) for value in inputs]
    return pl.pallas_call(
        kernel,
        out_shape=outs,
        in_specs=[pl.BlockSpec(memory_space=space)] * len(inputs),
        out_specs=[pl.BlockSpec(memory_space=out_space or VMEM)] * len(outs),
        scratch_shapes=list(scratches),
        input_output_aliases=dict(aliases),
        compiler_params=pltpu.CompilerParams(vmem_limit_bytes=12 * 2**20),
    )(*inputs)


def turned(value, axis, count, shift):
    return lax.ppermute(value, axis, [(i, (i + shift) % count) for i in range(count)])


def paired(value, distance):
    rows = lax.axis_size("section") * lax.axis_size("gx")
    columns = lax.axis_size("gy")
    values = value if isinstance(value, tuple) else (value, value)
    result = [None, None]
    for which in (1, 0):
        pairs = []
        for row in range(rows):
            up = (row // distance) % 2 == which
            other = row + distance if up else row - distance
            for column in range(columns):
                target = (other, column)
                if not 0 <= other < rows:
                    target = (row, column ^ 1) if distance == 1 else (row ^ 1, column)
                pairs.append((row * columns + column, target[0] * columns + target[1]))
        result[which] = lax.ppermute(values[which], ("section", "gx", "gy"), pairs)
    return result


def local(voltage, capacity, node_class, via_sites, ball_sites, load_type, load_table):
    columns = lax.axis_size("gy")
    volts = voltage.reshape(64, 256)
    own, left, right = call(
        gather_kernel,
        (
            volts,
            capacity.reshape(64, 256),
            node_class.reshape(64, 256),
            via_sites.reshape(56, 256),
            ball_sites,
            load_type,
        ),
        [
            vregs(33, 2),
            pltpu.VMEM((264, 64), jnp.float32),
            pltpu.VMEM((264, 64), jnp.float32),
        ],
        [
            pltpu.VMEM((4, 2, 64, LANES), jnp.float32),
            pltpu.VMEM((64, 256), jnp.float32),
            pltpu.VMEM((64, 256), jnp.float32),
            pltpu.VMEM((64, 256), jnp.int32),
            pltpu.VMEM((56, 256), jnp.int32),
            pltpu.VMEM((8, 256), jnp.int32),
            pltpu.VMEM((8, 256), jnp.int32),
            pltpu.SemaphoreType.DMA((6,)),
            pltpu.VMEM((264, 256), jnp.float32),
        ],
        outside=True,
    )
    mixed_table = jnp.einsum(
        "tk,jk->tj", load_table, jnp.asarray(INVERSE, jnp.float32), precision=lax.Precision.HIGHEST
    )
    row_block = lax.axis_index("section") * lax.axis_size("gx") + lax.axis_index("gx")
    place = jnp.stack(
        [
            jnp.full((LAYERS, LANES), number, jnp.int32)
            for number in (row_block, lax.axis_index("gy"))
        ]
    )
    mixed_table = jnp.broadcast_to(
        mixed_table.reshape(LOADS * SECTIONS, 1, 1), (LOADS * SECTIONS, LAYERS, LANES)
    )
    near = paired(own, 1)
    from_lower = turned(right, "gy", columns, 1)
    from_upper = turned(left, "gy", columns, -1)
    (whole,) = call(rim_kernel, (own, from_lower, from_upper), [vregs(33, 3)])
    far = paired(whole, 2)
    go_right, go_left = call(edge_kernel, (place, *near), [vregs(33), vregs(33)])
    edge_left = turned(go_right, "gy", columns, 1)
    edge_right = turned(go_left, "gy", columns, -1)
    state_shapes = [
        vregs(EXT0, 4),
        vregs(EXT0, 5),
        vregs(EXT0, 4),
        vregs(EXT0, 4),
        vregs(EXT0, 4),
        vregs(EXT0, 4),
        vregs(EXT0, 20),
        vregs(EXT0, 20),
        vregs(EXT0, 20),
        vregs(EXT1, 2),
        vregs(EXT0, 4),
        vregs(EXT0, 4),
        pltpu.VMEM((EXT0 * TILES, LANES), jnp.float32),
        vregs(EXT0, 20),
    ]
    state = call(own_kernel, (place, mixed_table, whole), state_shapes)
    state = call(
        near_kernel,
        (place, mixed_table, *near, edge_left, edge_right, *state),
        [*state_shapes, vregs(EXT1, 10)],
        aliases=[(6 + n, n) for n in range(STATE)],
    )
    state = call(
        setup_kernel,
        (place, mixed_table, *far, *state),
        [
            *state_shapes,
            vregs(EXT1, 10),
            vregs(EXT1, 2),
            vregs(EXT1, 3),
            vregs(EXT1, 2),
            vregs(EXT1, 2),
            vregs(EXT1, 2),
            vregs(EXT1, 10),
            vregs(EXT1, 10),
            vregs(EXT2, 1),
            vregs(EXT2, 2),
            vregs(EXT2, 1),
            vregs(EXT2, 1),
            vregs(EXT2, 5),
            vregs(29),
            vregs(29),
        ],
        [scratch(EXT1, 10)],
        aliases=[(4 + n, n) for n in range(STATE + 1)],
    )
    fine, below1, f1 = state[:9], state[9], state[STATE]
    gx1, gy1, via1, cap1, total1, weights1, x1 = state[STATE + 1 : STATE + 8]
    middle = (gx1, gy1, via1, below1, cap1, total1, weights1, f1, x1)
    coarse = state[STATE + 8 : STATE + 13]
    got = paired(tuple(reversed(state[STATE + 13 :])), 2)
    x0, f1_own, go_side, gxw, gyw, viaw, beloww, weightsw = call(
        middle_kernel,
        (place, *fine, *middle, *coarse, *reversed(got)),
        [
            vregs(EXT0, 20),
            vregs(40),
            vregs(25),
            vregs(WIDE2 + 1, 1),
            vregs(WIDE2, 2),
            vregs(WIDE2, 1),
            vregs(WIDE2, 1),
            vregs(WIDE2, 5),
        ],
        [
            scratch(WIDE2, 1),
            scratch(WIDE2, 1),
            scratch(WIDE2, 5),
            scratch(WIDE2, 5),
            scratch(WIDE2, 5),
            scratch(EXT1, 10),
            scratch(EXT1, 10),
            scratch(EXT0, 20),
            scratch(4, 10),
        ],
    )
    got = paired(go_side, 1)
    f1, x1, f2_own = call(
        lower_kernel,
        (place, *middle[:7], f1_own, *got),
        [vregs(EXT1, 10), vregs(EXT1, 10), vregs(4, 5)],
        [scratch(EXT1, 10)],
    )
    got = paired(f2_own, 2)
    sections, next_voltage = call(
        finish_kernel,
        (
            place,
            *fine[:4],
            *fine[6:8],
            x0,
            *middle[:4],
            middle[6],
            f1,
            x1,
            gxw,
            gyw,
            viaw,
            beloww,
            weightsw,
            f2_own,
            *got,
            volts,
        ),
        [
            jax.ShapeDtypeStruct((SECTIONS, 64, 256), jnp.float32),
            jax.ShapeDtypeStruct((64, 256), jnp.float32),
        ],
        [
            scratch(WIDE2, 5),
            scratch(WIDE2, 5),
            scratch(WIDE2, 5),
            scratch(EXT1, 10),
            scratch(EXT1, 10),
            scratch(EXT0, 20),
            scratch(EXT0, 20),
            scratch(2, 40),
            pltpu.VMEM((SECTIONS, 2, 64, LANES), jnp.float32),
            pltpu.VMEM((2, 64, LANES), jnp.float32),
            pltpu.SemaphoreType.DMA((12,)),
        ],
        out_space=pltpu.MemorySpace.HBM,
    )
    return sections.reshape((SECTIONS,) + voltage.shape), next_voltage.reshape(voltage.shape)


def solution(mesh):
    return jax.shard_map(
        local,
        mesh=mesh,
        in_specs=(
            P(None, ("section", "gx"), "gy"),
            P(None, ("section", "gx"), "gy"),
            P(None, ("section", "gx"), "gy"),
            P(None, ("section", "gx"), "gy"),
            P(("section", "gx"), "gy"),
            P(("section", "gx"), "gy"),
            P(),
        ),
        out_specs=(P(None, None, ("section", "gx"), "gy"), P(None, ("section", "gx"), "gy")),
        check_vma=False,
    )
```
